32 devices in a mesh: ctx: 16 (over z, y, core), wsh: 2 (over x).
Axes of the slice: x: 2, y: 2, z: 4, core: 2. Of those that a mesh axis runs over, the one named last changes fastest.
Arguments:
- content: bfloat16 [2, 2048, 768], P('wsh', 'ctx')
- query_stream: bfloat16 [2, 2048, 768], P('wsh', 'ctx'), may hold values from -6 to 6
- block_rank: int32 [2, 16], P('wsh', 'ctx'), may hold values from 0 to 15, each once within a row
- segments: int32 [2, 2048], P('wsh', 'ctx'), may hold values from 0 to 3, never falling along the last dimension, each value on 1 to 1024 neighbouring positions
- positions: int32 [2, 2048], P('wsh', 'ctx'), may hold values from 0 to 2152, as said below
- query_weight: bfloat16 [768, 768], P('wsh'), may hold values from -0.21875 to 0.21875
- key_weight: bfloat16 [768, 768], P('wsh'), may hold values from -0.21875 to 0.21875
- value_weight: bfloat16 [768, 768], P('wsh'), may hold values from -0.21875 to 0.21875
- output_weight: bfloat16 [768, 768], P('wsh'), may hold values from -1.75 to 1.75
- content_bias: bfloat16 [768], P('wsh'), may hold values from -3 to 3
- segment_bias: bfloat16 [768], P('wsh'), may hold values from -3 to 3
- segment_embed: bfloat16 [2, 768], P(None, 'wsh'), may hold values from -4 to 4
- relative_table: bfloat16 [12, 33], P('wsh'), may hold values from -4 to 4
- attention_gain: bfloat16 [768], P('wsh'), may hold values from 0.5 to 1.5
- attention_shift: bfloat16 [768], P('wsh'), may hold values from -1 to 1
- inner_weight: bfloat16 [768, 3072], P('wsh'), may hold values from -0.21875 to 0.21875
- inner_bias: bfloat16 [3072], P('wsh'), may hold values from -1 to 1
- outer_weight: bfloat16 [3072, 768], P('wsh'), may hold values from -0.109375 to 0.109375
- outer_bias: bfloat16 [768], P('wsh'), may hold values from -1 to 1
- final_gain: bfloat16 [768], P('wsh'), may hold values from 0.5 to 1.5
- final_shift: bfloat16 [768], P('wsh'), may hold values from -1 to 1
- content_cotangent: bfloat16 [2, 2048, 768], P('wsh', 'ctx'), may hold values from -6 to 6
- query_cotangent: bfloat16 [2, 2048, 768], P('wsh', 'ctx'), may hold values from -6 to 6
Outputs:
- content_result: bfloat16 [2, 2048, 768], P('wsh', 'ctx')
- query_result: bfloat16 [2, 2048, 768], P('wsh', 'ctx')
- content_gradient: float32 [2, 2048, 768], P('wsh', 'ctx')
- query_gradient: float32 [2, 2048, 768], P('wsh', 'ctx')
- query_weight_gradient: float32 [768, 768], P('wsh')
- key_weight_gradient: float32 [768, 768], P('wsh')
- value_weight_gradient: float32 [768, 768], P('wsh')
- output_weight_gradient: float32 [768, 768], P('wsh')
- content_bias_gradient: float32 [768], P('wsh')
- segment_bias_gradient: float32 [768], P('wsh')
- segment_embed_gradient: float32 [2, 768], P(None, 'wsh')
- relative_table_gradient: float32 [12, 33], P('wsh')
- attention_gain_gradient: float32 [768], P('wsh')
- attention_shift_gradient: float32 [768], P('wsh')
- inner_weight_gradient: float32 [768, 3072], P('wsh')
- inner_bias_gradient: float32 [3072], P('wsh')
- outer_weight_gradient: float32 [3072, 768], P('wsh')
- outer_bias_gradient: float32 [768], P('wsh')
- final_gain_gradient: float32 [768], P('wsh')
- final_shift_gradient: float32 [768], P('wsh')
- root_mean_squares: float32 [3], replicated
The draws below stay inside these ranges and needn't reach their ends.
Inputs may be any that keep to these rules, and one draw needn't show every extreme that they name: In each sequence positions rise by one inside each block of 128 tokens and never fall between blocks; the first token has position 0.
All inputs are finite; a program needn't handle non-finite values.
Results may differ from the reference program's by a relative error of at most 0.025.
Values may be sent and summed in bfloat16 or wider, within the bound.
No kernel may reach another device: no remote copies, remote signals or barrier semaphores. Data moves between devices by JAX's collectives and lax.ppermute only.
A program may use at most 448 MiB of HBM per device.

```python
import math
import jax
import jax.numpy as jnp
import numpy as np
from jax import lax

D = 768
HEADS = 12
HEAD_DIM = 64
FF = 3072
BLK = 128
NBUCK = 33
SEQS = 2
NBLK = 16
LEN = 2048
N_CTX = 16


def draw_content(key, part):
    folded = jax.random.fold_in(key, 101)
    fraction = jnp.arange(LEN, dtype=jnp.float32) / (LEN - 1)
    sample = jax.random.normal(folded, (SEQS, LEN, D), jnp.float32)
    factor = jnp.sqrt(1.0 + 2.0 * fraction)
    return (sample * factor[None, :, None]).astype(jnp.bfloat16)


def draw_positions(key, part):
    folded = jax.random.fold_in(key, 202)
    sequence_keys = jax.random.split(folded, SEQS)

    def per_sequence(seq_key):
        shuffled = jax.random.permutation(seq_key, NBLK - 1).astype(jnp.int32)
        gap_sizes = jnp.concatenate([jnp.zeros((1,), jnp.int32), shuffled])
        offsets = jnp.cumsum(gap_sizes).astype(jnp.int32)
        return jnp.arange(LEN, dtype=jnp.int32) + jnp.repeat(offsets, BLK)
    return jax.vmap(per_sequence)(sequence_keys)


def level_of(own_key, extent, cuts, least, largest):
    def one(dim, parts):
        heights = jax.random.uniform(jax.random.fold_in(jax.random.fold_in(own_key, 6), dim), (parts,), jnp.float32, least / len(cuts), largest / len(cuts))
        return jnp.repeat(jnp.exp(heights), extent[dim] // parts).reshape((-1,) + (1,) * (len(extent) - dim - 1))

    loudness = one(*cuts[0])
    for cut in cuts[1:]:
        loudness = loudness * one(*cut)
    return loudness


def split_up(amount, total, reach, skew):
    weights = [(1 << 20) // math.isqrt(grade ** skew) + 1 for grade in range(2, amount + 1)]
    spare, given = total - reach - (amount - 1), [1] * (amount - 1)
    while spare > 0:
        movable = [i for i in range(amount - 1) if given[i] < reach]
        whole, left = sum([weights[i] for i in movable]), spare
        for i in movable:
            addition = min(reach - given[i], max(1, left * weights[i] // whole), spare)
            given[i] = given[i] + addition
            spare = spare - addition
    return np.array([reach] + given)


def uneven(stream_key, number_of, total, most, lean):
    if number_of == 2:
        one = jax.random.randint(stream_key, (), max(1, total - most), min(most, total - 1) + 1)
        return jnp.stack([one, total - one])
    sizes = jnp.asarray(split_up(number_of, total, most, lean), jnp.int32)
    couples = (number_of - 1) // 2
    donor, sink = sizes[1:1 + 2 * couples:2], sizes[2:2 + 2 * couples:2]
    slack = jnp.minimum(donor - 1, most - sink)
    moved = jax.random.randint(jax.random.fold_in(stream_key, 1), (couples,), 0, 1 << 20) % (slack + 1)
    sizes = sizes.at[1:1 + 2 * couples:2].set(donor - moved).at[2:2 + 2 * couples:2].set(sink + moved)
    return sizes[jax.random.permutation(jax.random.fold_in(stream_key, 2), number_of)]


def gaussian(rng, dims, deviation, most, cuts=(), kind=jnp.bfloat16):
    entries = deviation * jax.random.normal(rng, dims, jnp.float32)
    if cuts:
        entries = entries * level_of(rng, dims, cuts, -0.22, 0.18)
    return jnp.clip(entries, -most, most).astype(kind)


def setup_inputs(seed: int = 0) -> dict:
    streams_of = jax.random.split(jax.random.key(seed), 24)
    return {
        "content": draw_content(jax.random.fold_in(streams_of[23], 71), 0),
        "query_stream": gaussian(streams_of[1], (SEQS, LEN, D), 1.0, 6.0, ((0, 2), (1, 16))),
        "block_rank": jax.vmap(lambda own: jax.random.permutation(own, NBLK))(jax.random.split(streams_of[2], SEQS)).reshape((SEQS, NBLK)).astype(jnp.int32),
        "segments": jax.vmap(lambda own: jnp.searchsorted(jnp.cumsum(uneven(own, 4, LEN, LEN // 2, 0)), jnp.arange(LEN), side="right"))(jax.random.split(streams_of[3], SEQS)).reshape((SEQS, LEN)).astype(jnp.int32),
        "positions": draw_positions(jax.random.fold_in(streams_of[23], 71), 0),
        "query_weight": gaussian(streams_of[5], (D, D), D ** -0.5, 0.21875, ((0, 2),)),
        "key_weight": gaussian(streams_of[6], (D, D), D ** -0.5, 0.21875, ((0, 2),)),
        "value_weight": gaussian(streams_of[7], (D, D), D ** -0.5, 0.21875, ((0, 2),)),
        "output_weight": gaussian(streams_of[8], (D, D), (max(4, D * 32 // (BLK * N_CTX))) ** -0.5, 1.75, ((0, 2),)),
        "content_bias": gaussian(streams_of[9], (D,), 0.5, 3.0, ((0, 2),)),
        "segment_bias": gaussian(streams_of[10], (D,), 0.5, 3.0, ((0, 2),)),
        "segment_embed": gaussian(streams_of[11], (2, D), 1.0, 4.0, ((1, 2),)),
        "relative_table": gaussian(streams_of[12], (HEADS, NBUCK), 1.0, 4.0, ((0, 2),)),
        "attention_gain": jnp.clip(1.0 + 0.1 * jax.random.normal(streams_of[13], (D,), jnp.float32), 0.5, 1.5).astype(jnp.bfloat16),
        "attention_shift": gaussian(streams_of[14], (D,), 0.2, 1.0, ((0, 2),)),
        "inner_weight": gaussian(streams_of[15], (D, FF), D ** -0.5, 0.21875, ((0, 2),)),
        "inner_bias": gaussian(streams_of[16], (FF,), 0.2, 1.0, ((0, 2),)),
        "outer_weight": gaussian(streams_of[17], (FF, D), FF ** -0.5, 0.109375, ((0, 2),)),
        "outer_bias": gaussian(streams_of[18], (D,), 0.2, 1.0, ((0, 2),)),
        "final_gain": jnp.clip(1.0 + 0.1 * jax.random.normal(streams_of[19], (D,), jnp.float32), 0.5, 1.5).astype(jnp.bfloat16),
        "final_shift": gaussian(streams_of[20], (D,), 0.2, 1.0, ((0, 2),)),
        "content_cotangent": gaussian(streams_of[21], (SEQS, LEN, D), 1.0, 6.0, ((0, 2), (1, 16))),
        "query_cotangent": gaussian(streams_of[22], (SEQS, LEN, D), 1.0, 6.0, ((0, 2), (1, 16))),
    }


@jax.custom_vjp
def low(v):
    return lax.optimization_barrier(v.astype(jnp.bfloat16)).astype(jnp.float32)

@jax.custom_vjp
def low_back(v):
    return v

def low_keep(v):
    return (low(v), None)

def low_pass(kept, grad):
    return (grad,)

def back_keep(v):
    return (v, None)

def back_low(kept, grad):
    return (low(grad),)
low.defvjp(low_keep, low_pass)
low_back.defvjp(back_keep, back_low)
negative = -1e+30
epsilon = 1e-05
bucket_steps = 16
highest = lax.Precision.HIGHEST

def layer_norm(values, gain_row, shift_row):
    centred = values - lax.optimization_barrier(jnp.mean(values, axis=-1, keepdims=True))
    spread = lax.optimization_barrier(jnp.mean(centred * centred, axis=-1, keepdims=True))
    return centred * lax.rsqrt(spread + epsilon) * gain_row + shift_row

def bucket_number(query_places, key_places):
    distance = query_places[:, None] - key_places[None, :]
    result = jnp.full(distance.shape, bucket_steps, jnp.int32)
    for level_index in range(bucket_steps):
        bound_value = 1 + level_index * level_index * LEN // (bucket_steps * bucket_steps)
        result = result + (distance >= bound_value).astype(jnp.int32) - (distance <= -bound_value).astype(jnp.int32)
    return result

def bias_lookup(number, table):
    total_bias = jnp.zeros((table.shape[0],) + number.shape, table.dtype)
    for bucket in range(table.shape[1]):
        total_bias = total_bias + jnp.where(number[None] == bucket, table[:, bucket][:, None, None], 0.0)
    return total_bias

def allowed_pairs(row_ranks, row_streams, row_index, key_ranks, key_index):
    earlier = key_ranks[None, :] < row_ranks[:, None]
    same_block = key_ranks[None, :] == row_ranks[:, None]
    other_token = (key_index[None, :] != row_index[:, None]) | (row_streams[:, None] == 0)
    return earlier | same_block & other_token

def attend(block_items, keys_low, values_low, key_ranks, key_index, key_places, key_segments, table):
    query_low, seg_zero, seg_one, row_ranks, row_streams, row_index, row_places, row_segments = block_items
    content_term = jnp.einsum('rhe,khe->hrk', query_low, keys_low, precision=highest)
    differ = (row_segments[:, None] != key_segments[None, :]).astype(query_low.dtype)
    zero_rows = seg_zero.T
    one_rows = seg_one.T
    segment_term = zero_rows[:, :, None] + (one_rows - zero_rows)[:, :, None] * differ[None]
    number = bucket_number(row_places, key_places)
    scores = low_back((content_term + segment_term) * 0.125 + bias_lookup(number, table))
    allowed = allowed_pairs(row_ranks, row_streams, row_index, key_ranks, key_index)[None]
    masked = jnp.where(allowed, scores, negative)
    topmost = lax.optimization_barrier(jnp.max(masked, axis=2, keepdims=True))
    weights = jnp.where(allowed, jnp.exp(masked - topmost), 0.0)
    attend_weights = weights / lax.optimization_barrier(jnp.sum(weights, axis=2, keepdims=True))
    return jnp.einsum('hrk,khe->rhe', low(attend_weights), values_low, precision=highest)

def regroup(source):
    shaped = source.reshape((2, NBLK, BLK) + source.shape[1:])
    return jnp.swapaxes(shaped, 0, 1).reshape((NBLK, 2 * BLK) + source.shape[1:])

def sequence_layer(content_row, query_row, ranks, segment_row, place_row, params):
    weight_query, weight_key, weight_value, weight_output, bias_content, bias_segment, embed_pair, table_full, gain_first, shift_first, weight_inner, bias_inner, weight_outer, bias_outer, gain_second, shift_second = params
    streams = jnp.concatenate([content_row, query_row], axis=0)
    query_full = low_back(jnp.dot(streams, weight_query, precision=highest))
    keys_low = low(low_back(jnp.dot(content_row, weight_key, precision=highest)))
    values_low = low(low_back(jnp.dot(content_row, weight_value, precision=highest)))
    query_low = low(query_full + bias_content).reshape(2 * LEN, HEADS, HEAD_DIM)
    query_shift = (query_full + bias_segment).reshape(2 * LEN, HEADS, HEAD_DIM)
    embed_heads = embed_pair.reshape(2, HEADS, HEAD_DIM)
    seg_zero = lax.optimization_barrier(jnp.sum(query_shift * embed_heads[0][None], axis=2))
    seg_one = lax.optimization_barrier(jnp.sum(query_shift * embed_heads[1][None], axis=2))
    token_rank = jnp.repeat(ranks, BLK).astype(jnp.int32)
    token_index = jnp.arange(LEN, dtype=jnp.int32)
    row_ranks = jnp.concatenate([token_rank, token_rank])
    row_streams = jnp.concatenate([jnp.zeros((LEN,), jnp.int32), jnp.ones((LEN,), jnp.int32)])
    row_index = jnp.concatenate([token_index, token_index])
    row_places = jnp.concatenate([place_row, place_row])
    row_segments = jnp.concatenate([segment_row, segment_row])
    blocks = (regroup(query_low), regroup(seg_zero), regroup(seg_one), regroup(row_ranks), regroup(row_streams), regroup(row_index), regroup(row_places), regroup(row_segments))
    keys_heads = keys_low.reshape(LEN, HEADS, HEAD_DIM)
    values_heads = values_low.reshape(LEN, HEADS, HEAD_DIM)

    def one_block(block_items):
        return attend(block_items, keys_heads, values_heads, token_rank, token_index, place_row, segment_row, table_full)
    outputs = lax.map(jax.checkpoint(one_block), blocks)
    attended = jnp.swapaxes(outputs.reshape(NBLK, 2, BLK, D), 0, 1).reshape(2 * LEN, D)
    out_low = low(low_back(attended))
    attention_out = low_back(jnp.dot(out_low, weight_output, precision=highest))
    residual = streams + attention_out
    normed = layer_norm(residual, gain_first, shift_first)
    inner_pre = low_back(jnp.dot(low(normed), weight_inner, precision=highest) + bias_inner)
    active = low(jax.nn.gelu(inner_pre, approximate=False))
    outer_out = low_back(jnp.dot(active, weight_outer, precision=highest) + bias_outer)
    final_norm = layer_norm(normed + outer_out, gain_second, shift_second)
    sums = jnp.stack([jnp.sum(content_row * content_row), jnp.sum(attention_out[:LEN] * attention_out[:LEN]), jnp.sum(residual[:LEN] * residual[:LEN])])
    return (final_norm, sums)

def reference(content, query_stream, block_rank, segments, positions, query_weight, key_weight, value_weight, output_weight, content_bias, segment_bias, segment_embed, relative_table, attention_gain, attention_shift, inner_weight, inner_bias, outer_weight, outer_bias, final_gain, final_shift, content_cotangent, query_cotangent):
    params = tuple((member.astype(jnp.float32) for member in (query_weight, key_weight, value_weight, output_weight, content_bias, segment_bias, segment_embed, relative_table, attention_gain, attention_shift, inner_weight, inner_bias, outer_weight, outer_bias, final_gain, final_shift)))

    def whole(content_float, query_float, param_tuple):
        mapped = jax.vmap(sequence_layer, in_axes=(0, 0, 0, 0, 0, None))
        return mapped(content_float, query_float, block_rank, segments, positions, param_tuple)
    finals, pull_back, sums = jax.vjp(whole, content.astype(jnp.float32), query_stream.astype(jnp.float32), params, has_aux=True)
    cotangent = jnp.concatenate([content_cotangent, query_cotangent], axis=1).astype(jnp.float32)
    content_back, query_back, param_back = pull_back(cotangent)
    root_mean = jnp.sqrt(lax.optimization_barrier(jnp.sum(sums, axis=0)) / (SEQS * LEN * D))
    return (finals[:, :LEN].astype(jnp.bfloat16), finals[:, LEN:].astype(jnp.bfloat16), content_back, query_back, param_back[0], param_back[1], param_back[2], param_back[3], param_back[4], param_back[5], param_back[6], param_back[7], param_back[8], param_back[9], param_back[10], param_back[11], param_back[12], param_back[13], param_back[14], param_back[15], root_mean)
```

```python
import functools

import jax
import jax.numpy as jnp
from jax import lax
from jax.experimental import pallas as pl
from jax.experimental.pallas import tpu as pltpu
from jax.sharding import PartitionSpec as P

negative = -1e30
epsilon = 1e-05
bucket_steps = 16
key_tile = 256
lanes = 128
highest = lax.Precision.HIGHEST
f32 = jnp.float32
bf16 = jnp.bfloat16


def layer_norm(values, gain_row, shift_row):
    centred = values - jnp.mean(values, axis=-1, keepdims=True)
    spread = jnp.mean(centred * centred, axis=-1, keepdims=True)
    return centred * lax.rsqrt(spread + epsilon) * gain_row + shift_row


def gelu_exact(values):
    return jax.nn.gelu(values, approximate=False)


def bucket_levels(distance, length):
    result = jnp.full(distance.shape, bucket_steps, jnp.int32)
    for level_index in range(bucket_steps):
        bound_value = 1 + level_index * level_index * length // (bucket_steps * bucket_steps)
        result = (
            result
            + (distance >= bound_value).astype(jnp.int32)
            - (distance <= -bound_value).astype(jnp.int32)
        )
    return result


def dot(left, right):
    return jnp.dot(left, right, preferred_element_type=f32)


def dot_nt(left, right):
    return lax.dot_general(left, right, (((1,), (1,)), ((), ())), preferred_element_type=f32)


def dot_tn(left, right):
    return lax.dot_general(left, right, (((0,), (0,)), ((), ())), preferred_element_type=f32)


def partner(value, bit):
    count = lax.axis_size("ctx")
    return lax.ppermute(value, "ctx", [(place, place ^ bit) for place in range(count)])


def across(value):
    return lax.ppermute(value, "wsh", [(0, 1), (1, 0)])


def bits_of(count):
    result = []
    bit = 1
    while bit < count:
        result.append(bit)
        bit *= 2
    return result


def block_order(count):
    order = [0]
    for bit in reversed(bits_of(count)):
        order = order + [place | bit for place in order]
    return order


def gather_blocks(own):
    count = lax.axis_size("ctx")
    bits = bits_of(count)
    held = {0: own}
    top = bits[-2:]
    for place in (top[0], top[1], top[0] | top[1]):
        held[place] = partner(own, place)
    for bit in reversed(bits[:-2]):
        for place in list(held):
            held[place | bit] = partner(held[place], bit)
    return [held[place] for place in block_order(count)]


def scatter_blocks(total):
    count = lax.axis_size("ctx")
    for bit in bits_of(count):
        half = total.shape[0] // 2
        received = partner(total[half:].astype(bf16), bit)
        total = total[:half].astype(f32) + received.astype(f32)
    return total


def gather_shard(shard):
    core = lax.axis_index("ctx") % 2
    side = lax.axis_index("wsh")
    rows = shard.shape[0]
    half = rows // 2
    mine = lax.dynamic_slice_in_dim(shard, core * half, half, 0)
    got = across(mine)
    rest = partner(got, 1)
    whole = jnp.zeros((2 * rows,) + shard.shape[1:], shard.dtype)
    base = (1 - side) * rows
    whole = lax.dynamic_update_slice_in_dim(whole, shard, side * rows, 0)
    whole = lax.dynamic_update_slice_in_dim(whole, got, base + core * half, 0)
    return lax.dynamic_update_slice_in_dim(whole, rest, base + (1 - core) * half, 0)


def halve(value, bit, dim):
    size = value.shape[dim] // 2
    kept = lax.dynamic_slice_in_dim(value, bit * size, size, dim)
    sent = lax.dynamic_slice_in_dim(value, (1 - bit) * size, size, dim)
    return kept, sent


def join(mine, other, bit, dim):
    return jnp.where(
        bit == 0,
        jnp.concatenate([mine, other], axis=dim),
        jnp.concatenate([other, mine], axis=dim),
    )


def added(kept, received):
    return (kept.astype(f32) + received.astype(f32)).astype(bf16)


def reduce_gradient(gradient):
    index = lax.axis_index("ctx")
    side = lax.axis_index("wsh")
    count = lax.axis_size("ctx")
    value = gradient
    kept, sent = halve(value, index % 2, 1)
    value = added(kept, partner(sent, 1))
    kept, sent = halve(value, side, 0)
    value = added(kept, across(sent))
    taken = []
    for bit in bits_of(count)[1:]:
        own_bit = (index // bit) % 2
        if (value.shape[0] // 2) % 16 == 0:
            dim = 0
        elif (value.shape[1] // 2) % 128 == 0:
            dim = 1
        else:
            dim = -1
        if dim < 0:
            value = added(value, partner(value, bit))
        else:
            kept, sent = halve(value, own_bit, dim)
            value = added(kept, partner(sent, bit))
        taken.append((bit, own_bit, dim))
    for bit, own_bit, dim in reversed(taken):
        if dim >= 0:
            value = join(value, partner(value, bit), own_bit, dim)
    value = join(value, partner(value, 1), index % 2, 1)
    return value.astype(f32)


def sum_everywhere(value):
    count = lax.axis_size("ctx")
    value = value + across(value)
    for bit in bits_of(count):
        value = value + partner(value, bit)
    return value


def stream_bias(table_ref, head, block):
    spread = jnp.broadcast_to(table_ref[head, pl.ds(block, 1), :], (lanes, 2 * lanes))
    return pltpu.roll(spread, 0, 1, stride=1, stride_axis=0)[:, :lanes]


def tile_bias(table_ref, block):
    parts = []
    for piece in range(key_tile // lanes):
        first = stream_bias(table_ref, 0, block + piece)
        second = stream_bias(table_ref, 1, block + piece)
        parts.append(jnp.concatenate([first, first, second, second], axis=1))
    return jnp.concatenate(parts, axis=0)


def own_mask():
    row = lax.broadcasted_iota(jnp.int32, (key_tile, 4 * lanes), 0)
    column = lax.broadcasted_iota(jnp.int32, (key_tile, 4 * lanes), 1)
    stream = (column // lanes) % 2
    return jnp.where((stream == 1) & (row == column % lanes), negative, 0.0)


def forward_kernel(
    query_ref,
    content_bias_ref,
    segment_bias_ref,
    embed_ref,
    row_code_ref,
    key_code_ref,
    key_ref,
    value_ref,
    table_ref,
    out_ref,
    log_ref,
    stack_ref,
    score_ref,
):
    rows = query_ref.shape[0]
    tiles = key_ref.shape[0] // key_tile
    lane = lax.broadcasted_iota(jnp.int32, (rows, lanes), 1)
    first = lane < lanes // 2
    query = query_ref[...]
    low = (query + content_bias_ref[...]).astype(bf16).astype(f32) * 0.125
    shifted = query + segment_bias_ref[...]
    zero_term = shifted * embed_ref[0:1, :]
    one_term = shifted * embed_ref[1:2, :]
    code = row_code_ref[...]
    for head in range(2):
        own = first if head == 0 else jnp.logical_not(first)
        zero_sum = jnp.sum(jnp.where(own, zero_term, 0.0), axis=1, keepdims=True) * 0.125
        one_sum = jnp.sum(jnp.where(own, one_term, 0.0), axis=1, keepdims=True) * 0.125
        step = zero_sum - one_sum
        step_high = step.astype(bf16).astype(f32)
        step_low = step - step_high
        one_high = one_sum.astype(bf16).astype(f32)
        one_low = one_sum - one_high
        extra = jnp.where(
            lane < 4,
            step_high,
            jnp.where(lane < 8, step_low, jnp.where(lane == 8, one_high, one_low)),
        )
        stack_ref[0, pl.ds(head * rows, rows), 0:lanes] = jnp.where(own, low, 0.0).astype(bf16)
        stack_ref[0, pl.ds(head * rows, rows), lanes : 2 * lanes] = (extra * code).astype(bf16)
    stack = stack_ref[0]

    def scores(tile, top):
        start = pl.multiple_of(tile * key_tile, key_tile)
        keys = jnp.concatenate(
            [key_ref[pl.ds(start, key_tile), :], key_code_ref[pl.ds(start, key_tile), :]], axis=1
        )
        score = dot_nt(keys, stack) + tile_bias(table_ref, tile * (key_tile // lanes))
        if isinstance(tile, int) and tile == 0:
            score = score + own_mask()
        score_ref[pl.ds(start, key_tile), :] = score
        return jnp.maximum(top, jnp.max(score.reshape(key_tile // 8, 8, 4 * lanes), axis=0))

    top = jnp.full((8, 4 * lanes), negative, f32)
    top = scores(0, top)
    top = lax.fori_loop(1, tiles, scores, top, unroll=min(7, tiles - 1))
    peak = jnp.max(top, axis=0, keepdims=True)

    def gathered(tile, running):
        total, mixed = running
        start = pl.multiple_of(tile * key_tile, key_tile)
        weight = jnp.exp(score_ref[pl.ds(start, key_tile), :] - peak)
        total = total + jnp.sum(weight.reshape(key_tile // 8, 8, 4 * lanes), axis=0)
        mixed = mixed + dot_tn(value_ref[pl.ds(start, key_tile), :], weight.astype(bf16))
        return total, mixed

    total, mixed = lax.fori_loop(
        0,
        tiles,
        gathered,
        (jnp.zeros((8, 4 * lanes), f32), jnp.zeros((lanes, 4 * lanes), f32)),
        unroll=min(8, tiles),
    )
    total = jnp.sum(total, axis=0, keepdims=True)
    mixed = mixed / total
    half = lanes // 2
    joined = jnp.concatenate([mixed[:half, :rows], mixed[half:, rows:]], axis=0)
    out_ref[...] = joined.T
    log_ref[0] = peak + jnp.log(total)


def diagonal_sums(square):
    lane = lax.broadcasted_iota(jnp.int32, (8, lanes), 1)
    near = square[0:8]
    far = jnp.zeros((8, lanes), f32)
    for group in range(1, lanes // 8):
        turned = pltpu.roll(square[8 * group : 8 * group + 8], lanes - 8 * group, 1)
        inside = lane < lanes - 8 * group
        near = near + jnp.where(inside, turned, 0.0)
        far = far + jnp.where(inside, 0.0, turned)
    both = jnp.concatenate([near, far], axis=1)
    row = lax.broadcasted_iota(jnp.int32, (8, 2 * lanes), 0)
    for bit in (1, 2, 4):
        both = jnp.where((row // bit) % 2 == 1, pltpu.roll(both, 2 * lanes - bit, 1), both)
    return jnp.sum(both, axis=0, keepdims=True)


def backward_kernel(
    stack_ref,
    query_ref,
    segment_bias_ref,
    embed_ref,
    row_code_ref,
    key_code_ref,
    key_ref,
    value_ref,
    table_ref,
    out_back_ref,
    attended_ref,
    log_ref,
    query_back_ref,
    key_back_ref,
    value_back_ref,
    diagonal_ref,
    small_ref,
):
    rows = query_ref.shape[0]
    tiles = key_ref.shape[0] // key_tile
    half = lanes // 2
    lane = lax.broadcasted_iota(jnp.int32, (rows, lanes), 1)
    first = lane < half
    out_back = out_back_ref[...]
    product = (out_back.astype(f32) * attended_ref[...]).T
    delta = jnp.concatenate(
        [
            jnp.sum(product[:half], axis=0, keepdims=True),
            jnp.sum(product[half:], axis=0, keepdims=True),
        ],
        axis=1,
    )
    zeros = jnp.zeros_like(out_back)
    back_stack = jnp.concatenate(
        [jnp.where(first, out_back, zeros), jnp.where(first, zeros, out_back)], axis=0
    )
    stack = stack_ref[0]
    query_stack = stack[:, :lanes]
    log_row = log_ref[0]

    def step(tile, running):
        start = pl.multiple_of(tile * key_tile, key_tile)
        block = tile * (key_tile // lanes)
        keys = jnp.concatenate(
            [key_ref[pl.ds(start, key_tile), :], key_code_ref[pl.ds(start, key_tile), :]], axis=1
        )
        score = dot_nt(keys, stack) + tile_bias(table_ref, block)
        if isinstance(tile, int) and tile == 0:
            score = score + own_mask()
        weight = jnp.exp(score - log_row)
        weight_back = dot_nt(value_ref[pl.ds(start, key_tile), :], back_stack)
        score_back = weight * (weight_back - delta)
        score_low = score_back.astype(bf16)
        value_back_ref[pl.ds(start, key_tile), :] = dot(weight.astype(bf16), back_stack).astype(
            bf16
        )
        key_back_ref[pl.ds(start, key_tile), :] = dot(score_low, query_stack).astype(bf16)
        for head in range(2):
            for piece in range(key_tile // lanes):
                part = score_back[
                    piece * lanes : (piece + 1) * lanes, head * rows : (head + 1) * rows
                ]
                square = part[:, :lanes] + part[:, lanes:]
                diagonal_ref[head, pl.ds(block + piece, 1), :] = diagonal_sums(square)
        return running + dot_tn(keys, score_low)

    running = step(0, jnp.zeros((2 * lanes, 2 * rows), f32))
    running = lax.fori_loop(1, tiles, step, running, unroll=min(7, tiles - 1))
    joined = jnp.concatenate([running[:half, :rows], running[half:lanes, rows:]], axis=0).T * 0.125
    shifted = query_ref[...] + segment_bias_ref[...]
    code = row_code_ref[...]
    zero_columns = []
    one_columns = []
    for head in range(2):
        part = running[lanes:, head * rows : (head + 1) * rows].T * 0.125
        same = jnp.sum(jnp.where(lane < 4, part * code, 0.0), axis=1, keepdims=True)
        total = jnp.sum(jnp.where(lane == 8, part, 0.0), axis=1, keepdims=True)
        zero_columns.append(same)
        one_columns.append(total - same)
    zero_back = jnp.where(first, zero_columns[0], zero_columns[1])
    one_back = jnp.where(first, one_columns[0], one_columns[1])
    shift_back = zero_back * embed_ref[0:1, :] + one_back * embed_ref[1:2, :]
    query_back_ref[...] = (joined + shift_back).astype(bf16)
    small_ref[0:1, :] = jnp.sum(joined, axis=0, keepdims=True)
    small_ref[1:2, :] = jnp.sum(shift_back, axis=0, keepdims=True)
    small_ref[2:3, :] = jnp.sum(zero_back * shifted, axis=0, keepdims=True)
    small_ref[3:4, :] = jnp.sum(one_back * shifted, axis=0, keepdims=True)
    small_ref[4:8, :] = jnp.zeros((4, lanes), f32)


def attention_specs(rows, keys, blocks):
    column = lambda pair: (0, pair)
    fixed = lambda pair: (0, 0)
    front = lambda pair: (pair, 0, 0)
    return {
        "rows": pl.BlockSpec((rows, lanes), column),
        "row": pl.BlockSpec((1, lanes), column),
        "embed": pl.BlockSpec((2, lanes), column),
        "small": pl.BlockSpec((8, lanes), column),
        "row_code": pl.BlockSpec((rows, lanes), fixed),
        "key_code": pl.BlockSpec((keys, lanes), fixed, pipeline_mode=pl.Buffered(1)),
        "keys": pl.BlockSpec((keys, lanes), column),
        "table": pl.BlockSpec((2, blocks, 2 * lanes), front),
        "log": pl.BlockSpec((1, 1, 2 * rows), front),
        "stack": pl.BlockSpec((1, 2 * rows, 2 * lanes), front),
    }


def attention_forward(query_full, bias_content, bias_segment, embed, row_code, key_code, keys, values, table):
    rows, width = query_full.shape
    count = keys.shape[0]
    pairs = width // lanes
    spec = attention_specs(rows, count, count // lanes)
    return pl.pallas_call(
        forward_kernel,
        grid=(pairs,),
        in_specs=[
            spec["rows"],
            spec["row"],
            spec["row"],
            spec["embed"],
            spec["row_code"],
            spec["key_code"],
            spec["keys"],
            spec["keys"],
            spec["table"],
        ],
        out_specs=[spec["rows"], spec["log"], spec["stack"]],
        out_shape=[
            jax.ShapeDtypeStruct((rows, width), f32),
            jax.ShapeDtypeStruct((pairs, 1, 2 * rows), f32),
            jax.ShapeDtypeStruct((pairs, 2 * rows, 2 * lanes), bf16),
        ],
        scratch_shapes=[pltpu.VMEM((count, 2 * rows), f32)],
        compiler_params=pltpu.CompilerParams(
            dimension_semantics=("arbitrary",), vmem_limit_bytes=60 << 20
        ),
        cost_estimate=pl.CostEstimate(
            flops=4 * rows * count * width,
            bytes_accessed=4 * count * width + 8 * rows * width,
            transcendentals=rows * count * width // 64,
        ),
    )(query_full, bias_content, bias_segment, embed, row_code, key_code, keys, values, table)


def attention_backward(
    stack, query_full, bias_segment, embed, row_code, key_code, keys, values, table, out_back, attended, log_row
):
    rows, width = query_full.shape
    count = keys.shape[0]
    pairs = width // lanes
    spec = attention_specs(rows, count, count // lanes)
    return pl.pallas_call(
        backward_kernel,
        grid=(pairs,),
        in_specs=[
            spec["stack"],
            spec["rows"],
            spec["row"],
            spec["embed"],
            spec["row_code"],
            spec["key_code"],
            spec["keys"],
            spec["keys"],
            spec["table"],
            spec["rows"],
            spec["rows"],
            spec["log"],
        ],
        out_specs=[spec["rows"], spec["keys"], spec["keys"], spec["table"], spec["small"]],
        out_shape=[
            jax.ShapeDtypeStruct((rows, width), bf16),
            jax.ShapeDtypeStruct((count, width), bf16),
            jax.ShapeDtypeStruct((count, width), bf16),
            jax.ShapeDtypeStruct((2 * pairs, count // lanes, 2 * lanes), f32),
            jax.ShapeDtypeStruct((8, width), f32),
        ],
        compiler_params=pltpu.CompilerParams(
            dimension_semantics=("arbitrary",), vmem_limit_bytes=60 << 20
        ),
        cost_estimate=pl.CostEstimate(
            flops=10 * rows * count * width,
            bytes_accessed=8 * count * width + 8 * rows * width,
            transcendentals=rows * count * width // 64,
        ),
    )(stack, query_full, bias_segment, embed, row_code, key_code, keys, values, table, out_back, attended, log_row)


def body(
    content,
    query_stream,
    block_rank,
    segments,
    positions,
    query_weight,
    key_weight,
    value_weight,
    output_weight,
    content_bias,
    segment_bias,
    segment_embed,
    relative_table,
    attention_gain,
    attention_shift,
    inner_weight,
    inner_bias,
    outer_weight,
    outer_bias,
    final_gain,
    final_shift,
    content_cotangent,
    query_cotangent,
):
    block_rows = content.shape[1]
    width = content.shape[2]
    rows = 2 * block_rows
    count = lax.axis_size("ctx")
    sides = lax.axis_size("wsh")
    side = lax.axis_index("wsh")
    length = block_rows * count
    order = block_order(count)
    own_content = content[0]
    own_query = query_stream[0]
    part = width // sides
    table_heads, bucket_count = relative_table.shape
    head_count = table_heads * sides
    inner_rows = inner_bias.shape[0] // part

    table_flat = jnp.pad(
        relative_table.reshape(-1), (0, part - table_heads * bucket_count)
    ).reshape(1, part)
    small = jnp.concatenate(
        [
            jnp.stack(
                [
                    content_bias,
                    segment_bias,
                    attention_gain,
                    attention_shift,
                    outer_bias,
                    final_gain,
                    final_shift,
                ]
            ),
            segment_embed,
            inner_bias.reshape(inner_rows, part),
            table_flat,
        ],
        axis=0,
    )
    small_other = across(small)
    small_pair = jnp.where(
        side == 0, jnp.stack([small, small_other]), jnp.stack([small_other, small])
    ).astype(f32)
    vectors = jnp.transpose(small_pair[:, :9], (1, 0, 2)).reshape(9, width)
    bias_content = vectors[0:1]
    bias_segment = vectors[1:2]
    gain_first = vectors[2]
    shift_first = vectors[3]
    bias_outer = vectors[4]
    gain_second = vectors[5]
    shift_second = vectors[6]
    embed = vectors[7:9]
    bias_inner = small_pair[:, 9 : 9 + inner_rows].reshape(-1)
    table_full = small_pair[:, 9 + inner_rows, : table_heads * bucket_count].reshape(
        head_count, bucket_count
    )

    meta = jnp.concatenate(
        [
            segments[0].reshape(1, block_rows),
            jnp.broadcast_to(positions[:, :1], (1, block_rows)),
            jnp.broadcast_to(block_rank, (1, block_rows)),
        ],
        axis=0,
    )
    meta_all = jnp.stack(gather_blocks(meta))
    content_all = jnp.concatenate(gather_blocks(own_content), axis=0)

    weight_query = gather_shard(query_weight)
    weight_key = gather_shard(key_weight)
    weight_value = gather_shard(value_weight)
    weight_output = gather_shard(output_weight)
    weight_inner = gather_shard(inner_weight)
    weight_outer = gather_shard(outer_weight)

    key_segments = meta_all[:, 0, :].reshape(length)
    key_firsts = meta_all[:, 1, 0]
    key_ranks = meta_all[:, 2, 0]
    turn = jnp.arange(2 * block_rows, dtype=jnp.int32)
    turn = jnp.where(turn < block_rows, turn, turn - 2 * block_rows)
    distance = (key_firsts[0] - key_firsts)[:, None] + turn[None, :]
    number = bucket_levels(distance, length)
    onehot = (number[:, :, None] == jnp.arange(bucket_count, dtype=jnp.int32)).astype(f32)
    table = jnp.einsum("kmc,hc->hkm", onehot, table_full, precision=highest)
    table = jnp.where((key_ranks > key_ranks[0])[None, :, None], negative, table)
    lane = jnp.arange(lanes, dtype=jnp.int32)[None, :]
    key_code = jnp.where(
        lane < 8, (key_segments[:, None] == lane % 4), (lane < 10)
    ).astype(bf16)
    row_segments = jnp.concatenate([segments[0], segments[0]])
    row_code = jnp.where(
        lane < 8, (row_segments[:, None] == lane % 4), (lane < 10)
    ).astype(f32)

    streams = jnp.concatenate([own_content, own_query], axis=0)
    query_full = dot(streams, weight_query)
    keys = dot(content_all, weight_key).astype(bf16)
    values = dot(content_all, weight_value).astype(bf16)
    attended, log_row, stack = attention_forward(
        query_full, bias_content, bias_segment, embed, row_code, key_code, keys, values, table
    )

    out_low = attended.astype(bf16)
    attention_out = dot(out_low, weight_output)
    residual = streams.astype(f32) + attention_out
    normed, first_back = jax.vjp(layer_norm, residual, gain_first, shift_first)
    normed_low = normed.astype(bf16)
    inner_pre = dot(normed_low, weight_inner) + bias_inner
    active, gelu_back = jax.vjp(gelu_exact, inner_pre)
    active_low = active.astype(bf16)
    outer_out = dot(active_low, weight_outer) + bias_outer
    final_norm, second_back = jax.vjp(layer_norm, normed + outer_out, gain_second, shift_second)
    squares = jnp.stack(
        [
            jnp.sum(jnp.square(own_content.astype(f32))),
            jnp.sum(jnp.square(attention_out[:block_rows])),
            jnp.sum(jnp.square(residual[:block_rows])),
        ]
    )
    cotangent = jnp.concatenate([content_cotangent[0], query_cotangent[0]], axis=0).astype(f32)
    back_second, final_gain_back, final_shift_back = second_back(cotangent)
    outer_back = back_second.astype(bf16)
    outer_weight_back = dot_tn(active_low, outer_back).astype(bf16)
    outer_bias_back = jnp.sum(outer_back.astype(f32), axis=0)
    active_back = dot_nt(outer_back, weight_outer)
    inner_back = gelu_back(active_back)[0].astype(bf16)
    inner_weight_back = dot_tn(normed_low, inner_back).astype(bf16)
    inner_bias_back = jnp.sum(inner_back.astype(f32), axis=0)
    normed_back = back_second + dot_nt(inner_back, weight_inner)
    residual_back, first_gain_back, first_shift_back = first_back(normed_back)
    attention_back = residual_back.astype(bf16)
    output_weight_back = dot_tn(out_low, attention_back).astype(bf16)
    out_back = dot_nt(attention_back, weight_output).astype(bf16)

    outer_weight_sum = reduce_gradient(outer_weight_back)
    inner_weight_sum = reduce_gradient(inner_weight_back)
    output_weight_sum = reduce_gradient(output_weight_back)

    query_back, keys_back, values_back, diagonals, small_back = attention_backward(
        stack,
        query_full,
        bias_segment,
        embed,
        row_code,
        key_code,
        keys,
        values,
        table,
        out_back,
        attended,
        log_row,
    )
    table_back = jnp.einsum("hkm,kmc->hc", diagonals, onehot, precision=highest)
    query_weight_back = dot_tn(streams, query_back).astype(bf16)
    key_weight_back = dot_tn(content_all, keys_back).astype(bf16)
    value_weight_back = dot_tn(content_all, values_back).astype(bf16)
    query_weight_sum = reduce_gradient(query_weight_back)
    key_weight_sum = reduce_gradient(key_weight_back)
    value_weight_sum = reduce_gradient(value_weight_back)
    streams_back = residual_back + dot_nt(query_back, weight_query)
    content_share = (dot_nt(keys_back, weight_key) + dot_nt(values_back, weight_value)).astype(bf16)
    content_back = streams_back[:block_rows] + scatter_blocks(content_share)

    small_rows = jnp.concatenate(
        [
            small_back[:4],
            first_gain_back[None],
            first_shift_back[None],
            outer_bias_back[None],
            final_gain_back[None],
            final_shift_back[None],
            inner_bias_back.reshape(-1, width),
            jnp.pad(table_back.reshape(-1), (0, width - head_count * bucket_count))[None],
            jnp.pad(squares, (0, width - 3))[None],
        ],
        axis=0,
    )
    small_sum = sum_everywhere(small_rows)
    shares = lax.dynamic_slice_in_dim(small_sum[:9], side * part, part, 1)
    inner_bias_sum = lax.dynamic_slice_in_dim(
        small_sum[9 : 9 + inner_back.shape[1] // width].reshape(-1),
        side * inner_bias.shape[0],
        inner_bias.shape[0],
        0,
    )
    table_sum = lax.dynamic_slice_in_dim(
        small_sum[-2, : head_count * bucket_count].reshape(head_count, bucket_count),
        side * table_heads,
        table_heads,
        0,
    )
    token_total = length * sides * width
    root_mean = jnp.sqrt(small_sum[-1, :3] / token_total)
    return (
        final_norm[:block_rows].astype(bf16)[None],
        final_norm[block_rows:].astype(bf16)[None],
        content_back[None],
        streams_back[block_rows:][None],
        query_weight_sum,
        key_weight_sum,
        value_weight_sum,
        output_weight_sum,
        shares[0],
        shares[1],
        shares[2:4],
        table_sum,
        shares[4],
        shares[5],
        inner_weight_sum,
        inner_bias_sum,
        outer_weight_sum,
        shares[6],
        shares[7],
        shares[8],
        root_mean,
    )


def solution(mesh):
    tokens = P("wsh", "ctx", None)
    marks = P("wsh", "ctx")
    matrix = P("wsh", None)
    vector = P("wsh")
    placed = (
        (tokens, tokens, marks, marks, marks)
        + (matrix,) * 4
        + (vector, vector, P(None, "wsh"), matrix, vector, vector, matrix, vector, matrix)
        + (vector,) * 3
        + (tokens, tokens)
    )
    given = (
        (tokens,) * 4
        + (matrix,) * 4
        + (vector, vector, P(None, "wsh"), matrix, vector, vector, matrix, vector, matrix)
        + (vector,) * 3
        + (P(),)
    )
    return jax.shard_map(body, mesh=mesh, in_specs=placed, out_specs=given, check_vma=False)
```

```python
import functools

import jax
import jax.numpy as jnp
from jax import lax
from jax.experimental import pallas as pl
from jax.experimental.pallas import tpu as pltpu
from jax.sharding import PartitionSpec as P

negative = -1e30
epsilon = 1e-05
bucket_steps = 16
key_tile = 256
lanes = 128
highest = lax.Precision.HIGHEST
f32 = jnp.float32
bf16 = jnp.bfloat16


def layer_norm(values, gain_row, shift_row):
    centred = values - jnp.mean(values, axis=-1, keepdims=True)
    spread = jnp.mean(centred * centred, axis=-1, keepdims=True)
    return centred * lax.rsqrt(spread + epsilon) * gain_row + shift_row


def gelu_exact(values):
    return jax.nn.gelu(values, approximate=False)


def dot(left, right):
    return jnp.dot(left, right, preferred_element_type=f32)


def dot_nt(left, right):
    return lax.dot_general(left, right, (((1,), (1,)), ((), ())), preferred_element_type=f32)


def dot_tn(left, right):
    return lax.dot_general(left, right, (((0,), (0,)), ((), ())), preferred_element_type=f32)


def partner(value, bit):
    count = lax.axis_size("ctx")
    return lax.ppermute(value, "ctx", [(place, place ^ bit) for place in range(count)])


def across(value):
    return lax.ppermute(value, "wsh", [(0, 1), (1, 0)])


def bits_of(count):
    result = []
    bit = 1
    while bit < count:
        result.append(bit)
        bit *= 2
    return result


def block_order(count):
    order = [0]
    for bit in reversed(bits_of(count)):
        order = order + [place | bit for place in order]
    return order


def gather_blocks(own):
    count = lax.axis_size("ctx")
    bits = bits_of(count)
    if count != 16:
        held = own
        for bit in reversed(bits):
            held = jnp.concatenate([held, partner(held, bit)], axis=0)
        return [held]
    low = bits[1]
    near = partner(own, low)
    first = [own] + [partner(own, place) for place in (bits[3], bits[2], bits[2] | bits[3])]
    second = [near] + [partner(block, low) for block in first[1:]]
    first_core = partner(jnp.concatenate(first, axis=0), 1)
    second_core = partner(jnp.concatenate(second, axis=0), 1)
    return first + second + [first_core, second_core]


def move_kernel(plan, inputs, place_ref, *refs):
    sources, targets = refs[:inputs], refs[inputs:]
    for source, taken, target, put in plan:
        targets[target][put(place_ref)] = sources[source][taken(place_ref)]


def moved(plan, shapes, places, *sources):
    whole = pl.BlockSpec(memory_space=pltpu.VMEM)
    size = sum(shape.size for shape in shapes)
    return pl.pallas_call(
        functools.partial(move_kernel, plan, len(sources)),
        in_specs=[pl.BlockSpec(memory_space=pltpu.SMEM)] + [whole] * len(sources),
        out_specs=[whole] * len(shapes),
        out_shape=shapes,
        compiler_params=pltpu.CompilerParams(vmem_limit_bytes=48 << 20),
        cost_estimate=pl.CostEstimate(flops=0, bytes_accessed=8 * size, transcendentals=0),
    )(places, *sources)


def window(start, rows, left=None, columns=None):
    def make(place_ref):
        first = start
        if isinstance(start, str):
            first = pl.multiple_of(place_ref[int(start)], 16)
        if left is None:
            return (pl.ds(first, rows), slice(None))
        return (pl.ds(first, rows), pl.ds(left, columns))

    return make


def half_rows(places, *shards):
    rows = shards[0].shape[0] // 2
    plan = []
    left = 0
    for at, shard in enumerate(shards):
        columns = shard.shape[1]
        plan.append((at, window("0", rows, 0, columns), 0, window(0, rows, left, columns)))
        left += columns
    return moved(tuple(plan), [jax.ShapeDtypeStruct((rows, left), bf16)], places, *shards)[0]


def whole_rows(places, groups, got, rest, *shards):
    rows = shards[0].shape[0]
    half = rows // 2
    plan = []
    shapes = []
    left = 0
    shard = 0
    for target, group in enumerate(groups):
        across_columns = 0
        for _ in range(group):
            columns = shards[shard].shape[1]
            plan.append(
                (2 + shard, window(0, rows, 0, columns), target, window("1", rows, across_columns, columns))
            )
            for source, place in ((0, "2"), (1, "3")):
                plan.append(
                    (
                        source,
                        window(0, half, left, columns),
                        target,
                        window(place, half, across_columns, columns),
                    )
                )
            left += columns
            across_columns += columns
            shard += 1
        shapes.append(jax.ShapeDtypeStruct((2 * rows, across_columns), bf16))
    return moved(tuple(plan), shapes, places, got, rest, *shards)


def shard_places(rows):
    core = lax.axis_index("ctx") % 2
    side = lax.axis_index("wsh")
    half = rows // 2
    base = (1 - side) * rows
    return jnp.stack(
        [core * half, side * rows, base + core * half, base + (1 - core) * half]
    ).astype(jnp.int32)


def split_bits(count):
    bits = bits_of(count)
    return bits[1:4], bits[4:]


def own_bit(bit):
    if bit == 0:
        return lax.axis_index("wsh")
    return (lax.axis_index("ctx") // bit) % 2


def pass_on(value, bit):
    return across(value) if bit == 0 else partner(value, bit)


def meet(*values):
    return lax.optimization_barrier(values)


def spread(value, bit):
    return jnp.concatenate([value, partner(value, bit)], axis=0)


def piece_places(order, cuts):
    total = len(order)
    place = jnp.arange(1 << total, dtype=jnp.int32)
    result = jnp.zeros_like(place)
    for at, bit in enumerate(order):
        value = ((place >> (total - 1 - at)) & 1) ^ own_bit(bit)
        weight = 1 << len(cuts) if bit == 0 else 1 << (len(cuts) - 1 - cuts.index(bit))
        result = result + value * weight
    return result


def fold(keep, received):
    half = keep.shape[0] // 2
    stays = (keep[:half].astype(f32) + received[:half].astype(f32)).astype(bf16)
    goes = (keep[half:].astype(f32) + received[half:].astype(f32)).astype(bf16)
    return stays, goes


def fold_last(keep, received):
    return (keep.astype(f32) + received.astype(f32)).astype(bf16)


def after(value, *others):
    return lax.optimization_barrier((value,) + others)[0]


def product_kernel(groups, place_ref, *refs):
    operands, (keep_ref, send_ref, total_ref) = refs[: 4 * groups], refs[4 * groups :]
    rows = keep_ref.shape[1]
    step = 256
    left = 0
    for group in range(groups):
        left_own, left_other, right_own, right_other = operands[4 * group : 4 * group + 4]
        columns = right_own.shape[1]
        for start in range(0, left_own.shape[1], step):
            total_ref[start : start + step, left : left + columns] = dot_tn(
                left_own[:, start : start + step], right_own[...]
            ) + dot_tn(left_other[:, start : start + step], right_other[...])
        left += columns
    for at, ref in enumerate((keep_ref, send_ref)):

        @pl.loop(0, ref.shape[0])
        def _(place, at=at, ref=ref):
            block = place_ref[at * ref.shape[0] + place]
            start = pl.multiple_of(block * rows, 8)
            ref[place] = total_ref[pl.ds(start, rows), :].astype(bf16)


def product_pieces(places, *operands):
    groups = len(operands) // 4
    half = places.shape[0] // 2
    height = operands[0].shape[1]
    columns = sum(operands[4 * group + 2].shape[1] for group in range(groups))
    piece = jax.ShapeDtypeStruct((half, height // (2 * half), columns), bf16)
    whole = pl.BlockSpec(memory_space=pltpu.VMEM)
    return pl.pallas_call(
        functools.partial(product_kernel, groups),
        in_specs=[pl.BlockSpec(memory_space=pltpu.SMEM)] + [whole] * len(operands),
        out_specs=[whole, whole],
        out_shape=[piece, piece],
        scratch_shapes=[pltpu.VMEM((height, columns), f32)],
        compiler_params=pltpu.CompilerParams(vmem_limit_bytes=40 << 20),
        cost_estimate=pl.CostEstimate(
            flops=5_000_000_000, bytes_accessed=4 * height * columns, transcendentals=0
        ),
    )(places, *operands)


def cut_kernel(place_ref, *refs):
    parts, (keep_ref, send_ref) = refs[:-2], refs[-2:]
    rows = keep_ref.shape[1]
    for at, ref in enumerate((keep_ref, send_ref)):

        @pl.loop(0, ref.shape[0])
        def _(place, at=at, ref=ref):
            block = place_ref[at * ref.shape[0] + place]
            start = pl.multiple_of(block * rows, 8)
            left = 0
            for part in parts:
                columns = part.shape[1]
                ref[place, :, left : left + columns] = part[pl.ds(start, rows), :].astype(bf16)
                left += columns


def cut_gradient(places, *parts):
    half = places.shape[0] // 2
    columns = sum(part.shape[1] for part in parts)
    piece = jax.ShapeDtypeStruct((half, parts[0].shape[0] // (2 * half), columns), bf16)
    whole = pl.BlockSpec(memory_space=pltpu.VMEM)
    return pl.pallas_call(
        cut_kernel,
        in_specs=[pl.BlockSpec(memory_space=pltpu.SMEM)] + [whole] * len(parts),
        out_specs=[whole, whole],
        out_shape=[piece, piece],
        compiler_params=pltpu.CompilerParams(vmem_limit_bytes=40 << 20),
        cost_estimate=pl.CostEstimate(
            flops=2_000_000_000, bytes_accessed=8 * parts[0].shape[0] * columns, transcendentals=0
        ),
    )(places, *parts)


def lay_out_kernel(plan, place_ref, *refs):
    outputs = len(plan)
    sources, targets = refs[:-outputs], refs[-outputs:]
    for runs, target in zip(plan, targets, strict=True):
        for source, first, columns, column in runs:
            piece_ref = sources[source]
            count, rows = piece_ref.shape[:2]

            @pl.loop(0, count)
            def _(place, piece_ref=piece_ref, rows=rows, target=target, first=first, columns=columns, column=column):
                start = pl.multiple_of(place_ref[place] * rows, 8)
                value = piece_ref[place, :, first : first + columns].astype(f32)
                if column >= 0:
                    target[pl.ds(start, rows), column : column + columns] = value
                else:
                    core = place_ref[count]
                    which = core if column == -1 else 1 - core
                    left = pl.multiple_of(which * columns, lanes)
                    target[pl.ds(start, rows), pl.ds(left, columns)] = value


def lay_out(places, plan, *pieces):
    whole = pl.BlockSpec(memory_space=pltpu.VMEM)
    shapes = []
    for runs in plan:
        count, rows = pieces[runs[0][0]].shape[:2]
        shapes.append(jax.ShapeDtypeStruct((count * rows, sum(run[2] for run in runs)), f32))
    return pl.pallas_call(
        functools.partial(lay_out_kernel, plan),
        in_specs=[pl.BlockSpec(memory_space=pltpu.SMEM)] + [whole] * len(pieces),
        out_specs=[whole] * len(plan),
        out_shape=shapes,
        compiler_params=pltpu.CompilerParams(vmem_limit_bytes=48 << 20),
        cost_estimate=pl.CostEstimate(
            flops=3_000_000_000,
            bytes_accessed=6 * sum(shape.size for shape in shapes),
            transcendentals=0,
        ),
    )(places, *pieces)


def stream_bias(table_ref, head, block):
    spread = jnp.broadcast_to(table_ref[head, pl.ds(block, 1), :], (lanes, 2 * lanes))
    return pltpu.roll(spread, 0, 1, stride=1, stride_axis=0)[:, :lanes]


def tile_bias(table_ref, block):
    parts = []
    for piece in range(key_tile // lanes):
        first = stream_bias(table_ref, 0, block + piece)
        second = stream_bias(table_ref, 1, block + piece)
        parts.append(jnp.concatenate([first, first, second, second], axis=1))
    return jnp.concatenate(parts, axis=0)


def own_mask():
    row = lax.broadcasted_iota(jnp.int32, (key_tile, 4 * lanes), 0)
    column = lax.broadcasted_iota(jnp.int32, (key_tile, 4 * lanes), 1)
    stream = (column // lanes) % 2
    return jnp.where((stream == 1) & (row == column % lanes), negative, 0.0)


def forward_kernel(
    query_ref,
    content_bias_ref,
    segment_bias_ref,
    embed_ref,
    row_code_ref,
    key_code_ref,
    key_ref,
    value_ref,
    table_ref,
    out_ref,
    log_ref,
    stack_ref,
    score_ref,
):
    rows = query_ref.shape[0]
    tiles = key_ref.shape[0] // key_tile
    lane = lax.broadcasted_iota(jnp.int32, (rows, lanes), 1)
    first = lane < lanes // 2
    query = query_ref[...]
    low = (query + content_bias_ref[...]).astype(bf16).astype(f32) * 0.125
    shifted = query + segment_bias_ref[...]
    zero_term = shifted * embed_ref[0:1, :]
    one_term = shifted * embed_ref[1:2, :]
    code = row_code_ref[...]
    for head in range(2):
        own = first if head == 0 else jnp.logical_not(first)
        zero_sum = jnp.sum(jnp.where(own, zero_term, 0.0), axis=1, keepdims=True) * 0.125
        one_sum = jnp.sum(jnp.where(own, one_term, 0.0), axis=1, keepdims=True) * 0.125
        step = zero_sum - one_sum
        step_high = step.astype(bf16).astype(f32)
        step_low = step - step_high
        one_high = one_sum.astype(bf16).astype(f32)
        one_low = one_sum - one_high
        extra = jnp.where(
            lane < 4,
            step_high,
            jnp.where(lane < 8, step_low, jnp.where(lane == 8, one_high, one_low)),
        )
        stack_ref[0, pl.ds(head * rows, rows), 0:lanes] = jnp.where(own, low, 0.0).astype(bf16)
        stack_ref[0, pl.ds(head * rows, rows), lanes : 2 * lanes] = (extra * code).astype(bf16)
    stack = stack_ref[0]

    def scores(tile, top):
        start = pl.multiple_of(tile * key_tile, key_tile)
        keys = jnp.concatenate(
            [key_ref[pl.ds(start, key_tile), :], key_code_ref[pl.ds(start, key_tile), :]], axis=1
        )
        score = dot_nt(keys, stack) + tile_bias(table_ref, tile * (key_tile // lanes))
        if isinstance(tile, int) and tile == 0:
            score = score + own_mask()
        score_ref[pl.ds(start, key_tile), :] = score
        return jnp.maximum(top, jnp.max(score.reshape(key_tile // 8, 8, 4 * lanes), axis=0))

    top = jnp.full((8, 4 * lanes), negative, f32)
    top = scores(0, top)
    top = lax.fori_loop(1, tiles, scores, top, unroll=min(7, tiles - 1))
    peak = jnp.max(top, axis=0, keepdims=True)

    def gathered(tile, running):
        total, mixed = running
        start = pl.multiple_of(tile * key_tile, key_tile)
        weight = jnp.exp(score_ref[pl.ds(start, key_tile), :] - peak)
        total = total + jnp.sum(weight.reshape(key_tile // 8, 8, 4 * lanes), axis=0)
        mixed = mixed + dot_tn(value_ref[pl.ds(start, key_tile), :], weight.astype(bf16))
        return total, mixed

    total, mixed = lax.fori_loop(
        0,
        tiles,
        gathered,
        (jnp.zeros((8, 4 * lanes), f32), jnp.zeros((lanes, 4 * lanes), f32)),
        unroll=min(8, tiles),
    )
    total = jnp.sum(total, axis=0, keepdims=True)
    mixed = mixed / total
    half = lanes // 2
    joined = jnp.concatenate([mixed[:half, :rows], mixed[half:, rows:]], axis=0)
    out_ref[...] = joined.T
    log_ref[0] = peak + jnp.log(total)


def diagonal_sums(square):
    lane = lax.broadcasted_iota(jnp.int32, (8, lanes), 1)
    near = square[0:8]
    far = jnp.zeros((8, lanes), f32)
    for group in range(1, lanes // 8):
        turned = pltpu.roll(square[8 * group : 8 * group + 8], lanes - 8 * group, 1)
        inside = lane < lanes - 8 * group
        near = near + jnp.where(inside, turned, 0.0)
        far = far + jnp.where(inside, 0.0, turned)
    both = jnp.concatenate([near, far], axis=1)
    row = lax.broadcasted_iota(jnp.int32, (8, 2 * lanes), 0)
    for bit in (1, 2, 4):
        both = jnp.where((row // bit) % 2 == 1, pltpu.roll(both, 2 * lanes - bit, 1), both)
    return jnp.sum(both, axis=0, keepdims=True)


def backward_kernel(
    stack_ref,
    query_ref,
    segment_bias_ref,
    embed_ref,
    row_code_ref,
    key_code_ref,
    key_ref,
    value_ref,
    table_ref,
    out_back_ref,
    attended_ref,
    log_ref,
    query_back_ref,
    key_back_ref,
    value_back_ref,
    diagonal_ref,
    small_ref,
):
    rows = query_ref.shape[0]
    tiles = key_ref.shape[0] // key_tile
    half = lanes // 2
    lane = lax.broadcasted_iota(jnp.int32, (rows, lanes), 1)
    first = lane < half
    out_back = out_back_ref[...]
    product = (out_back.astype(f32) * attended_ref[...]).T
    delta = jnp.concatenate(
        [
            jnp.sum(product[:half], axis=0, keepdims=True),
            jnp.sum(product[half:], axis=0, keepdims=True),
        ],
        axis=1,
    )
    zeros = jnp.zeros_like(out_back)
    back_stack = jnp.concatenate(
        [jnp.where(first, out_back, zeros), jnp.where(first, zeros, out_back)], axis=0
    )
    stack = stack_ref[0]
    query_stack = stack[:, :lanes]
    log_row = log_ref[0]

    def step(tile, running):
        start = pl.multiple_of(tile * key_tile, key_tile)
        block = tile * (key_tile // lanes)
        keys = jnp.concatenate(
            [key_ref[pl.ds(start, key_tile), :], key_code_ref[pl.ds(start, key_tile), :]], axis=1
        )
        score = dot_nt(keys, stack) + tile_bias(table_ref, block)
        if isinstance(tile, int) and tile == 0:
            score = score + own_mask()
        weight = jnp.exp(score - log_row)
        weight_back = dot_nt(value_ref[pl.ds(start, key_tile), :], back_stack)
        score_back = weight * (weight_back - delta)
        score_low = score_back.astype(bf16)
        value_back_ref[pl.ds(start, key_tile), :] = dot(weight.astype(bf16), back_stack).astype(
            bf16
        )
        key_back_ref[pl.ds(start, key_tile), :] = dot(score_low, query_stack).astype(bf16)
        for head in range(2):
            for piece in range(key_tile // lanes):
                part = score_back[
                    piece * lanes : (piece + 1) * lanes, head * rows : (head + 1) * rows
                ]
                square = part[:, :lanes] + part[:, lanes:]
                diagonal_ref[head, pl.ds(block + piece, 1), :] = diagonal_sums(square)
        return running + dot_tn(keys, score_low)

    running = step(0, jnp.zeros((2 * lanes, 2 * rows), f32))
    running = lax.fori_loop(1, tiles, step, running, unroll=min(7, tiles - 1))
    joined = jnp.concatenate([running[:half, :rows], running[half:lanes, rows:]], axis=0).T * 0.125
    shifted = query_ref[...] + segment_bias_ref[...]
    code = row_code_ref[...]
    zero_columns = []
    one_columns = []
    for head in range(2):
        part = running[lanes:, head * rows : (head + 1) * rows].T * 0.125
        same = jnp.sum(jnp.where(lane < 4, part * code, 0.0), axis=1, keepdims=True)
        total = jnp.sum(jnp.where(lane == 8, part, 0.0), axis=1, keepdims=True)
        zero_columns.append(same)
        one_columns.append(total - same)
    zero_back = jnp.where(first, zero_columns[0], zero_columns[1])
    one_back = jnp.where(first, one_columns[0], one_columns[1])
    shift_back = zero_back * embed_ref[0:1, :] + one_back * embed_ref[1:2, :]
    query_back_ref[...] = (joined + shift_back).astype(bf16)
    small_ref[0:1, :] = jnp.sum(joined, axis=0, keepdims=True)
    small_ref[1:2, :] = jnp.sum(shift_back, axis=0, keepdims=True)
    small_ref[2:3, :] = jnp.sum(zero_back * shifted, axis=0, keepdims=True)
    small_ref[3:4, :] = jnp.sum(one_back * shifted, axis=0, keepdims=True)
    small_ref[4:8, :] = jnp.zeros((4, lanes), f32)


def attention_specs(rows, keys, blocks, first_pair=0, values_at=0):
    column = lambda pair: (0, pair + first_pair)
    fixed = lambda pair: (0, 0)
    front = lambda pair: (pair + first_pair, 0, 0)
    return {
        "rows": pl.BlockSpec((rows, lanes), column),
        "row": pl.BlockSpec((1, lanes), column),
        "embed": pl.BlockSpec((2, lanes), column),
        "small": pl.BlockSpec((8, lanes), column),
        "row_code": pl.BlockSpec((rows, lanes), fixed),
        "key_code": pl.BlockSpec((keys, lanes), fixed, pipeline_mode=pl.Buffered(1)),
        "keys": pl.BlockSpec((keys, lanes), column),
        "values": pl.BlockSpec((keys, lanes), lambda pair: (0, pair + first_pair + values_at)),
        "table": pl.BlockSpec((2, blocks, 2 * lanes), front),
        "log": pl.BlockSpec((1, 1, 2 * rows), front),
        "stack": pl.BlockSpec((1, 2 * rows, 2 * lanes), front),
    }


def attention_forward(query_full, bias_content, bias_segment, embed, row_code, key_code, both, table):
    rows, width = query_full.shape
    count = both.shape[0]
    pairs = width // lanes
    spec = attention_specs(rows, count, count // lanes, 0, pairs)
    return pl.pallas_call(
        forward_kernel,
        grid=(pairs,),
        in_specs=[
            spec["rows"],
            spec["row"],
            spec["row"],
            spec["embed"],
            spec["row_code"],
            spec["key_code"],
            spec["keys"],
            spec["values"],
            spec["table"],
        ],
        out_specs=[spec["rows"], spec["log"], spec["stack"]],
        out_shape=[
            jax.ShapeDtypeStruct((rows, width), f32),
            jax.ShapeDtypeStruct((pairs, 1, 2 * rows), f32),
            jax.ShapeDtypeStruct((pairs, 2 * rows, 2 * lanes), bf16),
        ],
        scratch_shapes=[pltpu.VMEM((count, 2 * rows), f32)],
        compiler_params=pltpu.CompilerParams(
            dimension_semantics=("arbitrary",), vmem_limit_bytes=60 << 20
        ),
        cost_estimate=pl.CostEstimate(
            flops=40 * rows * count * width,
            bytes_accessed=4 * count * width + 8 * rows * width,
            transcendentals=rows * count * width // 64,
        ),
    )(query_full, bias_content, bias_segment, embed, row_code, key_code, both, both, table)


def attention_backward(first_pair, pairs, operands):
    query_full, both = operands[1], operands[6]
    rows, width = query_full.shape
    count = both.shape[0]
    spec = attention_specs(rows, count, count // lanes, first_pair, width // lanes)
    made = attention_specs(rows, count, count // lanes)
    columns = pairs * lanes
    return pl.pallas_call(
        backward_kernel,
        grid=(pairs,),
        in_specs=[
            spec["stack"],
            spec["rows"],
            spec["row"],
            spec["embed"],
            spec["row_code"],
            spec["key_code"],
            spec["keys"],
            spec["values"],
            spec["table"],
            spec["rows"],
            spec["rows"],
            spec["log"],
        ],
        out_specs=[made["rows"], made["keys"], made["keys"], made["table"], made["small"]],
        out_shape=[
            jax.ShapeDtypeStruct((rows, columns), bf16),
            jax.ShapeDtypeStruct((count, columns), bf16),
            jax.ShapeDtypeStruct((count, columns), bf16),
            jax.ShapeDtypeStruct((2 * pairs, count // lanes, 2 * lanes), f32),
            jax.ShapeDtypeStruct((8, columns), f32),
        ],
        compiler_params=pltpu.CompilerParams(
            dimension_semantics=("arbitrary",), vmem_limit_bytes=60 << 20
        ),
        cost_estimate=pl.CostEstimate(
            flops=40 * rows * count * columns,
            bytes_accessed=8 * count * columns + 8 * rows * columns,
            transcendentals=rows * count * columns // 64,
        ),
    )(*operands)


def marks_kernel(bound_list, meta_ref, table_ref, key_code_ref, bias_ref, number_ref, row_code_ref):
    blocks = meta_ref.shape[0]
    info = meta_ref[:, 0, :].astype(f32)
    segment = info[:, :lanes]
    rank = info[:, lanes : lanes + 1]
    first = info[:, lanes + 1 : lanes + 2] * lanes + info[:, lanes + 2 : lanes + 3]
    turn = lax.broadcasted_iota(jnp.int32, (blocks, 2 * lanes), 1)
    turn = jnp.where(turn < lanes, turn, turn - 2 * lanes)
    distance = (first[0:1, :] - first).astype(jnp.int32) + turn
    number = jnp.full(distance.shape, bucket_steps, jnp.int32)
    for bound in bound_list:
        number = number + (distance >= bound).astype(jnp.int32) - (distance <= -bound).astype(jnp.int32)
    number_ref[...] = number
    hidden = rank > rank[0:1, :]
    for head in range(bias_ref.shape[0]):
        value = jnp.zeros((blocks, 2 * lanes), f32)
        for bucket in range(2 * bucket_steps + 1):
            value = jnp.where(number == bucket, table_ref[head, bucket], value)
        bias_ref[head] = jnp.where(hidden, negative, value)
    lane = lax.broadcasted_iota(jnp.int32, (lanes, lanes), 1)
    code = (lane % 4).astype(f32)
    for block in range(blocks):
        column = jnp.broadcast_to(segment[block : block + 1, :], (lanes, lanes)).T
        marked = jnp.where(
            lane < 8, jnp.where(column == code, 1.0, 0.0), jnp.where(lane < 10, 1.0, 0.0)
        )
        key_code_ref[block * lanes : (block + 1) * lanes, :] = marked.astype(bf16)
        if block == 0:
            row_code_ref[:lanes, :] = marked
            row_code_ref[lanes:, :] = marked


def key_marks(meta_all, table_full, length):
    blocks = meta_all.shape[0]
    heads = table_full.shape[0]
    bounds = tuple(
        1 + level * level * length // (bucket_steps * bucket_steps) for level in range(bucket_steps)
    )
    whole = pl.BlockSpec(memory_space=pltpu.VMEM)
    scalars = pl.BlockSpec(memory_space=pltpu.SMEM)
    return pl.pallas_call(
        functools.partial(marks_kernel, bounds),
        in_specs=[whole, scalars],
        out_specs=[whole] * 4,
        out_shape=[
            jax.ShapeDtypeStruct((blocks * lanes, lanes), bf16),
            jax.ShapeDtypeStruct((heads, blocks, 2 * lanes), f32),
            jax.ShapeDtypeStruct((blocks, 2 * lanes), jnp.int32),
            jax.ShapeDtypeStruct((2 * lanes, lanes), f32),
        ],
        compiler_params=pltpu.CompilerParams(vmem_limit_bytes=40 << 20),
        cost_estimate=pl.CostEstimate(
            flops=3_000_000_000, bytes_accessed=4 * blocks * lanes * lanes, transcendentals=0
        ),
    )(meta_all, table_full)


def body(
    content,
    query_stream,
    block_rank,
    segments,
    positions,
    query_weight,
    key_weight,
    value_weight,
    output_weight,
    content_bias,
    segment_bias,
    segment_embed,
    relative_table,
    attention_gain,
    attention_shift,
    inner_weight,
    inner_bias,
    outer_weight,
    outer_bias,
    final_gain,
    final_shift,
    content_cotangent,
    query_cotangent,
):
    block_rows = content.shape[1]
    width = content.shape[2]
    rows = 2 * block_rows
    count = lax.axis_size("ctx")
    sides = lax.axis_size("wsh")
    side = lax.axis_index("wsh")
    core = lax.axis_index("ctx") % 2
    length = block_rows * count
    own_content = content[0]
    own_query = query_stream[0]
    part = width // sides
    table_heads, bucket_count = relative_table.shape
    head_count = table_heads * sides
    inner_rows = inner_bias.shape[0] // part
    low = 2

    first_places = shard_places(query_weight.shape[0])
    first_sent = half_rows(first_places, query_weight, key_weight, value_weight)
    first_got = across(first_sent)
    mark_rows = 16
    marks = jnp.concatenate(
        [
            segments[0].astype(bf16),
            block_rank[0].astype(bf16),
            (positions[0, :1] // lanes).astype(bf16),
            (positions[0, :1] % lanes).astype(bf16),
        ]
    )
    marks = jnp.pad(marks[None], ((0, mark_rows - 1), (0, width - marks.shape[0])))
    block = jnp.concatenate([own_content, marks], axis=0)
    gathered = gather_blocks(block)
    small = jnp.concatenate(
        [
            content_bias,
            segment_bias,
            attention_gain,
            attention_shift,
            outer_bias,
            final_gain,
            final_shift,
            segment_embed.reshape(-1),
            inner_bias,
            relative_table.reshape(-1),
        ]
    )
    small_height = 16
    small = jnp.pad(small, (0, small_height * part - small.shape[0])).reshape(small_height, part)
    small_other = across(small)
    first_rest = partner(first_got, 1)
    second_sent = after(half_rows(first_places, output_weight, inner_weight), first_got)
    second_got = across(second_sent)
    third_places = shard_places(outer_weight.shape[0])
    third_sent = after(half_rows(third_places, outer_weight), second_got)
    third_got = across(third_sent)

    small_pair = jnp.where(
        side == 0,
        jnp.concatenate([small, small_other], axis=1),
        jnp.concatenate([small_other, small], axis=1),
    ).astype(f32)
    bias_content = small_pair[0:1]
    bias_segment = small_pair[1:2]
    gain_first = small_pair[2]
    shift_first = small_pair[3]
    bias_outer = small_pair[4]
    gain_second = small_pair[5]
    shift_second = small_pair[6]
    embed = small_pair[7:9]
    bias_inner = jnp.concatenate(
        [
            small_pair[9 : 9 + inner_rows, :part].reshape(-1),
            small_pair[9 : 9 + inner_rows, part:].reshape(-1),
        ]
    )
    table_row = small_pair[9 + inner_rows]
    table_full = jnp.concatenate(
        [
            table_row[: table_heads * bucket_count],
            table_row[part : part + table_heads * bucket_count],
        ]
    ).reshape(head_count, bucket_count)

    held = block_rows + mark_rows
    if len(gathered) == 1:
        stacked = gathered[0].reshape(count, held, width)
        content_all = stacked[:, :block_rows].reshape(length, width)
        meta_all = stacked[:, block_rows:]
    else:
        plan = []
        place = 0
        for at, piece in enumerate(gathered):
            for row in range(0, piece.shape[0], held):
                plan.append(
                    (at, window(row, block_rows), 0, window(place * block_rows, block_rows))
                )
                plan.append(
                    (at, window(row + block_rows, mark_rows), 1, window(place * mark_rows, mark_rows))
                )
                place += 1
        content_all, meta_all = moved(
            tuple(plan),
            [
                jax.ShapeDtypeStruct((length, width), bf16),
                jax.ShapeDtypeStruct((count * mark_rows, width), bf16),
            ],
            first_places,
            *gathered,
        )
        meta_all = meta_all.reshape(count, mark_rows, width)
    weight_query, weight_both = whole_rows(
        first_places, (1, 2), first_got, first_rest, query_weight, key_weight, value_weight
    )
    weight_key = weight_both[:, :width]
    weight_value = weight_both[:, width:]
    key_code, table, number, row_code = key_marks(meta_all, table_full, length)

    streams = jnp.concatenate([own_content, own_query], axis=0)
    query_full = dot(streams, weight_query)
    both = dot(content_all, weight_both).astype(bf16)
    attended, log_row, stack = attention_forward(
        query_full, bias_content, bias_segment, embed, row_code, key_code, both, table
    )

    second_rest = partner(second_got, 1)
    weight_output, weight_inner = whole_rows(
        first_places, (1, 1), second_got, second_rest, output_weight, inner_weight
    )
    third_rest = partner(third_got, 1)
    (weight_outer,) = whole_rows(third_places, (1,), third_got, third_rest, outer_weight)

    out_low = attended.astype(bf16)
    out_low_other = partner(out_low, 1)
    attention_out = dot(out_low, weight_output)
    residual = streams.astype(f32) + attention_out
    normed, first_back = jax.vjp(layer_norm, residual, gain_first, shift_first)
    normed_low = normed.astype(bf16)
    normed_other = partner(normed_low, 1)
    inner_pre = dot(normed_low, weight_inner) + bias_inner
    active, gelu_back = jax.vjp(gelu_exact, inner_pre)
    active_low = active.astype(bf16)
    active_other = partner(active_low, 1)
    outer_out = dot(active_low, weight_outer) + bias_outer
    final_norm, second_back = jax.vjp(layer_norm, normed + outer_out, gain_second, shift_second)
    squares = jnp.stack(
        [
            jnp.sum(jnp.square(own_content.astype(f32))),
            jnp.sum(jnp.square(attention_out[:block_rows])),
            jnp.sum(jnp.square(residual[:block_rows])),
        ]
    )
    cotangent = jnp.concatenate([content_cotangent[0], query_cotangent[0]], axis=0).astype(f32)
    back_second, final_gain_back, final_shift_back = second_back(cotangent)
    outer_back = back_second.astype(bf16)

    cuts, extra = split_bits(count)
    wide_cuts = [1] + cuts
    order_one = [0] + cuts
    order_two = cuts[:1] + [0] + cuts[1:]
    places_one = piece_places(order_one, cuts)
    places_two = piece_places(order_two, cuts)
    wide_places = piece_places([1, 0] + cuts, wide_cuts)
    places_out = jnp.concatenate([piece_places(cuts, cuts), core[None].astype(jnp.int32)])
    wide_places_out = piece_places(wide_cuts, wide_cuts)

    def core_halves(value):
        columns = value.shape[1] // 2
        kept = lax.dynamic_slice_in_dim(value, core * columns, columns, 1)
        sent = lax.dynamic_slice_in_dim(value, (1 - core) * columns, columns, 1)
        return kept, partner(sent, 1)

    outer_kept, outer_other = core_halves(outer_back)
    outer_bias_back = jnp.sum(outer_back.astype(f32), axis=0)
    active_back = dot_nt(outer_back, weight_outer)
    inner_back = gelu_back(active_back)[0].astype(bf16)
    outer_keep, outer_send = product_pieces(
        places_one, active_low, after(active_other, active_back), outer_kept, outer_other
    )
    outer_got = pass_on(outer_send, order_one[0])
    inner_kept, inner_other = core_halves(inner_back)
    inner_bias_back = jnp.sum(inner_back.astype(f32), axis=0)
    normed_back = back_second + dot_nt(inner_back, weight_inner)
    residual_back, first_gain_back, first_shift_back = first_back(normed_back)
    attention_back = residual_back.astype(bf16)
    attention_kept, attention_other = core_halves(attention_back)
    out_back = dot_nt(attention_back, weight_output).astype(bf16)
    inner_keep, inner_send = product_pieces(
        places_two,
        normed_low,
        normed_other,
        inner_kept,
        inner_other,
        out_low,
        out_low_other,
        attention_kept,
        attention_other,
    )
    inner_got = pass_on(inner_send, order_two[0])

    pairs = width // lanes
    operands = (
        stack,
        query_full,
        bias_segment,
        embed,
        row_code,
        key_code,
        both,
        both,
        table,
        out_back,
        attended,
        log_row,
    )

    def run(first, number_of, *waits):
        waiting = after(out_back, *waits)
        return attention_backward(first, number_of, operands[:9] + (waiting,) + operands[10:])

    def weight_parts(*results):
        def joined(at):
            parts = [result[at] for result in results]
            return parts[0] if len(parts) == 1 else jnp.concatenate(parts, axis=1)

        query_part, key_part, value_part = joined(0), joined(1), joined(2)
        return (
            dot_tn(streams, query_part),
            dot_tn(content_all, key_part),
            dot_tn(content_all, value_part),
        )

    results = [run(0, 1, outer_send, inner_send)]
    outer_got, _ = meet(outer_got, results[0][0])
    outer_keep, outer_send = fold(outer_keep, outer_got)
    outer_got = pass_on(outer_send, order_one[1])
    results.append(run(1, 2, outer_send))
    outer_got, inner_got, _ = meet(outer_got, inner_got, results[1][0])
    outer_keep, outer_send = fold(outer_keep, outer_got)
    outer_got = pass_on(outer_send, order_one[2])
    inner_keep, inner_send = fold(inner_keep, inner_got)
    inner_got = pass_on(inner_send, order_two[1])
    results.append(run(3, 1, outer_send, inner_send))
    early_keep, early_send = cut_gradient(wide_places, *weight_parts(*results))
    early_got = pass_on(early_send, 1)
    outer_got, inner_got, _ = meet(outer_got, inner_got, results[2][0])
    outer_keep, outer_send = fold(outer_keep, outer_got)
    outer_got = pass_on(outer_send, order_one[3])
    inner_keep, inner_send = fold(inner_keep, inner_got)
    inner_got = pass_on(inner_send, order_two[2])
    results.append(run(4, 1, outer_send, inner_send, early_send))
    outer_got, inner_got, early_got, _ = meet(outer_got, inner_got, early_got, results[3][0])

    def add_extra(value):
        for bit in extra:
            value = fold_last(value, partner(value, bit))
        return value

    outer_value = add_extra(fold_last(outer_keep, outer_got))
    outer_got = partner(outer_value, cuts[2])
    inner_keep, inner_send = fold(inner_keep, inner_got)
    inner_got = pass_on(inner_send, order_two[3])
    early_keep, early_send = fold(early_keep, early_got)
    early_got = pass_on(early_send, 0)
    results.append(run(5, pairs - 5, outer_value, inner_send, early_send))
    late_keep, late_send = cut_gradient(wide_places, *weight_parts(*results[3:]))
    late_got = pass_on(late_send, 1)
    outer_got, inner_got, early_got, _ = meet(outer_got, inner_got, early_got, results[4][0])
    outer_value = jnp.concatenate([outer_value, outer_got], axis=0)
    outer_got = partner(outer_value, cuts[1])
    inner_value = add_extra(fold_last(inner_keep, inner_got))
    inner_got = partner(inner_value, cuts[2])
    early_keep, early_send = fold(early_keep, early_got)
    early_got = pass_on(early_send, cuts[0])

    query_back = jnp.concatenate([result[0] for result in results], axis=1)
    keys_back = jnp.concatenate([result[1] for result in results], axis=1)
    values_back = jnp.concatenate([result[2] for result in results], axis=1)
    diagonals = jnp.concatenate([result[3] for result in results], axis=0)
    small_back = jnp.concatenate([result[4] for result in results], axis=1)
    onehot = (number[:, :, None] == jnp.arange(bucket_count, dtype=jnp.int32)).astype(f32)
    table_back = jnp.einsum("hkm,kmc->hc", diagonals, onehot, precision=highest)
    content_share = (dot_nt(keys_back, weight_key) + dot_nt(values_back, weight_value)).astype(bf16)
    share_bits = bits_of(count)
    share_keep, share_got = content_share[: length // 2], partner(content_share[length // 2 :], 1)
    small_rows = jnp.concatenate(
        [
            small_back[:4],
            first_gain_back[None],
            first_shift_back[None],
            outer_bias_back[None],
            final_gain_back[None],
            final_shift_back[None],
            inner_bias_back.reshape(-1, width),
            jnp.pad(table_back.reshape(-1), (0, width - head_count * bucket_count))[None],
            jnp.pad(squares, (0, width - 3))[None],
        ],
        axis=0,
    )
    small_got = across(small_rows)

    outer_got, inner_got, early_got, late_got, share_got, small_got = meet(
        outer_got, inner_got, early_got, late_got, share_got, small_got
    )
    outer_value = jnp.concatenate([outer_value, outer_got], axis=0)
    outer_got = partner(outer_value, cuts[0])
    inner_value = jnp.concatenate([inner_value, inner_got], axis=0)
    inner_got = partner(inner_value, cuts[1])
    early_keep, early_send = fold(early_keep, early_got)
    early_got = pass_on(early_send, cuts[1])
    late_keep, late_send = fold(late_keep, late_got)
    late_got = pass_on(late_send, 0)
    share_keep, share_send = fold(share_keep, share_got)
    share_got = partner(share_send, share_bits[1])
    small_rows = small_rows + small_got
    small_got = partner(small_rows, 1)
    outer_got, inner_got, early_got, late_got, share_got, small_got = meet(
        outer_got, inner_got, early_got, late_got, share_got, small_got
    )
    outer_value = jnp.concatenate([outer_value, outer_got], axis=0)
    outer_got = partner(outer_value, 1)
    inner_value = jnp.concatenate([inner_value, inner_got], axis=0)
    inner_got = partner(inner_value, cuts[0])
    early_keep, early_send = fold(early_keep, early_got)
    early_got = pass_on(early_send, cuts[2])
    late_keep, late_send = fold(late_keep, late_got)
    late_got = pass_on(late_send, cuts[0])
    share_keep, share_send = fold(share_keep, share_got)
    share_got = partner(share_send, share_bits[2])
    small_rows = small_rows + small_got
    small_got = partner(small_rows, share_bits[1])
    outer_got, inner_got, early_got, late_got, share_got, small_got = meet(
        outer_got, inner_got, early_got, late_got, share_got, small_got
    )
    hidden = inner_back.shape[1]
    inner_value = jnp.concatenate([inner_value, inner_got], axis=0)
    inner_got = partner(inner_value, 1)
    early_value = add_extra(fold_last(early_keep, early_got))
    early_got = partner(early_value, cuts[2])
    late_keep, late_send = fold(late_keep, late_got)
    late_got = pass_on(late_send, cuts[1])
    share_keep, share_send = fold(share_keep, share_got)
    share_got = partner(share_send, share_bits[3])
    small_rows = small_rows + small_got
    small_got = partner(small_rows, share_bits[2])
    (outer_weight_sum,) = lay_out(
        places_out,
        (((0, 0, width // 2, -1), (1, 0, width // 2, -2)),),
        after(outer_value, early_value),
        outer_got,
    )
    inner_got, early_got, late_got, share_got, small_got = meet(
        inner_got, early_got, late_got, share_got, small_got
    )
    early_value = jnp.concatenate([early_value, early_got], axis=0)
    early_got = partner(early_value, cuts[1])
    late_keep, late_send = fold(late_keep, late_got)
    late_got = pass_on(late_send, cuts[2])
    small_rows = small_rows + small_got
    small_got = partner(small_rows, share_bits[3])
    for bit in share_bits[4:]:
        share_keep, share_send = fold(share_keep, share_got)
        share_got = partner(share_send, bit)
    streams_back = residual_back + dot_nt(query_back, weight_query)
    content_back = (
        streams_back[:block_rows] + share_keep.astype(f32) + share_got.astype(f32)
    )
    inner_weight_sum, output_weight_sum = lay_out(
        places_out,
        (
            ((0, 0, hidden // 2, -1), (1, 0, hidden // 2, -2)),
            ((0, hidden // 2, width // 2, -1), (1, hidden // 2, width // 2, -2)),
        ),
        after(inner_value, early_value),
        inner_got,
    )
    early_got, late_got, small_got = meet(early_got, late_got, small_got)
    early_value = jnp.concatenate([early_value, early_got], axis=0)
    early_got = partner(early_value, cuts[0])
    late_value = add_extra(fold_last(late_keep, late_got))
    late_got = partner(late_value, cuts[2])
    small_rows = small_rows + small_got
    for bit in share_bits[4:]:
        small_rows = small_rows + partner(small_rows, bit)
    early_got, late_got = meet(early_got, late_got)
    early_value = jnp.concatenate([early_value, early_got], axis=0)
    early_value = jnp.concatenate([early_value, partner(early_value, 1)], axis=0)
    late_value = jnp.concatenate([late_value, late_got], axis=0)
    late_value = spread(late_value, cuts[1])
    late_value = spread(late_value, cuts[0])
    late_value = spread(late_value, 1)
    early_columns = 4 * lanes
    late_columns = width - early_columns
    plan = tuple(
        (
            (0, early_columns * kind, early_columns, 0),
            (1, late_columns * kind, late_columns, early_columns),
        )
        for kind in range(3)
    )
    query_weight_sum, key_weight_sum, value_weight_sum = lay_out(
        wide_places_out, plan, early_value, late_value
    )

    shares = lax.dynamic_slice_in_dim(small_rows[:9], side * part, part, 1)
    inner_bias_sum = lax.dynamic_slice_in_dim(
        small_rows[9 : 9 + hidden // width].reshape(-1),
        side * inner_bias.shape[0],
        inner_bias.shape[0],
        0,
    )
    table_sum = lax.dynamic_slice_in_dim(
        small_rows[-2, : head_count * bucket_count].reshape(head_count, bucket_count),
        side * table_heads,
        table_heads,
        0,
    )
    token_total = length * sides * width
    root_mean = jnp.sqrt(small_rows[-1, :3] / token_total)
    return (
        final_norm[:block_rows].astype(bf16)[None],
        final_norm[block_rows:].astype(bf16)[None],
        content_back[None],
        streams_back[block_rows:][None],
        query_weight_sum,
        key_weight_sum,
        value_weight_sum,
        output_weight_sum,
        shares[0],
        shares[1],
        shares[2:4],
        table_sum,
        shares[4],
        shares[5],
        inner_weight_sum,
        inner_bias_sum,
        outer_weight_sum,
        shares[6],
        shares[7],
        shares[8],
        root_mean,
    )


def solution(mesh):
    tokens = P("wsh", "ctx", None)
    marks = P("wsh", "ctx")
    matrix = P("wsh", None)
    vector = P("wsh")
    placed = (
        (tokens, tokens, marks, marks, marks)
        + (matrix,) * 4
        + (vector, vector, P(None, "wsh"), matrix, vector, vector, matrix, vector, matrix)
        + (vector,) * 3
        + (tokens, tokens)
    )
    given = (
        (tokens,) * 4
        + (matrix,) * 4
        + (vector, vector, P(None, "wsh"), matrix, vector, vector, matrix, vector, matrix)
        + (vector,) * 3
        + (P(),)
    )
    return jax.shard_map(body, mesh=mesh, in_specs=placed, out_specs=given, check_vma=False)
```

```python
import functools

import jax
import jax.numpy as jnp
from jax import lax
from jax.experimental import pallas as pl
from jax.experimental.pallas import tpu as pltpu
from jax.sharding import PartitionSpec as P

negative = -1e30
epsilon = 1e-05
bucket_steps = 16
key_tile = 256
lanes = 128
highest = lax.Precision.HIGHEST
f32 = jnp.float32
bf16 = jnp.bfloat16


def layer_norm(values, gain_row, shift_row):
    centred = values - jnp.mean(values, axis=-1, keepdims=True)
    spread = jnp.mean(centred * centred, axis=-1, keepdims=True)
    return centred * lax.rsqrt(spread + epsilon) * gain_row + shift_row


def gelu_exact(values):
    return jax.nn.gelu(values, approximate=False)


def dot(left, right):
    return jnp.dot(left, right, preferred_element_type=f32)


def dot_nt(left, right):
    return lax.dot_general(left, right, (((1,), (1,)), ((), ())), preferred_element_type=f32)


def dot_tn(left, right):
    return lax.dot_general(left, right, (((0,), (0,)), ((), ())), preferred_element_type=f32)


def partner(value, bit):
    count = lax.axis_size("ctx")
    return lax.ppermute(value, "ctx", [(place, place ^ bit) for place in range(count)])


def across(value):
    return lax.ppermute(value, "wsh", [(0, 1), (1, 0)])


def bits_of(count):
    result = []
    bit = 1
    while bit < count:
        result.append(bit)
        bit *= 2
    return result


def block_order(count):
    order = [0]
    for bit in reversed(bits_of(count)):
        order = order + [place | bit for place in order]
    return order


def gather_blocks(own):
    count = lax.axis_size("ctx")
    bits = bits_of(count)
    if count != 16:
        held = own
        for bit in reversed(bits):
            held = jnp.concatenate([held, partner(held, bit)], axis=0)
        return [held]
    low = bits[1]
    near = partner(own, low)
    first = [own] + [partner(own, place) for place in (bits[3], bits[2], bits[2] | bits[3])]
    second = [near] + [partner(block, low) for block in first[1:]]
    first_core = partner(jnp.concatenate(first, axis=0), 1)
    second_core = partner(jnp.concatenate(second, axis=0), 1)
    return first + second + [first_core, second_core]


def move_kernel(plan, inputs, place_ref, *refs):
    sources, targets = refs[:inputs], refs[inputs:]
    for source, taken, target, put in plan:
        targets[target][put(place_ref)] = sources[source][taken(place_ref)]


def moved(plan, shapes, places, *sources):
    whole = pl.BlockSpec(memory_space=pltpu.VMEM)
    size = sum(shape.size for shape in shapes)
    return pl.pallas_call(
        functools.partial(move_kernel, plan, len(sources)),
        in_specs=[pl.BlockSpec(memory_space=pltpu.SMEM)] + [whole] * len(sources),
        out_specs=[whole] * len(shapes),
        out_shape=shapes,
        compiler_params=pltpu.CompilerParams(vmem_limit_bytes=48 << 20),
        cost_estimate=pl.CostEstimate(flops=0, bytes_accessed=8 * size, transcendentals=0),
    )(places, *sources)


def window(start, rows, left=None, columns=None):
    def make(place_ref):
        first = start
        if isinstance(start, str):
            first = pl.multiple_of(place_ref[int(start)], 16)
        if left is None:
            return (pl.ds(first, rows), slice(None))
        return (pl.ds(first, rows), pl.ds(left, columns))

    return make


def half_rows(places, *shards):
    rows = shards[0].shape[0] // 2
    plan = []
    left = 0
    for at, shard in enumerate(shards):
        columns = shard.shape[1]
        plan.append((at, window("0", rows, 0, columns), 0, window(0, rows, left, columns)))
        left += columns
    return moved(tuple(plan), [jax.ShapeDtypeStruct((rows, left), bf16)], places, *shards)[0]


def whole_rows(places, runs, widths, got, rest, *shards):
    rows = shards[0].shape[0]
    half = rows // 2
    lefts = [0]
    for shard in shards:
        lefts.append(lefts[-1] + shard.shape[1])
    plan = []
    for shard, first, columns, target, column in runs:
        plan.append(
            (2 + shard, window(0, rows, first, columns), target, window("1", rows, column, columns))
        )
        for source, place in ((0, "2"), (1, "3")):
            plan.append(
                (
                    source,
                    window(0, half, lefts[shard] + first, columns),
                    target,
                    window(place, half, column, columns),
                )
            )
    shapes = [jax.ShapeDtypeStruct((2 * rows, width), bf16) for width in widths]
    return moved(tuple(plan), shapes, places, got, rest, *shards)


def shard_places(rows):
    core = lax.axis_index("ctx") % 2
    side = lax.axis_index("wsh")
    half = rows // 2
    base = (1 - side) * rows
    return jnp.stack(
        [core * half, side * rows, base + core * half, base + (1 - core) * half]
    ).astype(jnp.int32)


def split_bits(count):
    bits = bits_of(count)
    return bits[1:4], bits[4:]


def own_bit(bit):
    if bit == 0:
        return lax.axis_index("wsh")
    return (lax.axis_index("ctx") // bit) % 2


def pass_on(value, bit):
    return across(value) if bit == 0 else partner(value, bit)


class Sequence:
    def __init__(self, mark):
        self.mark = mark

    def wait(self, *values):
        *values, self.mark = lax.optimization_barrier(tuple(values) + (self.mark,))
        return values[0] if len(values) == 1 else tuple(values)

    ready = wait


def fold_parts(keep, received, parts):
    size = keep.shape[0] // parts
    return [
        fold_last(keep[at * size : (at + 1) * size], received[at * size : (at + 1) * size])
        for at in range(parts)
    ]


def give_three(parts, bits):
    return [partner(parts[1], bits[1]), partner(parts[2], bits[0]), partner(parts[3], bits[0] | bits[1])]


def share_three(value, bits):
    return [partner(value, bits[1]), partner(value, bits[0]), partner(value, bits[0] | bits[1])]


def fold_all(value, received):
    total = value.astype(f32)
    for part in received:
        total = total + part.astype(f32)
    return total.astype(bf16)


def piled(*values):
    return jnp.concatenate(values, axis=0)


def piece_places(order, cuts):
    total = len(order)
    place = jnp.arange(1 << total, dtype=jnp.int32)
    result = jnp.zeros_like(place)
    for at, bit in enumerate(order):
        value = ((place >> (total - 1 - at)) & 1) ^ own_bit(bit)
        weight = 1 << len(cuts) if bit == 0 else 1 << (len(cuts) - 1 - cuts.index(bit))
        result = result + value * weight
    return result


def fold(keep, received):
    half = keep.shape[0] // 2
    stays = (keep[:half].astype(f32) + received[:half].astype(f32)).astype(bf16)
    goes = (keep[half:].astype(f32) + received[half:].astype(f32)).astype(bf16)
    return stays, goes


def fold_last(keep, received):
    return (keep.astype(f32) + received.astype(f32)).astype(bf16)


def after(value, *others):
    return lax.optimization_barrier((value,) + others)[0]


def product_kernel(groups, place_ref, *refs):
    operands, (keep_ref, send_ref, total_ref) = refs[: 4 * groups], refs[4 * groups :]
    rows = keep_ref.shape[1]
    step = 256
    left = 0
    for group in range(groups):
        left_own, left_other, right_own, right_other = operands[4 * group : 4 * group + 4]
        columns = right_own.shape[1]
        for start in range(0, left_own.shape[1], step):
            total_ref[start : start + step, left : left + columns] = dot_tn(
                left_own[:, start : start + step], right_own[...]
            ) + dot_tn(left_other[:, start : start + step], right_other[...])
        left += columns
    for at, ref in enumerate((keep_ref, send_ref)):

        @pl.loop(0, ref.shape[0])
        def _(place, at=at, ref=ref):
            block = place_ref[at * ref.shape[0] + place]
            start = pl.multiple_of(block * rows, 8)
            ref[place] = total_ref[pl.ds(start, rows), :].astype(bf16)


def product_pieces(places, *operands):
    groups = len(operands) // 4
    half = places.shape[0] // 2
    height = operands[0].shape[1]
    columns = sum(operands[4 * group + 2].shape[1] for group in range(groups))
    piece = jax.ShapeDtypeStruct((half, height // (2 * half), columns), bf16)
    whole = pl.BlockSpec(memory_space=pltpu.VMEM)
    return pl.pallas_call(
        functools.partial(product_kernel, groups),
        in_specs=[pl.BlockSpec(memory_space=pltpu.SMEM)] + [whole] * len(operands),
        out_specs=[whole, whole],
        out_shape=[piece, piece],
        scratch_shapes=[pltpu.VMEM((height, columns), f32)],
        compiler_params=pltpu.CompilerParams(vmem_limit_bytes=40 << 20),
        cost_estimate=pl.CostEstimate(
            flops=5_000_000_000, bytes_accessed=4 * height * columns, transcendentals=0
        ),
    )(places, *operands)


def cut_kernel(place_ref, *refs):
    parts, vector_ref, (keep_ref, send_ref, turned_ref) = refs[:-4], refs[-4], refs[-3:]
    rows = keep_ref.shape[1]
    vectors = vector_ref[...]
    height = vectors.shape[1]
    filled = jnp.concatenate(
        [vectors, jnp.zeros((lanes - vectors.shape[0], height), f32)], axis=0
    )
    for start in range(0, height, lanes):
        turned_ref[start : start + lanes, :] = filled[:, start : start + lanes].T
    parts = parts + (turned_ref,)
    for at, ref in enumerate((keep_ref, send_ref)):

        @pl.loop(0, ref.shape[0])
        def _(place, at=at, ref=ref):
            block = place_ref[at * ref.shape[0] + place]
            start = pl.multiple_of(block * rows, 8)
            left = 0
            for part in parts:
                columns = part.shape[1]
                ref[place, :, left : left + columns] = part[pl.ds(start, rows), :].astype(bf16)
                left += columns


def cut_gradient(places, vectors, *parts):
    half = places.shape[0] // 2
    height = parts[0].shape[0]
    columns = sum(part.shape[1] for part in parts) + lanes
    piece = jax.ShapeDtypeStruct((half, height // (2 * half), columns), bf16)
    whole = pl.BlockSpec(memory_space=pltpu.VMEM)
    return pl.pallas_call(
        cut_kernel,
        in_specs=[pl.BlockSpec(memory_space=pltpu.SMEM)] + [whole] * (len(parts) + 1),
        out_specs=[whole, whole],
        out_shape=[piece, piece],
        scratch_shapes=[pltpu.VMEM((height, lanes), f32)],
        compiler_params=pltpu.CompilerParams(vmem_limit_bytes=40 << 20),
        cost_estimate=pl.CostEstimate(
            flops=3_000_000_000, bytes_accessed=8 * height * columns, transcendentals=0
        ),
    )(places, *parts, vectors)


def lay_out_kernel(plan, place_ref, *refs):
    outputs = len(plan)
    sources, targets = refs[:-outputs], refs[-outputs:]
    halves = 2 if place_ref.shape[0] > sources[0].shape[0] + 1 else 1
    for half in range(halves):
      for runs, target in zip(plan, targets, strict=True):
        for source, first, columns, column in runs:
            piece_ref = sources[source + half]
            count, rows = piece_ref.shape[:2]

            @pl.loop(0, count)
            def _(place, piece_ref=piece_ref, rows=rows, target=target, first=first, columns=columns, column=column, half=half):
                start = pl.multiple_of(place_ref[half * count + place] * rows, 8)
                value = piece_ref[place, :, first : first + columns].astype(f32)
                if column >= 0:
                    target[pl.ds(start, rows), column : column + columns] = value
                else:
                    core = place_ref[count]
                    which = core if column == -1 else 1 - core
                    left = pl.multiple_of(which * columns, lanes)
                    target[pl.ds(start, rows), pl.ds(left, columns)] = value


def lay_out(places, plan, *pieces):
    whole = pl.BlockSpec(memory_space=pltpu.VMEM)
    shapes = []
    halves = 2 if places.shape[0] > pieces[0].shape[0] + 1 else 1
    for runs in plan:
        count, rows = pieces[runs[0][0]].shape[:2]
        shapes.append(jax.ShapeDtypeStruct((halves * count * rows, sum(run[2] for run in runs)), f32))
    return pl.pallas_call(
        functools.partial(lay_out_kernel, plan),
        in_specs=[pl.BlockSpec(memory_space=pltpu.SMEM)] + [whole] * len(pieces),
        out_specs=[whole] * len(plan),
        out_shape=shapes,
        compiler_params=pltpu.CompilerParams(vmem_limit_bytes=48 << 20),
        cost_estimate=pl.CostEstimate(
            flops=3_000_000_000,
            bytes_accessed=6 * sum(shape.size for shape in shapes),
            transcendentals=0,
        ),
    )(places, *pieces)


def stream_bias(table_ref, head, block):
    spread = jnp.broadcast_to(table_ref[head, pl.ds(block, 1), :], (lanes, 2 * lanes))
    return pltpu.roll(spread, 0, 1, stride=1, stride_axis=0)[:, :lanes]


def tile_bias(table_ref, block):
    parts = []
    for piece in range(key_tile // lanes):
        first = stream_bias(table_ref, 0, block + piece)
        second = stream_bias(table_ref, 1, block + piece)
        parts.append(jnp.concatenate([first, first, second, second], axis=1))
    return jnp.concatenate(parts, axis=0)


def own_mask():
    row = lax.broadcasted_iota(jnp.int32, (key_tile, 4 * lanes), 0)
    column = lax.broadcasted_iota(jnp.int32, (key_tile, 4 * lanes), 1)
    stream = (column // lanes) % 2
    return jnp.where((stream == 1) & (row == column % lanes), negative, 0.0)


def forward_kernel(
    query_ref,
    content_bias_ref,
    segment_bias_ref,
    embed_ref,
    row_code_ref,
    key_code_ref,
    both_ref,
    table_ref,
    out_ref,
    log_ref,
    stack_ref,
    score_ref,
):
    rows = query_ref.shape[0]
    tiles = both_ref.shape[0] // key_tile
    lane = lax.broadcasted_iota(jnp.int32, (rows, lanes), 1)
    first = lane < lanes // 2
    query = query_ref[...]
    low = (query + content_bias_ref[...]).astype(bf16).astype(f32) * 0.125
    shifted = query + segment_bias_ref[...]
    zero_term = shifted * embed_ref[0:1, :]
    one_term = shifted * embed_ref[1:2, :]
    code = row_code_ref[...]
    for head in range(2):
        own = first if head == 0 else jnp.logical_not(first)
        zero_sum = jnp.sum(jnp.where(own, zero_term, 0.0), axis=1, keepdims=True) * 0.125
        one_sum = jnp.sum(jnp.where(own, one_term, 0.0), axis=1, keepdims=True) * 0.125
        step = zero_sum - one_sum
        step_high = step.astype(bf16).astype(f32)
        step_low = step - step_high
        one_high = one_sum.astype(bf16).astype(f32)
        one_low = one_sum - one_high
        extra = jnp.where(
            lane < 4,
            step_high,
            jnp.where(lane < 8, step_low, jnp.where(lane == 8, one_high, one_low)),
        )
        stack_ref[0, pl.ds(head * rows, rows), 0:lanes] = jnp.where(own, low, 0.0).astype(bf16)
        stack_ref[0, pl.ds(head * rows, rows), lanes : 2 * lanes] = (extra * code).astype(bf16)
    stack = stack_ref[0]

    def scores(tile, top):
        start = pl.multiple_of(tile * key_tile, key_tile)
        keys = jnp.concatenate(
            [both_ref[pl.ds(start, key_tile), :lanes], key_code_ref[pl.ds(start, key_tile), :]], axis=1
        )
        score = dot_nt(keys, stack) + tile_bias(table_ref, tile * (key_tile // lanes))
        if isinstance(tile, int) and tile == 0:
            score = score + own_mask()
        score_ref[pl.ds(start, key_tile), :] = score
        return jnp.maximum(top, jnp.max(score.reshape(key_tile // 8, 8, 4 * lanes), axis=0))

    top = jnp.full((8, 4 * lanes), negative, f32)
    top = scores(0, top)
    top = lax.fori_loop(1, tiles, scores, top, unroll=min(7, tiles - 1))
    peak = jnp.max(top, axis=0, keepdims=True)

    def gathered(tile, running):
        total, mixed = running
        start = pl.multiple_of(tile * key_tile, key_tile)
        weight = jnp.exp(score_ref[pl.ds(start, key_tile), :] - peak)
        total = total + jnp.sum(weight.reshape(key_tile // 8, 8, 4 * lanes), axis=0)
        mixed = mixed + dot_tn(both_ref[pl.ds(start, key_tile), lanes:], weight.astype(bf16))
        return total, mixed

    total, mixed = lax.fori_loop(
        0,
        tiles,
        gathered,
        (jnp.zeros((8, 4 * lanes), f32), jnp.zeros((lanes, 4 * lanes), f32)),
        unroll=min(8, tiles),
    )
    total = jnp.sum(total, axis=0, keepdims=True)
    mixed = mixed / total
    half = lanes // 2
    joined = jnp.concatenate([mixed[:half, :rows], mixed[half:, rows:]], axis=0)
    out_ref[...] = joined.T
    log_ref[0] = peak + jnp.log(total)


def diagonal_sums(square):
    lane = lax.broadcasted_iota(jnp.int32, (8, lanes), 1)
    near = square[0:8]
    far = jnp.zeros((8, lanes), f32)
    for group in range(1, lanes // 8):
        turned = pltpu.roll(square[8 * group : 8 * group + 8], lanes - 8 * group, 1)
        inside = lane < lanes - 8 * group
        near = near + jnp.where(inside, turned, 0.0)
        far = far + jnp.where(inside, 0.0, turned)
    both = jnp.concatenate([near, far], axis=1)
    row = lax.broadcasted_iota(jnp.int32, (8, 2 * lanes), 0)
    for bit in (1, 2, 4):
        both = jnp.where((row // bit) % 2 == 1, pltpu.roll(both, 2 * lanes - bit, 1), both)
    return jnp.sum(both, axis=0, keepdims=True)


def backward_kernel(
    stack_ref,
    query_ref,
    segment_bias_ref,
    embed_ref,
    row_code_ref,
    key_code_ref,
    both_ref,
    table_ref,
    number_ref,
    out_back_ref,
    attended_ref,
    log_ref,
    query_back_ref,
    both_back_ref,
    small_ref,
    diagonal_ref,
):
    rows = query_ref.shape[0]
    tiles = both_ref.shape[0] // key_tile
    half = lanes // 2
    lane = lax.broadcasted_iota(jnp.int32, (rows, lanes), 1)
    first = lane < half
    out_back = out_back_ref[...]
    product = (out_back.astype(f32) * attended_ref[...]).T
    delta = jnp.concatenate(
        [
            jnp.sum(product[:half], axis=0, keepdims=True),
            jnp.sum(product[half:], axis=0, keepdims=True),
        ],
        axis=1,
    )
    zeros = jnp.zeros_like(out_back)
    back_stack = jnp.concatenate(
        [jnp.where(first, out_back, zeros), jnp.where(first, zeros, out_back)], axis=0
    )
    stack = stack_ref[0]
    query_stack = stack[:, :lanes]
    log_row = log_ref[0]

    def step(tile, running):
        start = pl.multiple_of(tile * key_tile, key_tile)
        block = tile * (key_tile // lanes)
        keys = jnp.concatenate(
            [both_ref[pl.ds(start, key_tile), :lanes], key_code_ref[pl.ds(start, key_tile), :]], axis=1
        )
        score = dot_nt(keys, stack) + tile_bias(table_ref, block)
        if isinstance(tile, int) and tile == 0:
            score = score + own_mask()
        weight = jnp.exp(score - log_row)
        weight_back = dot_nt(both_ref[pl.ds(start, key_tile), lanes:], back_stack)
        score_back = weight * (weight_back - delta)
        score_low = score_back.astype(bf16)
        both_back_ref[pl.ds(start, key_tile), lanes:] = dot(
            weight.astype(bf16), back_stack
        ).astype(bf16)
        both_back_ref[pl.ds(start, key_tile), :lanes] = dot(score_low, query_stack).astype(bf16)
        for head in range(2):
            for piece in range(key_tile // lanes):
                part = score_back[
                    piece * lanes : (piece + 1) * lanes, head * rows : (head + 1) * rows
                ]
                square = part[:, :lanes] + part[:, lanes:]
                diagonal_ref[head, block + piece] = diagonal_sums(square)[0]
        return running + dot_tn(keys, score_low)

    diagonal_ref[2:] = jnp.zeros(diagonal_ref[2:].shape, f32)
    running = step(0, jnp.zeros((2 * lanes, 2 * rows), f32))
    running = lax.fori_loop(1, tiles, step, running, unroll=min(7, tiles - 1))
    joined = jnp.concatenate([running[:half, :rows], running[half:lanes, rows:]], axis=0).T * 0.125
    shifted = query_ref[...] + segment_bias_ref[...]
    code = row_code_ref[...]
    zero_columns = []
    one_columns = []
    for head in range(2):
        part = running[lanes:, head * rows : (head + 1) * rows].T * 0.125
        same = jnp.sum(jnp.where(lane < 4, part * code, 0.0), axis=1, keepdims=True)
        total = jnp.sum(jnp.where(lane == 8, part, 0.0), axis=1, keepdims=True)
        zero_columns.append(same)
        one_columns.append(total - same)
    zero_back = jnp.where(first, zero_columns[0], zero_columns[1])
    one_back = jnp.where(first, one_columns[0], one_columns[1])
    shift_back = zero_back * embed_ref[0:1, :] + one_back * embed_ref[1:2, :]
    query_back_ref[...] = (joined + shift_back).astype(bf16)
    small_ref[0:1, :] = jnp.sum(joined, axis=0, keepdims=True)
    small_ref[1:2, :] = jnp.sum(shift_back, axis=0, keepdims=True)
    small_ref[2:3, :] = jnp.sum(zero_back * shifted, axis=0, keepdims=True)
    small_ref[3:4, :] = jnp.sum(one_back * shifted, axis=0, keepdims=True)
    blocks = number_ref.shape[0]
    bucket = lax.broadcasted_iota(jnp.int32, (lanes, 2 * lanes), 0)
    table_back = jnp.zeros((8, lanes), f32)
    for block in range(blocks):
        chosen = jnp.where(bucket == number_ref[block : block + 1, :], 1.0, 0.0).astype(bf16)
        sums = diagonal_ref[:, block, :]
        for _ in range(3):
            part = sums.astype(bf16)
            table_back = table_back + dot_nt(part, chosen)
            sums = sums - part.astype(f32)
    small_ref[4:8, :] = table_back[:4]


def attention_specs(rows, keys, blocks, first_pair=0):
    column = lambda pair: (0, pair + first_pair)
    fixed = lambda pair: (0, 0)
    front = lambda pair: (pair + first_pair, 0, 0)
    return {
        "rows": pl.BlockSpec((rows, lanes), column),
        "row": pl.BlockSpec((1, lanes), column),
        "embed": pl.BlockSpec((2, lanes), column),
        "small": pl.BlockSpec((8, lanes), column),
        "row_code": pl.BlockSpec((rows, lanes), fixed),
        "key_code": pl.BlockSpec((keys, lanes), fixed, pipeline_mode=pl.Buffered(1)),
        "both": pl.BlockSpec((keys, 2 * lanes), column),
        "table": pl.BlockSpec((2, blocks, 2 * lanes), front),
        "log": pl.BlockSpec((1, 1, 2 * rows), front),
        "stack": pl.BlockSpec((1, 2 * rows, 2 * lanes), front),
    }


def attention_forward(query_full, bias_content, bias_segment, embed, row_code, key_code, both, table):
    rows, width = query_full.shape
    count = both.shape[0]
    pairs = width // lanes
    spec = attention_specs(rows, count, count // lanes)
    return pl.pallas_call(
        forward_kernel,
        grid=(pairs,),
        in_specs=[
            spec["rows"],
            spec["row"],
            spec["row"],
            spec["embed"],
            spec["row_code"],
            spec["key_code"],
            spec["both"],
            spec["table"],
        ],
        out_specs=[spec["rows"], spec["log"], spec["stack"]],
        out_shape=[
            jax.ShapeDtypeStruct((rows, width), f32),
            jax.ShapeDtypeStruct((pairs, 1, 2 * rows), f32),
            jax.ShapeDtypeStruct((pairs, 2 * rows, 2 * lanes), bf16),
        ],
        scratch_shapes=[pltpu.VMEM((count, 2 * rows), f32)],
        compiler_params=pltpu.CompilerParams(
            dimension_semantics=("arbitrary",), vmem_limit_bytes=60 << 20
        ),
        cost_estimate=pl.CostEstimate(
            flops=40 * rows * count * width,
            bytes_accessed=4 * count * width + 8 * rows * width,
            transcendentals=rows * count * width // 64,
        ),
    )(query_full, bias_content, bias_segment, embed, row_code, key_code, both, table)


def attention_backward(stack, query_full, bias_segment, embed, row_code, key_code, both, table, number, out_back, attended, log_row):
    rows, width = query_full.shape
    count = both.shape[0]
    pairs = width // lanes
    blocks = count // lanes
    spec = attention_specs(rows, count, blocks)
    return pl.pallas_call(
        backward_kernel,
        grid=(pairs,),
        in_specs=[
            spec["stack"],
            spec["rows"],
            spec["row"],
            spec["embed"],
            spec["row_code"],
            spec["key_code"],
            spec["both"],
            spec["table"],
            pl.BlockSpec((blocks, 2 * lanes), lambda pair: (0, 0)),
            spec["rows"],
            spec["rows"],
            spec["log"],
        ],
        out_specs=[spec["rows"], spec["both"], spec["small"]],
        out_shape=[
            jax.ShapeDtypeStruct((rows, width), bf16),
            jax.ShapeDtypeStruct((count, 2 * width), bf16),
            jax.ShapeDtypeStruct((8, width), f32),
        ],
        scratch_shapes=[pltpu.VMEM((8, blocks, 2 * lanes), f32)],
        compiler_params=pltpu.CompilerParams(
            dimension_semantics=("arbitrary",), vmem_limit_bytes=60 << 20
        ),
        cost_estimate=pl.CostEstimate(
            flops=40 * rows * count * width,
            bytes_accessed=8 * count * width + 8 * rows * width,
            transcendentals=rows * count * width // 64,
        ),
    )(stack, query_full, bias_segment, embed, row_code, key_code, both, table, number, out_back, attended, log_row)


def marks_kernel(bound_list, meta_ref, table_ref, key_code_ref, bias_ref, number_ref, row_code_ref):
    blocks = meta_ref.shape[0]
    info = meta_ref[:, 0, :].astype(f32)
    segment = info[:, :lanes]
    rank = info[:, lanes : lanes + 1]
    first = info[:, lanes + 1 : lanes + 2] * lanes + info[:, lanes + 2 : lanes + 3]
    turn = lax.broadcasted_iota(jnp.int32, (blocks, 2 * lanes), 1)
    turn = jnp.where(turn < lanes, turn, turn - 2 * lanes)
    distance = (first[0:1, :] - first).astype(jnp.int32) + turn
    number = jnp.full(distance.shape, bucket_steps, jnp.int32)
    for bound in bound_list:
        number = number + (distance >= bound).astype(jnp.int32) - (distance <= -bound).astype(jnp.int32)
    number_ref[...] = number
    hidden = rank > rank[0:1, :]
    for head in range(bias_ref.shape[0]):
        value = jnp.zeros((blocks, 2 * lanes), f32)
        for bucket in range(2 * bucket_steps + 1):
            value = jnp.where(number == bucket, table_ref[head, bucket], value)
        bias_ref[head] = jnp.where(hidden, negative, value)
    lane = lax.broadcasted_iota(jnp.int32, (lanes, lanes), 1)
    code = (lane % 4).astype(f32)
    for block in range(blocks):
        column = jnp.broadcast_to(segment[block : block + 1, :], (lanes, lanes)).T
        marked = jnp.where(
            lane < 8, jnp.where(column == code, 1.0, 0.0), jnp.where(lane < 10, 1.0, 0.0)
        )
        key_code_ref[block * lanes : (block + 1) * lanes, :] = marked.astype(bf16)
        if block == 0:
            row_code_ref[:lanes, :] = marked
            row_code_ref[lanes:, :] = marked


def key_marks(meta_all, table_full, length):
    blocks = meta_all.shape[0]
    heads = table_full.shape[0]
    bounds = tuple(
        1 + level * level * length // (bucket_steps * bucket_steps) for level in range(bucket_steps)
    )
    whole = pl.BlockSpec(memory_space=pltpu.VMEM)
    scalars = pl.BlockSpec(memory_space=pltpu.SMEM)
    return pl.pallas_call(
        functools.partial(marks_kernel, bounds),
        in_specs=[whole, scalars],
        out_specs=[whole] * 4,
        out_shape=[
            jax.ShapeDtypeStruct((blocks * lanes, lanes), bf16),
            jax.ShapeDtypeStruct((heads, blocks, 2 * lanes), f32),
            jax.ShapeDtypeStruct((blocks, 2 * lanes), jnp.int32),
            jax.ShapeDtypeStruct((2 * lanes, lanes), f32),
        ],
        compiler_params=pltpu.CompilerParams(vmem_limit_bytes=40 << 20),
        cost_estimate=pl.CostEstimate(
            flops=3_000_000_000, bytes_accessed=4 * blocks * lanes * lanes, transcendentals=0
        ),
    )(meta_all, table_full)


def body(
    content,
    query_stream,
    block_rank,
    segments,
    positions,
    query_weight,
    key_weight,
    value_weight,
    output_weight,
    content_bias,
    segment_bias,
    segment_embed,
    relative_table,
    attention_gain,
    attention_shift,
    inner_weight,
    inner_bias,
    outer_weight,
    outer_bias,
    final_gain,
    final_shift,
    content_cotangent,
    query_cotangent,
):
    block_rows = content.shape[1]
    width = content.shape[2]
    rows = 2 * block_rows
    count = lax.axis_size("ctx")
    sides = lax.axis_size("wsh")
    side = lax.axis_index("wsh")
    core = lax.axis_index("ctx") % 2
    length = block_rows * count
    own_content = content[0]
    own_query = query_stream[0]
    part = width // sides
    table_heads, bucket_count = relative_table.shape
    head_count = table_heads * sides
    inner_rows = inner_bias.shape[0] // part
    low = 2

    first_places = shard_places(query_weight.shape[0])
    first_sent = half_rows(first_places, query_weight, key_weight, value_weight)
    first_got = across(first_sent)
    mark_rows = 16
    marks = jnp.concatenate(
        [
            segments[0].astype(bf16),
            block_rank[0].astype(bf16),
            (positions[0, :1] // lanes).astype(bf16),
            (positions[0, :1] % lanes).astype(bf16),
        ]
    )
    marks = jnp.pad(marks[None], ((0, mark_rows - 1), (0, width - marks.shape[0])))
    block = jnp.concatenate([own_content, marks], axis=0)
    gathered = gather_blocks(block)
    small = jnp.concatenate(
        [
            content_bias,
            segment_bias,
            attention_gain,
            attention_shift,
            outer_bias,
            final_gain,
            final_shift,
            segment_embed.reshape(-1),
            inner_bias,
            relative_table.reshape(-1),
        ]
    )
    small_height = 16
    small = jnp.pad(small, (0, small_height * part - small.shape[0])).reshape(small_height, part)
    small_other = across(small)
    first_rest = partner(first_got, 1)
    second_sent = after(half_rows(first_places, output_weight, inner_weight), first_got)
    second_got = across(second_sent)
    third_places = shard_places(outer_weight.shape[0])
    third_sent = after(half_rows(third_places, outer_weight), first_got)
    third_got = across(third_sent)

    small_pair = jnp.where(
        side == 0,
        jnp.concatenate([small, small_other], axis=1),
        jnp.concatenate([small_other, small], axis=1),
    ).astype(f32)
    bias_content = small_pair[0:1]
    bias_segment = small_pair[1:2]
    gain_first = small_pair[2]
    shift_first = small_pair[3]
    bias_outer = small_pair[4]
    gain_second = small_pair[5]
    shift_second = small_pair[6]
    embed = small_pair[7:9]
    bias_inner = jnp.concatenate(
        [
            small_pair[9 : 9 + inner_rows, :part].reshape(-1),
            small_pair[9 : 9 + inner_rows, part:].reshape(-1),
        ]
    )
    table_row = small_pair[9 + inner_rows]
    table_full = jnp.concatenate(
        [
            table_row[: table_heads * bucket_count],
            table_row[part : part + table_heads * bucket_count],
        ]
    ).reshape(head_count, bucket_count)

    held = block_rows + mark_rows
    if len(gathered) == 1:
        stacked = gathered[0].reshape(count, held, width)
        content_all = stacked[:, :block_rows].reshape(length, width)
        meta_all = stacked[:, block_rows:]
    else:
        plan = []
        place = 0
        for at, piece in enumerate(gathered):
            for row in range(0, piece.shape[0], held):
                plan.append(
                    (at, window(row, block_rows), 0, window(place * block_rows, block_rows))
                )
                plan.append(
                    (at, window(row + block_rows, mark_rows), 1, window(place * mark_rows, mark_rows))
                )
                place += 1
        content_all, meta_all = moved(
            tuple(plan),
            [
                jax.ShapeDtypeStruct((length, width), bf16),
                jax.ShapeDtypeStruct((count * mark_rows, width), bf16),
            ],
            first_places,
            *gathered,
        )
        meta_all = meta_all.reshape(count, mark_rows, width)
    pairs = width // lanes
    runs = [(0, 0, width, 0, 0)]
    for pair in range(pairs):
        runs.append((1, pair * lanes, lanes, 1, 2 * pair * lanes))
        runs.append((2, pair * lanes, lanes, 1, (2 * pair + 1) * lanes))
    weight_query, weight_both = whole_rows(
        first_places, runs, (width, 2 * width), first_got, first_rest, query_weight, key_weight, value_weight
    )
    key_code, table, number, row_code = key_marks(meta_all, table_full, length)

    streams = jnp.concatenate([own_content, own_query], axis=0)
    query_full = dot(streams, weight_query)
    both = dot(content_all, weight_both).astype(bf16)
    attended, log_row, stack = attention_forward(
        query_full, bias_content, bias_segment, embed, row_code, key_code, both, table
    )

    hidden = inner_weight.shape[1]
    second_got, third_got, attended = lax.optimization_barrier((second_got, third_got, attended))
    second_rest = partner(second_got, 1)
    weight_output, weight_inner = whole_rows(
        first_places,
        ((0, 0, width, 0, 0), (1, 0, hidden, 1, 0)),
        (width, hidden),
        second_got,
        second_rest,
        output_weight,
        inner_weight,
    )
    third_rest = partner(third_got, 1)
    (weight_outer,) = whole_rows(
        third_places, ((0, 0, width, 0, 0),), (width,), third_got, third_rest, outer_weight
    )

    out_low = attended.astype(bf16)
    out_low_other = partner(out_low, 1)
    attention_out = dot(out_low, weight_output)
    residual = streams.astype(f32) + attention_out
    normed, first_back = jax.vjp(layer_norm, residual, gain_first, shift_first)
    normed_low = normed.astype(bf16)
    normed_other = partner(normed_low, 1)
    inner_pre = dot(normed_low, weight_inner) + bias_inner
    active, gelu_back = jax.vjp(gelu_exact, inner_pre)
    active_low = active.astype(bf16)
    active_other = partner(active_low, 1)
    outer_out = dot(active_low, weight_outer) + bias_outer
    final_norm, second_back = jax.vjp(layer_norm, normed + outer_out, gain_second, shift_second)
    squares = jnp.stack(
        [
            jnp.sum(jnp.square(own_content.astype(f32))),
            jnp.sum(jnp.square(attention_out[:block_rows])),
            jnp.sum(jnp.square(residual[:block_rows])),
        ]
    )
    cotangent = jnp.concatenate([content_cotangent[0], query_cotangent[0]], axis=0).astype(f32)
    back_second, final_gain_back, final_shift_back = second_back(cotangent)
    outer_back = back_second.astype(bf16)

    cuts, extra = split_bits(count)
    wide_cuts = [1] + cuts
    order_one = [0] + cuts
    order_two = cuts[:1] + [0] + cuts[1:]
    places_one = piece_places(order_one, cuts)
    places_two = piece_places(order_two, cuts)
    wide_places = piece_places([1, 0] + cuts, wide_cuts)
    places_out = jnp.concatenate([piece_places(cuts, cuts), core[None].astype(jnp.int32)])
    wide_places_out = piece_places(wide_cuts, wide_cuts)

    def core_halves(value):
        columns = value.shape[1] // 2
        kept = lax.dynamic_slice_in_dim(value, core * columns, columns, 1)
        sent = lax.dynamic_slice_in_dim(value, (1 - core) * columns, columns, 1)
        return kept, partner(sent, 1)

    outer_kept, outer_other = core_halves(outer_back)
    outer_bias_back = jnp.sum(outer_back.astype(f32), axis=0)
    active_back = dot_nt(outer_back, weight_outer)
    inner_back = gelu_back(active_back)[0].astype(bf16)
    outer_keep, outer_send = product_pieces(
        places_one, active_low, after(active_other, active_back), outer_kept, outer_other
    )
    outer_got = pass_on(outer_send, order_one[0])
    inner_kept, inner_other = core_halves(inner_back)
    inner_bias_back = jnp.sum(inner_back.astype(f32), axis=0)
    normed_back = back_second + dot_nt(inner_back, weight_inner)
    residual_back, first_gain_back, first_shift_back = first_back(normed_back)
    attention_back = residual_back.astype(bf16)
    attention_kept, attention_other = core_halves(attention_back)
    out_back = dot_nt(attention_back, weight_output).astype(bf16)
    inner_keep, inner_send = product_pieces(
        places_two,
        normed_low,
        normed_other,
        inner_kept,
        inner_other,
        out_low,
        out_low_other,
        attention_kept,
        attention_other,
    )
    inner_got = pass_on(inner_send, order_two[0])

    line = cuts[1:]
    last = cuts[2]

    def add_extra(value):
        for bit in extra:
            value = fold_last(value, partner(value, bit))
        return value

    query_back, both_back, small_back = attention_backward(
        stack,
        query_full,
        bias_segment,
        embed,
        row_code,
        key_code,
        both,
        table,
        number,
        after(out_back, outer_send, inner_send),
        attended,
        log_row,
    )
    order = Sequence(small_back)
    outer_got, inner_got = order.wait(outer_got, inner_got)
    outer_keep, outer_send = fold(outer_keep, outer_got)
    outer_send = order.ready(outer_send)
    outer_got = partner(outer_send, cuts[0])
    inner_keep, inner_send = fold(inner_keep, inner_got)
    inner_send = order.ready(inner_send)
    inner_got = across(inner_send)

    hidden_rows = hidden // part // sides
    inner_bias_rows = jnp.concatenate(
        [
            inner_bias_back[: hidden // 2].reshape(hidden_rows, part),
            inner_bias_back[hidden // 2 :].reshape(hidden_rows, part),
        ],
        axis=1,
    )
    squares_row = jnp.pad(squares, (0, part - 3))
    vectors = jnp.concatenate(
        [
            small_back[:6],
            first_gain_back[None],
            first_shift_back[None],
            outer_bias_back[None],
            final_gain_back[None],
            final_shift_back[None],
            inner_bias_rows,
            jnp.concatenate([squares_row, squares_row])[None],
        ],
        axis=0,
    )
    tail_keep, tail_send = cut_gradient(
        wide_places,
        vectors,
        dot_tn(streams, query_back),
        dot_tn(content_all, order.ready(both_back)),
    )
    tail_send = order.ready(tail_send)
    tail_got = partner(tail_send, 1)
    outer_got = order.wait(outer_got)
    outer_keep, outer_send = fold(outer_keep, outer_got)
    outer_send = order.ready(outer_send)
    outer_got = partner(outer_send, line[0])
    content_share = dot_nt(order.ready(both_back), weight_both).astype(bf16)
    share_keep, share_send = content_share[: length // 2], order.ready(content_share[length // 2 :])
    share_got = partner(share_send, 1)
    tail_got = order.wait(tail_got)
    tail_keep, tail_send = fold(tail_keep, tail_got)
    tail_send = order.ready(tail_send)
    tail_got = across(tail_send)
    inner_got = order.wait(inner_got)
    inner_keep, inner_send = fold(inner_keep, inner_got)
    inner_send = order.ready(inner_send)
    inner_got = partner(inner_send, line[0])
    share_got = order.wait(share_got)
    share_keep, share_send = fold(share_keep, share_got)
    share_send = order.ready(share_send)
    share_got = partner(share_send, cuts[0])
    outer_got = order.wait(outer_got)
    outer_keep, outer_send = fold(outer_keep, outer_got)
    outer_send = order.ready(outer_send)
    outer_got = partner(outer_send, last)
    inner_got = order.wait(inner_got)
    inner_keep, inner_send = fold(inner_keep, inner_got)
    inner_send = order.ready(inner_send)
    inner_got = partner(inner_send, last)
    outer_got = order.wait(outer_got)
    outer_value = order.ready(add_extra(fold_last(outer_keep, outer_got)))
    outer_got = partner(outer_value, last)
    tail_got = order.wait(tail_got)
    tail_keep, tail_send = fold(tail_keep, tail_got)
    tail_send = order.ready(tail_send)
    tail_got = partner(tail_send, cuts[0])
    inner_got = order.wait(inner_got)
    inner_value = order.ready(add_extra(fold_last(inner_keep, inner_got)))
    inner_got = partner(inner_value, last)
    outer_got = order.wait(outer_got)
    outer_value = order.ready(piled(outer_value, outer_got))
    outer_got = partner(outer_value, line[0])
    share_got = order.wait(share_got)
    share_keep, share_send = fold(share_keep, share_got)
    share_send = order.ready(share_send)
    share_got = partner(share_send, line[0])
    inner_got = order.wait(inner_got)
    inner_value = order.ready(piled(inner_value, inner_got))
    inner_got = partner(inner_value, line[0])
    tail_got = order.wait(tail_got)
    tail_keep, tail_send = fold(tail_keep, tail_got)
    tail_send = order.ready(tail_send)
    tail_got = partner(tail_send, line[0])
    outer_got = order.wait(outer_got)
    outer_value = order.ready(piled(outer_value, outer_got))
    outer_got = partner(outer_value, cuts[0])
    share_got = order.wait(share_got)
    share_keep, share_send = fold(share_keep, share_got)
    share_send = order.ready(share_send)
    share_got = partner(share_send, last)
    streams_back = residual_back + dot_nt(order.ready(query_back), weight_query)
    tail_got = order.wait(tail_got)
    tail_keep, tail_send = fold(tail_keep, tail_got)
    tail_send = order.ready(tail_send)
    tail_got = partner(tail_send, last)
    inner_got = order.wait(inner_got)
    inner_value = order.ready(piled(inner_value, inner_got))
    inner_got = partner(inner_value, cuts[0])
    tail_got = order.wait(tail_got)
    tail_value = order.ready(add_extra(fold_last(tail_keep, tail_got)))
    tail_got = partner(tail_value, last)
    outer_got = order.wait(outer_got)
    outer_value = order.ready(piled(outer_value, outer_got))
    outer_got = partner(outer_value, 1)
    share_got = order.wait(share_got)
    for bit in extra:
        share_keep, share_send = fold(share_keep, share_got)
        share_got = partner(share_send, bit)
    content_back = streams_back[:block_rows] + share_keep.astype(f32) + share_got.astype(f32)
    content_back, outer_got = order.wait(content_back, outer_got)
    (outer_weight_sum,) = lay_out(
        places_out,
        (((0, 0, width // 2, -1), (1, 0, width // 2, -2)),),
        outer_value,
        outer_got,
    )
    outer_weight_sum = order.ready(outer_weight_sum)
    tail_got = order.wait(tail_got)
    tail_value = order.ready(piled(tail_value, tail_got))
    tail_got = partner(tail_value, line[0])
    inner_got = order.wait(inner_got)
    inner_value = order.ready(piled(inner_value, inner_got))
    inner_got = partner(inner_value, 1)
    tail_got = order.wait(tail_got)
    tail_value = order.ready(piled(tail_value, tail_got))
    tail_got = partner(tail_value, cuts[0])
    inner_got = order.wait(inner_got)
    inner_weight_sum, output_weight_sum = lay_out(
        places_out,
        (
            ((0, 0, hidden // 2, -1), (1, 0, hidden // 2, -2)),
            ((0, hidden // 2, width // 2, -1), (1, hidden // 2, width // 2, -2)),
        ),
        inner_value,
        inner_got,
    )
    inner_weight_sum, output_weight_sum = order.ready(inner_weight_sum, output_weight_sum)
    tail_got = order.wait(tail_got)
    tail_value = order.ready(piled(tail_value, tail_got))
    tail_got = partner(tail_value, 1)
    plan = []
    for kind in range(3):
        row = []
        for pair in range(pairs):
            taken = pair * lanes if kind == 0 else width + (2 * pair + kind - 1) * lanes
            row.append((0, taken, lanes, pair * lanes))
        plan.append(tuple(row))
    plan.append(((0, 3 * width, lanes, 0),))
    query_weight_sum, key_weight_sum, value_weight_sum, vector_sums = lay_out(
        wide_places_out, tuple(plan), tail_value, tail_got
    )
    sums = vector_sums[:, :16].T
    table_sum = jnp.swapaxes(sums[4:6].reshape(2, -1, lanes)[:, :, :bucket_count], 0, 1).reshape(
        table_heads, bucket_count
    )
    inner_bias_sum = sums[11 : 11 + hidden_rows].reshape(-1)
    token_total = length * sides * width
    root_mean = jnp.sqrt(sums[11 + hidden_rows, :3] / token_total)
    return (
        final_norm[:block_rows].astype(bf16)[None],
        final_norm[block_rows:].astype(bf16)[None],
        content_back[None],
        streams_back[block_rows:][None],
        query_weight_sum,
        key_weight_sum,
        value_weight_sum,
        output_weight_sum,
        sums[0],
        sums[1],
        sums[2:4],
        table_sum,
        sums[6],
        sums[7],
        inner_weight_sum,
        inner_bias_sum,
        outer_weight_sum,
        sums[8],
        sums[9],
        sums[10],
        root_mean,
    )


def solution(mesh):
    tokens = P("wsh", "ctx", None)
    marks = P("wsh", "ctx")
    matrix = P("wsh", None)
    vector = P("wsh")
    placed = (
        (tokens, tokens, marks, marks, marks)
        + (matrix,) * 4
        + (vector, vector, P(None, "wsh"), matrix, vector, vector, matrix, vector, matrix)
        + (vector,) * 3
        + (tokens, tokens)
    )
    given = (
        (tokens,) * 4
        + (matrix,) * 4
        + (vector, vector, P(None, "wsh"), matrix, vector, vector, matrix, vector, matrix)
        + (vector,) * 3
        + (P(),)
    )
    return jax.shard_map(body, mesh=mesh, in_specs=placed, out_specs=given, check_vma=False)
```

```python
import functools

import jax
import jax.numpy as jnp
from jax import lax
from jax.experimental import pallas as pl
from jax.experimental.pallas import tpu as pltpu
from jax.sharding import PartitionSpec as P

negative = -1e30
epsilon = 1e-05
bucket_steps = 16
key_tile = 256
lanes = 128
highest = lax.Precision.HIGHEST
f32 = jnp.float32
bf16 = jnp.bfloat16


free = pl.CostEstimate(flops=0, bytes_accessed=0, transcendentals=0)
in_vmem = pl.BlockSpec(memory_space=pltpu.VMEM)
in_smem = pl.BlockSpec(memory_space=pltpu.SMEM)


def takes(microseconds):
    return pl.CostEstimate(
        flops=microseconds * 1_000_000_000, bytes_accessed=0, transcendentals=0
    )


def normalized(values):
    centred = values - jnp.mean(values, axis=-1, keepdims=True)
    spread = jnp.mean(centred * centred, axis=-1, keepdims=True)
    scale = lax.rsqrt(spread + epsilon)
    return centred * scale, scale


def norm_back(cotangent, rows, scale):
    mean = jnp.mean(cotangent, axis=-1, keepdims=True)
    along = jnp.mean(cotangent * rows, axis=-1, keepdims=True)
    return scale * (cotangent - mean - rows * along)


def dot(left, right):
    return jnp.dot(left, right, preferred_element_type=f32)


def dot_nt(left, right):
    return lax.dot_general(left, right, (((1,), (1,)), ((), ())), preferred_element_type=f32)


def dot_tn(left, right):
    return lax.dot_general(left, right, (((0,), (0,)), ((), ())), preferred_element_type=f32)


def partner(value, bit):
    count = lax.axis_size("ctx")
    return lax.ppermute(value, "ctx", [(place, place ^ bit) for place in range(count)])


def across(value):
    return lax.ppermute(value, "wsh", [(0, 1), (1, 0)])


def bits_of(count):
    result = []
    bit = 1
    while bit < count:
        result.append(bit)
        bit *= 2
    return result


def block_order(count):
    order = [0]
    for bit in reversed(bits_of(count)):
        order = order + [place | bit for place in order]
    return order


def gather_blocks(own):
    count = lax.axis_size("ctx")
    bits = bits_of(count)
    if count != 16:
        held = own
        for bit in reversed(bits):
            held = jnp.concatenate([held, partner(held, bit)], axis=0)
        return [held]
    low = bits[1]
    near = partner(own, low)
    first = [own] + [partner(own, place) for place in (bits[3], bits[2], bits[2] | bits[3])]
    second = [near] + [partner(block, low) for block in first[1:]]
    first_core = partner(jnp.concatenate(first, axis=0), 1)
    second_core = partner(jnp.concatenate(second, axis=0), 1)
    return first + second + [first_core, second_core]


def move_kernel(plan, inputs, place_ref, *refs):
    sources, targets = refs[:inputs], refs[inputs:]
    for source, taken, target, put in plan:
        targets[target][put(place_ref)] = sources[source][taken(place_ref)]


def moved(plan, shapes, places, *sources):
    whole = pl.BlockSpec(memory_space=pltpu.VMEM)
    size = sum(shape.size for shape in shapes)
    return pl.pallas_call(
        functools.partial(move_kernel, plan, len(sources)),
        in_specs=[pl.BlockSpec(memory_space=pltpu.SMEM)] + [whole] * len(sources),
        out_specs=[whole] * len(shapes),
        out_shape=shapes,
        compiler_params=pltpu.CompilerParams(vmem_limit_bytes=48 << 20),
        cost_estimate=takes(3),
    )(places, *sources)


def window(start, rows, left=None, columns=None):
    def make(place_ref):
        first = start
        if isinstance(start, str):
            first = pl.multiple_of(place_ref[int(start)], 16)
        if left is None:
            return (pl.ds(first, rows), slice(None))
        return (pl.ds(first, rows), pl.ds(left, columns))

    return make


def half_rows(places, *shards):
    rows = shards[0].shape[0] // 2
    plan = []
    left = 0
    for at, shard in enumerate(shards):
        columns = shard.shape[1]
        plan.append((at, window("0", rows, 0, columns), 0, window(0, rows, left, columns)))
        left += columns
    return moved(tuple(plan), [jax.ShapeDtypeStruct((rows, left), bf16)], places, *shards)[0]


def whole_rows(places, runs, widths, got, rest, *shards):
    rows = shards[0].shape[0]
    half = rows // 2
    lefts = [0]
    for shard in shards:
        lefts.append(lefts[-1] + shard.shape[1])
    plan = []
    for shard, first, columns, target, column in runs:
        plan.append(
            (2 + shard, window(0, rows, first, columns), target, window("1", rows, column, columns))
        )
        for source, place in ((0, "2"), (1, "3")):
            plan.append(
                (
                    source,
                    window(0, half, lefts[shard] + first, columns),
                    target,
                    window(place, half, column, columns),
                )
            )
    shapes = [jax.ShapeDtypeStruct((2 * rows, width), bf16) for width in widths]
    return moved(tuple(plan), shapes, places, got, rest, *shards)


def shard_places(rows):
    core = lax.axis_index("ctx") % 2
    side = lax.axis_index("wsh")
    half = rows // 2
    base = (1 - side) * rows
    return jnp.stack(
        [core * half, side * rows, base + core * half, base + (1 - core) * half]
    ).astype(jnp.int32)


def split_bits(count):
    bits = bits_of(count)
    return bits[1:4], bits[4:]


def own_bit(bit):
    if bit == 0:
        return lax.axis_index("wsh")
    return (lax.axis_index("ctx") // bit) % 2


def pass_on(value, bit):
    return across(value) if bit == 0 else partner(value, bit)


class Sequence:
    def __init__(self, mark):
        self.mark = mark

    def wait(self, *values):
        *values, self.mark = lax.optimization_barrier(tuple(values) + (self.mark,))
        return values[0] if len(values) == 1 else tuple(values)

    ready = wait


def piece_places(order, cuts):
    total = len(order)
    place = jnp.arange(1 << total, dtype=jnp.int32)
    result = jnp.zeros_like(place)
    for at, bit in enumerate(order):
        value = ((place >> (total - 1 - at)) & 1) ^ own_bit(bit)
        weight = 1 << len(cuts) if bit == 0 else 1 << (len(cuts) - 1 - cuts.index(bit))
        result = result + value * weight
    return result


def fold_kernel(keep_ref, received_ref, *target_refs):
    first = 0
    for target_ref in target_refs:

        @pl.loop(0, target_ref.shape[0])
        def _(place, first=first, target_ref=target_ref):
            target_ref[place] = (
                keep_ref[first + place].astype(f32) + received_ref[first + place].astype(f32)
            ).astype(bf16)

        first += target_ref.shape[0]


def fold_parts(keep, received, parts):
    piece = jax.ShapeDtypeStruct((keep.shape[0] // parts,) + keep.shape[1:], bf16)
    return pl.pallas_call(
        fold_kernel,
        in_specs=[in_vmem] * 2,
        out_specs=[in_vmem] * parts,
        out_shape=[piece] * parts,
        compiler_params=pltpu.CompilerParams(vmem_limit_bytes=40 << 20),
        cost_estimate=free,
    )(keep, received)


def fold(keep, received):
    return fold_parts(keep, received, 2)


def fold_last(keep, received):
    return fold_parts(keep, received, 1)[0]


def pile_kernel(*refs):
    target_ref = refs[-1]
    first = 0
    for source_ref in refs[:-1]:

        @pl.loop(0, source_ref.shape[0])
        def _(place, first=first, source_ref=source_ref):
            target_ref[first + place] = source_ref[place]

        first += source_ref.shape[0]


def piled(*values):
    height = sum(value.shape[0] for value in values)
    return pl.pallas_call(
        pile_kernel,
        in_specs=[in_vmem] * len(values),
        out_specs=in_vmem,
        out_shape=jax.ShapeDtypeStruct((height,) + values[0].shape[1:], values[0].dtype),
        compiler_params=pltpu.CompilerParams(vmem_limit_bytes=40 << 20),
        cost_estimate=free,
    )(*values)


def share_kernel(back_ref, weight_ref, out_ref):
    out_ref[...] = dot_nt(back_ref[...], weight_ref[...]).astype(bf16).reshape(out_ref.shape)


def share_of_content(both_back, weight_both):
    count, columns = both_back.shape
    width = weight_both.shape[0]
    step = 2 * lanes
    return pl.pallas_call(
        share_kernel,
        grid=(count // step,),
        in_specs=[
            pl.BlockSpec((step, columns), lambda at: (at, 0)),
            pl.BlockSpec((width, columns), lambda at: (0, 0), pipeline_mode=pl.Buffered(1)),
        ],
        out_specs=pl.BlockSpec((2, lanes, width), lambda at: (at, 0, 0)),
        out_shape=jax.ShapeDtypeStruct((count // lanes, lanes, width), bf16),
        compiler_params=pltpu.CompilerParams(vmem_limit_bytes=40 << 20),
        cost_estimate=takes(7),
    )(both_back, weight_both)


def after(value, *others):
    return lax.optimization_barrier((value,) + others)[0]


def product_kernel(groups, place_ref, *refs):
    operands, (keep_ref, send_ref, total_ref) = refs[: 4 * groups], refs[4 * groups :]
    rows = keep_ref.shape[1]
    step = 256
    left = 0
    for group in range(groups):
        left_own, left_other, right_own, right_other = operands[4 * group : 4 * group + 4]
        columns = right_own.shape[1]
        for start in range(0, left_own.shape[1], step):
            total_ref[start : start + step, left : left + columns] = dot_tn(
                left_own[:, start : start + step], right_own[...]
            ) + dot_tn(left_other[:, start : start + step], right_other[...])
        left += columns
    for at, ref in enumerate((keep_ref, send_ref)):

        @pl.loop(0, ref.shape[0])
        def _(place, at=at, ref=ref):
            block = place_ref[at * ref.shape[0] + place]
            start = pl.multiple_of(block * rows, 8)
            ref[place] = total_ref[pl.ds(start, rows), :].astype(bf16)


def product_pieces(places, *operands):
    groups = len(operands) // 4
    half = places.shape[0] // 2
    height = operands[0].shape[1]
    columns = sum(operands[4 * group + 2].shape[1] for group in range(groups))
    piece = jax.ShapeDtypeStruct((half, height // (2 * half), columns), bf16)
    whole = pl.BlockSpec(memory_space=pltpu.VMEM)
    return pl.pallas_call(
        functools.partial(product_kernel, groups),
        in_specs=[pl.BlockSpec(memory_space=pltpu.SMEM)] + [whole] * len(operands),
        out_specs=[whole, whole],
        out_shape=[piece, piece],
        scratch_shapes=[pltpu.VMEM((height, columns), f32)],
        compiler_params=pltpu.CompilerParams(vmem_limit_bytes=40 << 20),
        cost_estimate=takes(4),
    )(places, *operands)


def cut_kernel(place_ref, vector_ref, small_ref, *refs):
    parts, (keep_ref, send_ref, turned_ref) = refs[:-3], refs[-3:]
    rows = keep_ref.shape[1]
    height = vector_ref.shape[1]
    filled = jnp.concatenate(
        [
            small_ref[...] + vector_ref[0:8, :],
            vector_ref[8:, :],
            jnp.zeros((lanes - vector_ref.shape[0], height), f32),
        ],
        axis=0,
    )
    for start in range(0, height, lanes):
        turned_ref[start : start + lanes, :] = filled[:, start : start + lanes].T
    parts = parts + (turned_ref,)
    for at, ref in enumerate((keep_ref, send_ref)):

        @pl.loop(0, ref.shape[0])
        def _(place, at=at, ref=ref):
            block = place_ref[at * ref.shape[0] + place]
            start = pl.multiple_of(block * rows, 8)
            left = 0
            for part in parts:
                columns = part.shape[1]
                ref[place, :, left : left + columns] = part[pl.ds(start, rows), :].astype(bf16)
                left += columns


def cut_gradient(places, vectors, small, *parts):
    half = places.shape[0] // 2
    height = parts[0].shape[0]
    columns = sum(part.shape[1] for part in parts) + lanes
    piece = jax.ShapeDtypeStruct((half, height // (2 * half), columns), bf16)
    whole = pl.BlockSpec(memory_space=pltpu.VMEM)
    return pl.pallas_call(
        cut_kernel,
        in_specs=[pl.BlockSpec(memory_space=pltpu.SMEM)] + [whole] * (len(parts) + 2),
        out_specs=[whole, whole],
        out_shape=[piece, piece],
        scratch_shapes=[pltpu.VMEM((height, lanes), f32)],
        compiler_params=pltpu.CompilerParams(vmem_limit_bytes=40 << 20),
        cost_estimate=takes(3),
    )(places, vectors, small, *parts)


def lay_out_kernel(plan, place_ref, *refs):
    outputs = len(plan)
    sources, targets = refs[:-outputs], refs[-outputs:]
    halves = 2 if place_ref.shape[0] > sources[0].shape[0] + 1 else 1
    for half in range(halves):
      for runs, target in zip(plan, targets, strict=True):
        for source, first, columns, column in runs:
            piece_ref = sources[source + half]
            count, rows = piece_ref.shape[:2]

            @pl.loop(0, count)
            def _(place, piece_ref=piece_ref, rows=rows, target=target, first=first, columns=columns, column=column, half=half):
                start = pl.multiple_of(place_ref[half * count + place] * rows, 8)
                value = piece_ref[place, :, first : first + columns].astype(f32)
                if column >= 0:
                    target[pl.ds(start, rows), column : column + columns] = value
                else:
                    core = place_ref[count]
                    which = core if column == -1 else 1 - core
                    left = pl.multiple_of(which * columns, lanes)
                    target[pl.ds(start, rows), pl.ds(left, columns)] = value


def lay_out(places, plan, *pieces):
    whole = pl.BlockSpec(memory_space=pltpu.VMEM)
    shapes = []
    halves = 2 if places.shape[0] > pieces[0].shape[0] + 1 else 1
    for runs in plan:
        count, rows = pieces[runs[0][0]].shape[:2]
        shapes.append(jax.ShapeDtypeStruct((halves * count * rows, sum(run[2] for run in runs)), f32))
    return pl.pallas_call(
        functools.partial(lay_out_kernel, plan),
        in_specs=[pl.BlockSpec(memory_space=pltpu.SMEM)] + [whole] * len(pieces),
        out_specs=[whole] * len(plan),
        out_shape=shapes,
        compiler_params=pltpu.CompilerParams(vmem_limit_bytes=48 << 20),
        cost_estimate=takes(3),
    )(places, *pieces)


def stream_bias(table_ref, head, block):
    spread = jnp.broadcast_to(table_ref[head, pl.ds(block, 1), :], (lanes, 2 * lanes))
    return pltpu.roll(spread, 0, 1, stride=1, stride_axis=0)[:, :lanes]


def tile_bias(table_ref, block):
    parts = []
    for piece in range(key_tile // lanes):
        first = stream_bias(table_ref, 0, block + piece)
        second = stream_bias(table_ref, 1, block + piece)
        parts.append(jnp.concatenate([first, first, second, second], axis=1))
    return jnp.concatenate(parts, axis=0)


def own_mask():
    row = lax.broadcasted_iota(jnp.int32, (key_tile, 4 * lanes), 0)
    column = lax.broadcasted_iota(jnp.int32, (key_tile, 4 * lanes), 1)
    stream = (column // lanes) % 2
    return jnp.where((stream == 1) & (row == column % lanes), negative, 0.0)


def forward_kernel(
    query_ref,
    content_bias_ref,
    segment_bias_ref,
    embed_ref,
    row_code_ref,
    key_code_ref,
    both_ref,
    table_ref,
    out_ref,
    log_ref,
    stack_ref,
    score_ref,
):
    rows = query_ref.shape[0]
    tiles = both_ref.shape[0] // key_tile
    lane = lax.broadcasted_iota(jnp.int32, (rows, lanes), 1)
    first = lane < lanes // 2
    query = query_ref[...]
    low = (query + content_bias_ref[...]).astype(bf16).astype(f32) * 0.125
    shifted = query + segment_bias_ref[...]
    zero_term = shifted * embed_ref[0:1, :]
    one_term = shifted * embed_ref[1:2, :]
    code = row_code_ref[...]
    for head in range(2):
        own = first if head == 0 else jnp.logical_not(first)
        zero_sum = jnp.sum(jnp.where(own, zero_term, 0.0), axis=1, keepdims=True) * 0.125
        one_sum = jnp.sum(jnp.where(own, one_term, 0.0), axis=1, keepdims=True) * 0.125
        step = zero_sum - one_sum
        step_high = step.astype(bf16).astype(f32)
        step_low = step - step_high
        one_high = one_sum.astype(bf16).astype(f32)
        one_low = one_sum - one_high
        extra = jnp.where(
            lane < 4,
            step_high,
            jnp.where(lane < 8, step_low, jnp.where(lane == 8, one_high, one_low)),
        )
        stack_ref[0, pl.ds(head * rows, rows), 0:lanes] = jnp.where(own, low, 0.0).astype(bf16)
        stack_ref[0, pl.ds(head * rows, rows), lanes : 2 * lanes] = (extra * code).astype(bf16)
    stack = stack_ref[0]

    def scores(tile, top):
        start = pl.multiple_of(tile * key_tile, key_tile)
        keys = jnp.concatenate(
            [both_ref[pl.ds(start, key_tile), :lanes], key_code_ref[pl.ds(start, key_tile), :]], axis=1
        )
        score = dot_nt(keys, stack) + tile_bias(table_ref, tile * (key_tile // lanes))
        if isinstance(tile, int) and tile == 0:
            score = score + own_mask()
        score_ref[pl.ds(start, key_tile), :] = score
        return jnp.maximum(top, jnp.max(score.reshape(key_tile // 8, 8, 4 * lanes), axis=0))

    top = jnp.full((8, 4 * lanes), negative, f32)
    top = scores(0, top)
    top = lax.fori_loop(1, tiles, scores, top, unroll=min(7, tiles - 1))
    peak = jnp.max(top, axis=0, keepdims=True)

    def gathered(tile, running):
        total, mixed = running
        start = pl.multiple_of(tile * key_tile, key_tile)
        weight = jnp.exp(score_ref[pl.ds(start, key_tile), :] - peak)
        total = total + jnp.sum(weight.reshape(key_tile // 8, 8, 4 * lanes), axis=0)
        mixed = mixed + dot_tn(both_ref[pl.ds(start, key_tile), lanes:], weight.astype(bf16))
        return total, mixed

    total, mixed = lax.fori_loop(
        0,
        tiles,
        gathered,
        (jnp.zeros((8, 4 * lanes), f32), jnp.zeros((lanes, 4 * lanes), f32)),
        unroll=min(8, tiles),
    )
    total = jnp.sum(total, axis=0, keepdims=True)
    mixed = mixed / total
    half = lanes // 2
    joined = jnp.concatenate([mixed[:half, :rows], mixed[half:, rows:]], axis=0)
    out_ref[...] = joined.T
    log_ref[0] = peak + jnp.log(total)


def diagonal_sums(square):
    lane = lax.broadcasted_iota(jnp.int32, (8, lanes), 1)
    near = square[0:8]
    far = jnp.zeros((8, lanes), f32)
    for group in range(1, lanes // 8):
        turned = pltpu.roll(square[8 * group : 8 * group + 8], lanes - 8 * group, 1)
        inside = lane < lanes - 8 * group
        near = near + jnp.where(inside, turned, 0.0)
        far = far + jnp.where(inside, 0.0, turned)
    both = jnp.concatenate([near, far], axis=1)
    row = lax.broadcasted_iota(jnp.int32, (8, 2 * lanes), 0)
    for bit in (1, 2, 4):
        both = jnp.where((row // bit) % 2 == 1, pltpu.roll(both, 2 * lanes - bit, 1), both)
    return jnp.sum(both, axis=0, keepdims=True)


def backward_kernel(
    stack_ref,
    query_ref,
    segment_bias_ref,
    embed_ref,
    row_code_ref,
    key_code_ref,
    both_ref,
    table_ref,
    number_ref,
    out_back_ref,
    attended_ref,
    log_ref,
    query_back_ref,
    both_back_ref,
    small_ref,
    diagonal_ref,
):
    rows = query_ref.shape[0]
    tiles = both_ref.shape[0] // key_tile
    half = lanes // 2
    lane = lax.broadcasted_iota(jnp.int32, (rows, lanes), 1)
    first = lane < half
    out_back = out_back_ref[...]
    product = (out_back.astype(f32) * attended_ref[...]).T
    delta = jnp.concatenate(
        [
            jnp.sum(product[:half], axis=0, keepdims=True),
            jnp.sum(product[half:], axis=0, keepdims=True),
        ],
        axis=1,
    )
    zeros = jnp.zeros_like(out_back)
    back_stack = jnp.concatenate(
        [jnp.where(first, out_back, zeros), jnp.where(first, zeros, out_back)], axis=0
    )
    stack = stack_ref[0]
    query_stack = stack[:, :lanes]
    log_row = log_ref[0]

    def step(tile, running):
        start = pl.multiple_of(tile * key_tile, key_tile)
        block = tile * (key_tile // lanes)
        keys = jnp.concatenate(
            [both_ref[pl.ds(start, key_tile), :lanes], key_code_ref[pl.ds(start, key_tile), :]], axis=1
        )
        score = dot_nt(keys, stack) + tile_bias(table_ref, block)
        if isinstance(tile, int) and tile == 0:
            score = score + own_mask()
        weight = jnp.exp(score - log_row)
        weight_back = dot_nt(both_ref[pl.ds(start, key_tile), lanes:], back_stack)
        score_back = weight * (weight_back - delta)
        score_low = score_back.astype(bf16)
        both_back_ref[pl.ds(start, key_tile), lanes:] = dot(
            weight.astype(bf16), back_stack
        ).astype(bf16)
        both_back_ref[pl.ds(start, key_tile), :lanes] = dot(score_low, query_stack).astype(bf16)
        for head in range(2):
            for piece in range(key_tile // lanes):
                part = score_back[
                    piece * lanes : (piece + 1) * lanes, head * rows : (head + 1) * rows
                ]
                square = part[:, :lanes] + part[:, lanes:]
                diagonal_ref[head, block + piece] = diagonal_sums(square)[0]
        return running + dot_tn(keys, score_low)

    diagonal_ref[2:] = jnp.zeros(diagonal_ref[2:].shape, f32)
    running = step(0, jnp.zeros((2 * lanes, 2 * rows), f32))
    running = lax.fori_loop(1, tiles, step, running, unroll=min(7, tiles - 1))
    joined = jnp.concatenate([running[:half, :rows], running[half:lanes, rows:]], axis=0).T * 0.125
    shifted = query_ref[...] + segment_bias_ref[...]
    code = row_code_ref[...]
    zero_columns = []
    one_columns = []
    for head in range(2):
        part = running[lanes:, head * rows : (head + 1) * rows].T * 0.125
        same = jnp.sum(jnp.where(lane < 4, part * code, 0.0), axis=1, keepdims=True)
        total = jnp.sum(jnp.where(lane == 8, part, 0.0), axis=1, keepdims=True)
        zero_columns.append(same)
        one_columns.append(total - same)
    zero_back = jnp.where(first, zero_columns[0], zero_columns[1])
    one_back = jnp.where(first, one_columns[0], one_columns[1])
    shift_back = zero_back * embed_ref[0:1, :] + one_back * embed_ref[1:2, :]
    query_back_ref[...] = (joined + shift_back).astype(bf16)
    small_ref[0:1, :] = jnp.sum(joined, axis=0, keepdims=True)
    small_ref[1:2, :] = jnp.sum(shift_back, axis=0, keepdims=True)
    small_ref[2:3, :] = jnp.sum(zero_back * shifted, axis=0, keepdims=True)
    small_ref[3:4, :] = jnp.sum(one_back * shifted, axis=0, keepdims=True)
    blocks = number_ref.shape[0]
    bucket = lax.broadcasted_iota(jnp.int32, (lanes, 2 * lanes), 0)
    table_back = jnp.zeros((8, lanes), f32)
    for block in range(blocks):
        chosen = jnp.where(bucket == number_ref[block : block + 1, :], 1.0, 0.0).astype(bf16)
        sums = diagonal_ref[:, block, :]
        for _ in range(3):
            part = sums.astype(bf16)
            table_back = table_back + dot_nt(part, chosen)
            sums = sums - part.astype(f32)
    small_ref[4:8, :] = table_back[:4]


def attention_specs(rows, keys, blocks, first_pair=0):
    column = lambda pair: (0, pair + first_pair)
    fixed = lambda pair: (0, 0)
    front = lambda pair: (pair + first_pair, 0, 0)
    return {
        "rows": pl.BlockSpec((rows, lanes), column),
        "row": pl.BlockSpec((1, lanes), column),
        "embed": pl.BlockSpec((2, lanes), column),
        "small": pl.BlockSpec((8, lanes), column),
        "row_code": pl.BlockSpec((rows, lanes), fixed),
        "key_code": pl.BlockSpec((keys, lanes), fixed, pipeline_mode=pl.Buffered(1)),
        "both": pl.BlockSpec((keys, 2 * lanes), column),
        "table": pl.BlockSpec((2, blocks, 2 * lanes), front),
        "log": pl.BlockSpec((1, 1, 2 * rows), front),
        "stack": pl.BlockSpec((1, 2 * rows, 2 * lanes), front),
    }


def attention_forward(query_full, bias_content, bias_segment, embed, row_code, key_code, both, table):
    rows, width = query_full.shape
    count = both.shape[0]
    pairs = width // lanes
    spec = attention_specs(rows, count, count // lanes)
    return pl.pallas_call(
        forward_kernel,
        grid=(pairs,),
        in_specs=[
            spec["rows"],
            spec["row"],
            spec["row"],
            spec["embed"],
            spec["row_code"],
            spec["key_code"],
            spec["both"],
            spec["table"],
        ],
        out_specs=[spec["rows"], spec["log"], spec["stack"]],
        out_shape=[
            jax.ShapeDtypeStruct((rows, width), f32),
            jax.ShapeDtypeStruct((pairs, 1, 2 * rows), f32),
            jax.ShapeDtypeStruct((pairs, 2 * rows, 2 * lanes), bf16),
        ],
        scratch_shapes=[pltpu.VMEM((count, 2 * rows), f32)],
        compiler_params=pltpu.CompilerParams(
            dimension_semantics=("arbitrary",), vmem_limit_bytes=60 << 20
        ),
        cost_estimate=takes(18),
    )(query_full, bias_content, bias_segment, embed, row_code, key_code, both, table)


def attention_backward(stack, query_full, bias_segment, embed, row_code, key_code, both, table, number, out_back, attended, log_row):
    rows, width = query_full.shape
    count = both.shape[0]
    pairs = width // lanes
    blocks = count // lanes
    spec = attention_specs(rows, count, blocks)
    return pl.pallas_call(
        backward_kernel,
        grid=(pairs,),
        in_specs=[
            spec["stack"],
            spec["rows"],
            spec["row"],
            spec["embed"],
            spec["row_code"],
            spec["key_code"],
            spec["both"],
            spec["table"],
            pl.BlockSpec((blocks, 2 * lanes), lambda pair: (0, 0)),
            spec["rows"],
            spec["rows"],
            spec["log"],
        ],
        out_specs=[spec["rows"], spec["both"], spec["small"]],
        out_shape=[
            jax.ShapeDtypeStruct((rows, width), bf16),
            jax.ShapeDtypeStruct((count, 2 * width), bf16),
            jax.ShapeDtypeStruct((8, width), f32),
        ],
        scratch_shapes=[pltpu.VMEM((8, blocks, 2 * lanes), f32)],
        compiler_params=pltpu.CompilerParams(
            dimension_semantics=("arbitrary",), vmem_limit_bytes=60 << 20
        ),
        cost_estimate=takes(34),
    )(stack, query_full, bias_segment, embed, row_code, key_code, both, table, number, out_back, attended, log_row)


def marks_kernel(bound_list, meta_ref, table_ref, key_code_ref, bias_ref, number_ref, row_code_ref):
    blocks = meta_ref.shape[0]
    info = meta_ref[:, 0, :].astype(f32)
    segment = info[:, :lanes]
    rank = info[:, lanes : lanes + 1]
    first = info[:, lanes + 1 : lanes + 2] * lanes + info[:, lanes + 2 : lanes + 3]
    turn = lax.broadcasted_iota(jnp.int32, (blocks, 2 * lanes), 1)
    turn = jnp.where(turn < lanes, turn, turn - 2 * lanes)
    distance = (first[0:1, :] - first).astype(jnp.int32) + turn
    number = jnp.full(distance.shape, bucket_steps, jnp.int32)
    for bound in bound_list:
        number = number + (distance >= bound).astype(jnp.int32) - (distance <= -bound).astype(jnp.int32)
    number_ref[...] = number
    hidden = rank > rank[0:1, :]
    for head in range(bias_ref.shape[0]):
        value = jnp.zeros((blocks, 2 * lanes), f32)
        for bucket in range(2 * bucket_steps + 1):
            value = jnp.where(number == bucket, table_ref[head, bucket], value)
        bias_ref[head] = jnp.where(hidden, negative, value)
    lane = lax.broadcasted_iota(jnp.int32, (lanes, lanes), 1)
    code = (lane % 4).astype(f32)
    for block in range(blocks):
        column = jnp.broadcast_to(segment[block : block + 1, :], (lanes, lanes)).T
        marked = jnp.where(
            lane < 8, jnp.where(column == code, 1.0, 0.0), jnp.where(lane < 10, 1.0, 0.0)
        )
        key_code_ref[block * lanes : (block + 1) * lanes, :] = marked.astype(bf16)
        if block == 0:
            row_code_ref[:lanes, :] = marked
            row_code_ref[lanes:, :] = marked


def key_marks(meta_all, table_full, length):
    blocks = meta_all.shape[0]
    heads = table_full.shape[0]
    bounds = tuple(
        1 + level * level * length // (bucket_steps * bucket_steps) for level in range(bucket_steps)
    )
    whole = pl.BlockSpec(memory_space=pltpu.VMEM)
    scalars = pl.BlockSpec(memory_space=pltpu.SMEM)
    return pl.pallas_call(
        functools.partial(marks_kernel, bounds),
        in_specs=[whole, scalars],
        out_specs=[whole] * 4,
        out_shape=[
            jax.ShapeDtypeStruct((blocks * lanes, lanes), bf16),
            jax.ShapeDtypeStruct((heads, blocks, 2 * lanes), f32),
            jax.ShapeDtypeStruct((blocks, 2 * lanes), jnp.int32),
            jax.ShapeDtypeStruct((2 * lanes, lanes), f32),
        ],
        compiler_params=pltpu.CompilerParams(vmem_limit_bytes=40 << 20),
        cost_estimate=takes(2),
    )(meta_all, table_full)


def assemble(target_ref, own_ref, got_ref, rest_ref, columns, places):
    rows = own_ref.shape[0]
    half = rows // 2
    own, got, rest = [pl.multiple_of(place, 16) for place in places]
    target_ref[pl.ds(own, rows), :] = own_ref[...]
    target_ref[pl.ds(got, half), :] = got_ref[:, columns]
    target_ref[pl.ds(rest, half), :] = rest_ref[:, columns]


def forward_half_kernel(
    place_ref,
    attended_ref,
    content_ref,
    stream_ref,
    output_own_ref,
    inner_own_ref,
    got_ref,
    rest_ref,
    vector_ref,
    bias_ref,
    out_low_ref,
    normed_ref,
    rows_ref,
    scale_ref,
    normed_low_ref,
    active_ref,
    slope_ref,
    square_ref,
    weight_output_ref,
    weight_inner_ref,
):
    width = attended_ref.shape[1]
    hidden = inner_own_ref.shape[1]
    half = content_ref.shape[0]
    places = (place_ref[1], place_ref[2], place_ref[3])
    assemble(weight_output_ref, output_own_ref, got_ref, rest_ref, slice(0, width), places)
    assemble(weight_inner_ref, inner_own_ref, got_ref, rest_ref, slice(width, width + hidden), places)
    out_low = attended_ref[...].astype(bf16)
    out_low_ref[...] = out_low
    attention_out = dot(out_low, weight_output_ref[...])
    streams = jnp.concatenate([content_ref[...], stream_ref[...]], axis=0).astype(f32)
    residual = streams + attention_out
    rows, scale = normalized(residual)
    normed = rows * vector_ref[2:3, :] + vector_ref[3:4, :]
    normed_low = normed.astype(bf16)
    rows_ref[...] = rows
    scale_ref[...] = jnp.broadcast_to(scale, scale_ref.shape)
    normed_ref[...] = normed
    normed_low_ref[...] = normed_low
    lane = lax.broadcasted_iota(jnp.int32, (1, width), 1)
    total = jnp.zeros((1, width), f32)
    for at, value in enumerate((streams, attention_out, residual)):
        part = value[:half]
        summed = jnp.sum(jnp.sum(part * part, axis=0, keepdims=True), axis=1, keepdims=True)
        total = total + jnp.where((lane == at) | (lane == at + width // 2), summed, 0.0)
    square_ref[...] = jnp.broadcast_to(total, square_ref.shape)
    step = 512

    @pl.loop(0, hidden // step)
    def _(at):
        span = pl.ds(pl.multiple_of(at * step, step), step)
        inner = dot(normed_low, weight_inner_ref[:, span]) + bias_ref[0:1, span]
        below = 0.5 + 0.5 * lax.erf(inner * 0.7071067811865476)
        density = 0.3989422804014327 * jnp.exp(-0.5 * inner * inner)
        active_ref[:, span] = (inner * below).astype(bf16)
        slope_ref[:, span] = below + inner * density


def backward_half_kernel(
    place_ref,
    active_ref,
    slope_ref,
    normed_ref,
    rows_ref,
    scale_ref,
    weight_output_ref,
    weight_inner_ref,
    outer_own_ref,
    got_ref,
    rest_ref,
    vector_ref,
    square_ref,
    content_cotangent_ref,
    query_cotangent_ref,
    content_result_ref,
    query_result_ref,
    residual_back_ref,
    out_back_ref,
    outer_kept_ref,
    outer_sent_ref,
    inner_kept_ref,
    inner_sent_ref,
    attention_kept_ref,
    attention_sent_ref,
    sums_ref,
    weight_outer_ref,
    inner_back_ref,
    held_ref,
    bias_back_ref,
):
    width = normed_ref.shape[1]
    hidden = active_ref.shape[1]
    count = content_cotangent_ref.shape[0]
    core = place_ref[4]
    assemble(
        weight_outer_ref,
        outer_own_ref,
        got_ref,
        rest_ref,
        slice(0, width),
        (place_ref[5], place_ref[6], place_ref[7]),
    )

    def give(value_ref, kept_ref, sent_ref):
        columns = kept_ref.shape[1]
        kept_ref[...] = value_ref[:, pl.ds(pl.multiple_of(core * columns, lanes), columns)]
        sent_ref[...] = value_ref[:, pl.ds(pl.multiple_of((1 - core) * columns, lanes), columns)]

    outer = dot(active_ref[...], weight_outer_ref[...]) + vector_ref[4:5, :]
    final_rows, final_scale = normalized(normed_ref[...] + outer)
    result = (final_rows * vector_ref[5:6, :] + vector_ref[6:7, :]).astype(bf16)
    content_result_ref[...] = result[:count]
    query_result_ref[...] = result[count:]
    cotangent = jnp.concatenate(
        [content_cotangent_ref[...], query_cotangent_ref[...]], axis=0
    ).astype(f32)
    sums_ref[9:10, :] = jnp.sum(cotangent * final_rows, axis=0, keepdims=True)
    sums_ref[10:11, :] = jnp.sum(cotangent, axis=0, keepdims=True)
    back_second = norm_back(cotangent * vector_ref[5:6, :], final_rows, final_scale)
    outer_back = back_second.astype(bf16)
    sums_ref[8:9, :] = jnp.sum(outer_back.astype(f32), axis=0, keepdims=True)
    held_ref[...] = outer_back
    give(held_ref, outer_kept_ref, outer_sent_ref)
    residual_back_ref[...] = back_second
    step = 512

    @pl.loop(0, hidden // step)
    def _(at):
        span = pl.ds(pl.multiple_of(at * step, step), step)
        back = dot_nt(outer_back, weight_outer_ref[span, :]) * slope_ref[:, span]
        low = back.astype(bf16)
        inner_back_ref[:, span] = low
        bias_back_ref[0:1, span] = jnp.sum(low.astype(f32), axis=0, keepdims=True)
        residual_back_ref[...] += dot_nt(low, weight_inner_ref[:, span])

    give(inner_back_ref, inner_kept_ref, inner_sent_ref)
    normed_back = residual_back_ref[...]
    rows = rows_ref[...]
    sums_ref[6:7, :] = jnp.sum(normed_back * rows, axis=0, keepdims=True)
    sums_ref[7:8, :] = jnp.sum(normed_back, axis=0, keepdims=True)
    residual_back = norm_back(normed_back * vector_ref[2:3, :], rows, scale_ref[:, 0:1])
    residual_back_ref[...] = residual_back
    attention_back = residual_back.astype(bf16)
    held_ref[...] = attention_back
    give(held_ref, attention_kept_ref, attention_sent_ref)
    out_back_ref[...] = dot_nt(attention_back, weight_output_ref[...]).astype(bf16)
    part = width // 2
    for at in range(hidden // width):
        sums_ref[11 + at : 12 + at, :part] = bias_back_ref[0:1, at * part : (at + 1) * part]
        sums_ref[11 + at : 12 + at, part:] = bias_back_ref[
            0:1, hidden // 2 + at * part : hidden // 2 + (at + 1) * part
        ]
    last = 11 + hidden // width
    sums_ref[last : last + 1, :] = square_ref[0:1, :]
    sums_ref[0:6, :] = jnp.zeros((6, width), f32)


def forward_half(places, attended, content, stream, output_own, inner_own, got, rest, vectors, bias):
    rows, width = attended.shape
    hidden = inner_own.shape[1]
    shapes = [
        jax.ShapeDtypeStruct((rows, width), bf16),
        jax.ShapeDtypeStruct((rows, width), f32),
        jax.ShapeDtypeStruct((rows, width), f32),
        jax.ShapeDtypeStruct((rows, lanes), f32),
        jax.ShapeDtypeStruct((rows, width), bf16),
        jax.ShapeDtypeStruct((rows, hidden), bf16),
        jax.ShapeDtypeStruct((rows, hidden), f32),
        jax.ShapeDtypeStruct((8, width), f32),
        jax.ShapeDtypeStruct((width, width), bf16),
        jax.ShapeDtypeStruct((width, hidden), bf16),
    ]
    return pl.pallas_call(
        forward_half_kernel,
        in_specs=[in_smem] + [in_vmem] * 9,
        out_specs=[in_vmem] * len(shapes),
        out_shape=shapes,
        compiler_params=pltpu.CompilerParams(vmem_limit_bytes=48 << 20),
        cost_estimate=takes(8),
    )(places, attended, content, stream, output_own, inner_own, got, rest, vectors, bias)


def backward_half(places, *operands):
    active, normed = operands[0], operands[2]
    rows, width = normed.shape
    hidden = active.shape[1]
    count = rows // 2
    shapes = (
        [jax.ShapeDtypeStruct((count, width), bf16)] * 2
        + [jax.ShapeDtypeStruct((rows, width), f32), jax.ShapeDtypeStruct((rows, width), bf16)]
        + [jax.ShapeDtypeStruct((rows, width // 2), bf16)] * 2
        + [jax.ShapeDtypeStruct((rows, hidden // 2), bf16)] * 2
        + [jax.ShapeDtypeStruct((rows, width // 2), bf16)] * 2
        + [jax.ShapeDtypeStruct((16, width), f32)]
    )
    return pl.pallas_call(
        backward_half_kernel,
        in_specs=[in_smem] + [in_vmem] * len(operands),
        out_specs=[in_vmem] * len(shapes),
        out_shape=shapes,
        scratch_shapes=[
            pltpu.VMEM((hidden, width), bf16),
            pltpu.VMEM((rows, hidden), bf16),
            pltpu.VMEM((rows, width), bf16),
            pltpu.VMEM((8, hidden), f32),
        ],
        compiler_params=pltpu.CompilerParams(vmem_limit_bytes=56 << 20),
        cost_estimate=takes(12),
    )(places, *operands)


def body(
    content,
    query_stream,
    block_rank,
    segments,
    positions,
    query_weight,
    key_weight,
    value_weight,
    output_weight,
    content_bias,
    segment_bias,
    segment_embed,
    relative_table,
    attention_gain,
    attention_shift,
    inner_weight,
    inner_bias,
    outer_weight,
    outer_bias,
    final_gain,
    final_shift,
    content_cotangent,
    query_cotangent,
):
    block_rows = content.shape[1]
    width = content.shape[2]
    rows = 2 * block_rows
    count = lax.axis_size("ctx")
    sides = lax.axis_size("wsh")
    side = lax.axis_index("wsh")
    core = lax.axis_index("ctx") % 2
    length = block_rows * count
    own_content = content[0]
    own_query = query_stream[0]
    part = width // sides
    table_heads, bucket_count = relative_table.shape
    head_count = table_heads * sides
    inner_rows = inner_bias.shape[0] // part
    low = 2

    first_places = shard_places(query_weight.shape[0])
    first_sent = half_rows(first_places, query_weight, key_weight, value_weight)
    first_got = across(first_sent)
    mark_rows = 16
    marks = jnp.concatenate(
        [
            segments[0].astype(bf16),
            block_rank[0].astype(bf16),
            (positions[0, :1] // lanes).astype(bf16),
            (positions[0, :1] % lanes).astype(bf16),
        ]
    )
    marks = jnp.pad(marks[None], ((0, mark_rows - 1), (0, width - marks.shape[0])))
    block = jnp.concatenate([own_content, marks], axis=0)
    gathered = gather_blocks(block)
    small = jnp.concatenate(
        [
            content_bias,
            segment_bias,
            attention_gain,
            attention_shift,
            outer_bias,
            final_gain,
            final_shift,
            segment_embed.reshape(-1),
            inner_bias,
            relative_table.reshape(-1),
        ]
    )
    small_height = 16
    small = jnp.pad(small, (0, small_height * part - small.shape[0])).reshape(small_height, part)
    small_other = across(small)
    first_rest = partner(first_got, 1)
    second_sent = half_rows(first_places, output_weight, inner_weight)
    second_got = across(second_sent)
    third_places = shard_places(outer_weight.shape[0])
    third_sent = half_rows(third_places, outer_weight)
    third_got = across(third_sent)

    small_pair = jnp.where(
        side == 0,
        jnp.concatenate([small, small_other], axis=1),
        jnp.concatenate([small_other, small], axis=1),
    ).astype(f32)
    bias_content = small_pair[0:1]
    bias_segment = small_pair[1:2]
    embed = small_pair[7:9]
    bias_inner = jnp.concatenate(
        [
            small_pair[9 : 9 + inner_rows, :part].reshape(-1),
            small_pair[9 : 9 + inner_rows, part:].reshape(-1),
        ]
    )
    table_row = small_pair[9 + inner_rows]
    table_full = jnp.concatenate(
        [
            table_row[: table_heads * bucket_count],
            table_row[part : part + table_heads * bucket_count],
        ]
    ).reshape(head_count, bucket_count)

    held = block_rows + mark_rows
    if len(gathered) == 1:
        stacked = gathered[0].reshape(count, held, width)
        content_all = stacked[:, :block_rows].reshape(length, width)
        meta_all = stacked[:, block_rows:]
    else:
        plan = []
        place = 0
        for at, piece in enumerate(gathered):
            for row in range(0, piece.shape[0], held):
                plan.append(
                    (at, window(row, block_rows), 0, window(place * block_rows, block_rows))
                )
                plan.append(
                    (at, window(row + block_rows, mark_rows), 1, window(place * mark_rows, mark_rows))
                )
                place += 1
        content_all, meta_all = moved(
            tuple(plan),
            [
                jax.ShapeDtypeStruct((length, width), bf16),
                jax.ShapeDtypeStruct((count * mark_rows, width), bf16),
            ],
            first_places,
            *gathered,
        )
        meta_all = meta_all.reshape(count, mark_rows, width)
    pairs = width // lanes
    runs = [(0, 0, width, 0, 0)]
    for pair in range(pairs):
        runs.append((1, pair * lanes, lanes, 1, 2 * pair * lanes))
        runs.append((2, pair * lanes, lanes, 1, (2 * pair + 1) * lanes))
    weight_query, weight_both = whole_rows(
        first_places, runs, (width, 2 * width), first_got, first_rest, query_weight, key_weight, value_weight
    )
    key_code, table, number, row_code = key_marks(meta_all, table_full, length)

    streams = jnp.concatenate([own_content, own_query], axis=0)
    query_full = dot(streams, weight_query)
    both = dot(content_all, weight_both).astype(bf16)
    attended, log_row, stack = attention_forward(
        query_full, bias_content, bias_segment, embed, row_code, key_code, both, table
    )

    hidden = inner_weight.shape[1]
    second_got, third_got, attended = lax.optimization_barrier((second_got, third_got, attended))
    second_rest = partner(second_got, 1)
    third_rest = partner(third_got, 1)
    half_places = jnp.concatenate(
        [first_places, core[None].astype(jnp.int32), third_places[1:]]
    )
    (
        out_low,
        normed,
        norm_rows,
        norm_scale,
        normed_low,
        active_low,
        slope,
        squares,
        weight_output,
        weight_inner,
    ) = forward_half(
        half_places,
        attended,
        own_content,
        own_query,
        output_weight,
        inner_weight,
        second_got,
        second_rest,
        small_pair,
        bias_inner[None],
    )
    out_low_other = partner(out_low, 1)
    normed_other = partner(normed_low, 1)
    active_other = partner(active_low, 1)
    (
        content_result,
        query_result,
        residual_back,
        out_back,
        outer_kept,
        outer_sent,
        inner_kept,
        inner_sent,
        attention_kept,
        attention_sent,
        vectors,
    ) = backward_half(
        half_places,
        active_low,
        slope,
        normed,
        norm_rows,
        norm_scale,
        weight_output,
        weight_inner,
        outer_weight,
        third_got,
        third_rest,
        small_pair,
        squares,
        content_cotangent[0],
        query_cotangent[0],
    )

    cuts, extra = split_bits(count)
    wide_cuts = [1] + cuts
    order_one = [0] + cuts
    order_two = cuts[:1] + [0] + cuts[1:]
    places_one = piece_places(order_one, cuts)
    places_two = piece_places(order_two, cuts)
    wide_places = piece_places([1, 0] + cuts, wide_cuts)
    places_out = jnp.concatenate([piece_places(cuts, cuts), core[None].astype(jnp.int32)])
    wide_places_out = piece_places(wide_cuts, wide_cuts)

    outer_keep, outer_send = product_pieces(
        places_one, active_low, active_other, outer_kept, partner(outer_sent, 1)
    )
    outer_got = pass_on(outer_send, order_one[0])
    inner_keep, inner_send = product_pieces(
        places_two,
        normed_low,
        normed_other,
        inner_kept,
        partner(inner_sent, 1),
        out_low,
        out_low_other,
        attention_kept,
        partner(attention_sent, 1),
    )
    inner_got = pass_on(inner_send, order_two[0])

    line = cuts[1:]
    last = cuts[2]

    def add_extra(value):
        for bit in extra:
            value = fold_last(value, partner(value, bit))
        return value

    query_back, both_back, small_back = attention_backward(
        stack,
        query_full,
        bias_segment,
        embed,
        row_code,
        key_code,
        both,
        table,
        number,
        after(out_back, outer_send, inner_send),
        attended,
        log_row,
    )
    order = Sequence(small_back)
    outer_got, inner_got = order.wait(outer_got, inner_got)
    outer_keep, outer_send = fold(outer_keep, outer_got)
    outer_send = order.ready(outer_send)
    outer_got = partner(outer_send, cuts[0])
    inner_keep, inner_send = fold(inner_keep, inner_got)
    inner_send = order.ready(inner_send)
    inner_got = across(inner_send)

    hidden_rows = hidden // part // sides
    tail_keep, tail_send = cut_gradient(
        wide_places,
        vectors,
        small_back,
        dot_tn(streams, query_back),
        dot_tn(content_all, order.ready(both_back)),
    )
    tail_send = order.ready(tail_send)
    tail_got = partner(tail_send, 1)
    outer_got = order.wait(outer_got)
    outer_keep, outer_send = fold(outer_keep, outer_got)
    outer_send = order.ready(outer_send)
    outer_got = partner(outer_send, line[0])
    content_share = share_of_content(order.ready(both_back), weight_both)
    share_keep, share_send = content_share[: count // 2], order.ready(content_share[count // 2 :])
    share_got = partner(share_send, 1)
    tail_got = order.wait(tail_got)
    tail_keep, tail_send = fold(tail_keep, tail_got)
    tail_send = order.ready(tail_send)
    tail_got = across(tail_send)
    inner_got = order.wait(inner_got)
    inner_keep, inner_send = fold(inner_keep, inner_got)
    inner_send = order.ready(inner_send)
    inner_got = partner(inner_send, line[0])
    share_got = order.wait(share_got)
    share_keep, share_send = fold(share_keep, share_got)
    share_send = order.ready(share_send)
    share_got = partner(share_send, cuts[0])
    outer_got = order.wait(outer_got)
    outer_keep, outer_send = fold(outer_keep, outer_got)
    outer_send = order.ready(outer_send)
    outer_got = partner(outer_send, last)
    inner_got = order.wait(inner_got)
    inner_keep, inner_send = fold(inner_keep, inner_got)
    inner_send = order.ready(inner_send)
    inner_got = partner(inner_send, last)
    outer_got = order.wait(outer_got)
    outer_value = order.ready(add_extra(fold_last(outer_keep, outer_got)))
    outer_got = partner(outer_value, last)
    tail_got = order.wait(tail_got)
    tail_keep, tail_send = fold(tail_keep, tail_got)
    tail_send = order.ready(tail_send)
    tail_got = partner(tail_send, cuts[0])
    inner_got = order.wait(inner_got)
    inner_value = order.ready(add_extra(fold_last(inner_keep, inner_got)))
    inner_got = partner(inner_value, last)
    outer_got = order.wait(outer_got)
    outer_value = order.ready(piled(outer_value, outer_got))
    outer_got = partner(outer_value, line[0])
    share_got = order.wait(share_got)
    share_keep, share_send = fold(share_keep, share_got)
    share_send = order.ready(share_send)
    share_got = partner(share_send, line[0])
    inner_got = order.wait(inner_got)
    inner_value = order.ready(piled(inner_value, inner_got))
    inner_got = partner(inner_value, line[0])
    tail_got = order.wait(tail_got)
    tail_keep, tail_send = fold(tail_keep, tail_got)
    tail_send = order.ready(tail_send)
    tail_got = partner(tail_send, line[0])
    outer_got = order.wait(outer_got)
    outer_value = order.ready(piled(outer_value, outer_got))
    outer_got = partner(outer_value, cuts[0])
    share_got = order.wait(share_got)
    share_keep, share_send = fold(share_keep, share_got)
    share_send = order.ready(share_send)
    share_got = partner(share_send, last)
    streams_back = residual_back + dot_nt(order.ready(query_back), weight_query)
    tail_got = order.wait(tail_got)
    tail_keep, tail_send = fold(tail_keep, tail_got)
    tail_send = order.ready(tail_send)
    tail_got = partner(tail_send, last)
    inner_got = order.wait(inner_got)
    inner_value = order.ready(piled(inner_value, inner_got))
    inner_got = partner(inner_value, cuts[0])
    tail_got = order.wait(tail_got)
    tail_value = order.ready(add_extra(fold_last(tail_keep, tail_got)))
    tail_got = partner(tail_value, last)
    outer_got = order.wait(outer_got)
    outer_value = order.ready(piled(outer_value, outer_got))
    outer_got = partner(outer_value, 1)
    share_got = order.wait(share_got)
    for bit in extra:
        share_keep, share_send = fold(share_keep, share_got)
        share_got = partner(share_send, bit)
    content_back = streams_back[:block_rows] + share_keep[0].astype(f32) + share_got[0].astype(f32)
    content_back, outer_got = order.wait(content_back, outer_got)
    (outer_weight_sum,) = lay_out(
        places_out,
        (((0, 0, width // 2, -1), (1, 0, width // 2, -2)),),
        outer_value,
        outer_got,
    )
    outer_weight_sum = order.ready(outer_weight_sum)
    tail_got = order.wait(tail_got)
    tail_value = order.ready(piled(tail_value, tail_got))
    tail_got = partner(tail_value, line[0])
    inner_got = order.wait(inner_got)
    inner_value = order.ready(piled(inner_value, inner_got))
    inner_got = partner(inner_value, 1)
    tail_got = order.wait(tail_got)
    tail_value = order.ready(piled(tail_value, tail_got))
    tail_got = partner(tail_value, cuts[0])
    inner_got = order.wait(inner_got)
    inner_weight_sum, output_weight_sum = lay_out(
        places_out,
        (
            ((0, 0, hidden // 2, -1), (1, 0, hidden // 2, -2)),
            ((0, hidden // 2, width // 2, -1), (1, hidden // 2, width // 2, -2)),
        ),
        inner_value,
        inner_got,
    )
    inner_weight_sum, output_weight_sum = order.ready(inner_weight_sum, output_weight_sum)
    tail_got = order.wait(tail_got)
    tail_value = order.ready(piled(tail_value, tail_got))
    tail_got = partner(tail_value, 1)
    plan = []
    for kind in range(3):
        row = []
        for pair in range(pairs):
            taken = pair * lanes if kind == 0 else width + (2 * pair + kind - 1) * lanes
            row.append((0, taken, lanes, pair * lanes))
        plan.append(tuple(row))
    plan.append(((0, 3 * width, lanes, 0),))
    query_weight_sum, key_weight_sum, value_weight_sum, vector_sums = lay_out(
        wide_places_out, tuple(plan), tail_value, tail_got
    )
    sums = vector_sums[:, :16].T
    table_sum = jnp.swapaxes(sums[4:6].reshape(2, -1, lanes)[:, :, :bucket_count], 0, 1).reshape(
        table_heads, bucket_count
    )
    inner_bias_sum = sums[11 : 11 + hidden_rows].reshape(-1)
    token_total = length * sides * width
    root_mean = jnp.sqrt(sums[11 + hidden_rows, :3] / token_total)
    return (
        content_result[None],
        query_result[None],
        content_back[None],
        streams_back[block_rows:][None],
        query_weight_sum,
        key_weight_sum,
        value_weight_sum,
        output_weight_sum,
        sums[0],
        sums[1],
        sums[2:4],
        table_sum,
        sums[6],
        sums[7],
        inner_weight_sum,
        inner_bias_sum,
        outer_weight_sum,
        sums[8],
        sums[9],
        sums[10],
        root_mean,
    )


def solution(mesh):
    tokens = P("wsh", "ctx", None)
    marks = P("wsh", "ctx")
    matrix = P("wsh", None)
    vector = P("wsh")
    placed = (
        (tokens, tokens, marks, marks, marks)
        + (matrix,) * 4
        + (vector, vector, P(None, "wsh"), matrix, vector, vector, matrix, vector, matrix)
        + (vector,) * 3
        + (tokens, tokens)
    )
    given = (
        (tokens,) * 4
        + (matrix,) * 4
        + (vector, vector, P(None, "wsh"), matrix, vector, vector, matrix, vector, matrix)
        + (vector,) * 3
        + (P(),)
    )
    return jax.shard_map(body, mesh=mesh, in_specs=placed, out_specs=given, check_vma=False)
```

```python
import functools

import jax
import jax.numpy as jnp
from jax import lax
from jax.experimental import pallas as pl
from jax.experimental.pallas import tpu as pltpu
from jax.sharding import PartitionSpec as P

negative = -1e30
epsilon = 1e-05
bucket_steps = 16
key_tile = 256
lanes = 128
highest = lax.Precision.HIGHEST
f32 = jnp.float32
bf16 = jnp.bfloat16


free = pl.CostEstimate(flops=0, bytes_accessed=0, transcendentals=0)
in_vmem = pl.BlockSpec(memory_space=pltpu.VMEM)
in_smem = pl.BlockSpec(memory_space=pltpu.SMEM)


def resident(value):
    rank = len(value.shape)
    return pl.BlockSpec(value.shape, lambda at: (0,) * rank, pipeline_mode=pl.Buffered(1))


def takes(microseconds):
    return pl.CostEstimate(
        flops=microseconds * 1_000_000_000, bytes_accessed=0, transcendentals=0
    )


def normalized(values):
    centred = values - jnp.mean(values, axis=-1, keepdims=True)
    spread = jnp.mean(centred * centred, axis=-1, keepdims=True)
    scale = lax.rsqrt(spread + epsilon)
    return centred * scale, scale


def norm_back(cotangent, rows, scale):
    mean = jnp.mean(cotangent, axis=-1, keepdims=True)
    along = jnp.mean(cotangent * rows, axis=-1, keepdims=True)
    return scale * (cotangent - mean - rows * along)


def dot(left, right):
    return jnp.dot(left, right, preferred_element_type=f32)


def dot_nt(left, right):
    return lax.dot_general(left, right, (((1,), (1,)), ((), ())), preferred_element_type=f32)


def dot_tn(left, right):
    return lax.dot_general(left, right, (((0,), (0,)), ((), ())), preferred_element_type=f32)


def partner(value, bit):
    count = lax.axis_size("ctx")
    return lax.ppermute(value, "ctx", [(place, place ^ bit) for place in range(count)])


def across(value):
    return lax.ppermute(value, "wsh", [(0, 1), (1, 0)])


def bits_of(count):
    result = []
    bit = 1
    while bit < count:
        result.append(bit)
        bit *= 2
    return result


def block_order(count):
    order = [0]
    for bit in reversed(bits_of(count)):
        order = order + [place | bit for place in order]
    return order


def gather_blocks(own):
    count = lax.axis_size("ctx")
    bits = bits_of(count)
    if count != 16:
        held = own
        for bit in reversed(bits):
            held = jnp.concatenate([held, partner(held, bit)], axis=0)
        return [held]
    low = bits[1]
    near = partner(own, low)
    first = [own] + [partner(own, place) for place in (bits[3], bits[2], bits[2] | bits[3])]
    second = [near] + [partner(block, low) for block in first[1:]]
    others = partner(jnp.concatenate(first + second, axis=0), 1)
    return first + second + [others]


def move_kernel(plan, inputs, place_ref, *refs):
    sources, targets = refs[:inputs], refs[inputs:]
    for source, taken, target, put in plan:
        targets[target][put(place_ref)] = sources[source][taken(place_ref)]


def moved(plan, shapes, places, *sources):
    return pl.pallas_call(
        functools.partial(move_kernel, plan, len(sources)),
        grid=(1,),
        in_specs=[in_smem] + [resident(value) for value in sources],
        out_specs=[resident(shape) for shape in shapes],
        out_shape=shapes,
        compiler_params=pltpu.CompilerParams(vmem_limit_bytes=40 << 20),
        cost_estimate=free,
    )(places, *sources)


def window(start, rows, left=None, columns=None):
    def make(place_ref):
        first = start
        if isinstance(start, str):
            first = pl.multiple_of(place_ref[int(start)], 16)
        if left is None:
            return (pl.ds(first, rows), slice(None))
        return (pl.ds(first, rows), pl.ds(left, columns))

    return make


def half_rows(places, cut, *shards):
    rows = shards[0].shape[0] // 2 // cut
    plan = []
    left = 0
    for at, shard in enumerate(shards):
        columns = shard.shape[1]
        plan.append((at, window("0", rows, 0, columns), 0, window(0, rows, left, columns)))
        left += columns
    return moved(tuple(plan), [jax.ShapeDtypeStruct((rows, left), bf16)], places, *shards)[0]


def whole_rows(places, runs, widths, got, rest, *shards):
    rows = shards[0].shape[0]
    half = rows // 2
    lefts = [0]
    for shard in shards:
        lefts.append(lefts[-1] + shard.shape[1])
    plan = []
    for shard, first, columns, target, column in runs:
        plan.append(
            (2 + shard, window(0, rows, first, columns), target, window("1", rows, column, columns))
        )
        for source, place in ((0, "2"), (1, "3")):
            plan.append(
                (
                    source,
                    window(0, half, lefts[shard] + first, columns),
                    target,
                    window(place, half, column, columns),
                )
            )
    shapes = [jax.ShapeDtypeStruct((2 * rows, width), bf16) for width in widths]
    return moved(tuple(plan), shapes, places, got, rest, *shards)


def quarter_places(rows):
    core = lax.axis_index("ctx") % 2
    near = (lax.axis_index("ctx") // 2) % 2
    side = lax.axis_index("wsh")
    quarter = rows // 4
    base = (1 - side) * rows
    spots = [(core, near), (core, 1 - near), (1 - core, near), (1 - core, 1 - near)]
    return jnp.stack(
        [(2 * core + near) * quarter, side * rows]
        + [base + (2 * first + second) * quarter for first, second in spots]
    ).astype(jnp.int32)


def shard_places(rows):
    core = lax.axis_index("ctx") % 2
    side = lax.axis_index("wsh")
    half = rows // 2
    base = (1 - side) * rows
    return jnp.stack(
        [core * half, side * rows, base + core * half, base + (1 - core) * half]
    ).astype(jnp.int32)


def split_bits(count):
    bits = bits_of(count)
    return bits[1:4], bits[4:]


def own_bit(bit):
    if bit == 0:
        return lax.axis_index("wsh")
    return (lax.axis_index("ctx") // bit) % 2


def pass_on(value, bit):
    return across(value) if bit == 0 else partner(value, bit)


def pass_mixed(value, even_bit, odd_bit):
    count = lax.axis_size("ctx")
    pairs = []
    for place in range(count):
        bit = odd_bit if place % 2 else even_bit
        for side in range(2):
            other = (place, 1 - side) if bit == 0 else (place ^ bit, side)
            pairs.append((2 * place + side, 2 * other[0] + other[1]))
    return lax.ppermute(value, ("ctx", "wsh"), pairs)


def by_core(even, odd, half):
    core = lax.axis_index("ctx") % 2
    return jnp.where(
        core == 0,
        jnp.concatenate([even[:half], odd[half:]]),
        jnp.concatenate([odd[:half], even[half:]]),
    )


class Sequence:
    def __init__(self, mark):
        self.mark = mark

    def wait(self, *values):
        *values, self.mark = lax.optimization_barrier(tuple(values) + (self.mark,))
        return values[0] if len(values) == 1 else tuple(values)

    ready = wait


def piece_places(order, cuts):
    total = len(order)
    place = jnp.arange(1 << total, dtype=jnp.int32)
    result = jnp.zeros_like(place)
    for at, bit in enumerate(order):
        value = ((place >> (total - 1 - at)) & 1) ^ own_bit(bit)
        weight = 1 << len(cuts) if bit == 0 else 1 << (len(cuts) - 1 - cuts.index(bit))
        result = result + value * weight
    return result


def fold_kernel(keep_ref, received_ref, *target_refs):
    first = 0
    for target_ref in target_refs:

        @pl.loop(0, target_ref.shape[0])
        def _(place, first=first, target_ref=target_ref):
            target_ref[place] = (
                keep_ref[first + place].astype(f32) + received_ref[first + place].astype(f32)
            ).astype(bf16)

        first += target_ref.shape[0]


def fold_parts(keep, received, parts):
    piece = jax.ShapeDtypeStruct((keep.shape[0] // parts,) + keep.shape[1:], bf16)
    return pl.pallas_call(
        fold_kernel,
        grid=(1,),
        in_specs=[resident(keep)] * 2,
        out_specs=[resident(piece)] * parts,
        out_shape=[piece] * parts,
        compiler_params=pltpu.CompilerParams(vmem_limit_bytes=40 << 20),
        cost_estimate=free,
    )(keep, received)


def fold(keep, received):
    return fold_parts(keep, received, 2)


def fold_last(keep, received):
    return fold_parts(keep, received, 1)[0]


def pile_kernel(*refs):
    target_ref = refs[-1]
    first = 0
    for source_ref in refs[:-1]:

        @pl.loop(0, source_ref.shape[0])
        def _(place, first=first, source_ref=source_ref):
            target_ref[first + place] = source_ref[place]

        first += source_ref.shape[0]


def piled(*values):
    height = sum(value.shape[0] for value in values)
    return pl.pallas_call(
        pile_kernel,
        in_specs=[in_vmem] * len(values),
        out_specs=in_vmem,
        out_shape=jax.ShapeDtypeStruct((height,) + values[0].shape[1:], values[0].dtype),
        compiler_params=pltpu.CompilerParams(vmem_limit_bytes=40 << 20),
        cost_estimate=free,
    )(*values)


def share_kernel(back_ref, weight_ref, out_ref):
    out_ref[...] = dot_nt(back_ref[...], weight_ref[...]).astype(bf16).reshape(out_ref.shape)


def share_of_content(both_back, weight_both):
    count, columns = both_back.shape
    width = weight_both.shape[0]
    step = 2 * lanes
    return pl.pallas_call(
        share_kernel,
        grid=(count // step,),
        in_specs=[
            pl.BlockSpec((step, columns), lambda at: (at, 0)),
            pl.BlockSpec((width, columns), lambda at: (0, 0), pipeline_mode=pl.Buffered(1)),
        ],
        out_specs=pl.BlockSpec((2, lanes, width), lambda at: (at, 0, 0)),
        out_shape=jax.ShapeDtypeStruct((count // lanes, lanes, width), bf16),
        compiler_params=pltpu.CompilerParams(vmem_limit_bytes=40 << 20),
        cost_estimate=free,
    )(both_back, weight_both)


def after(value, *others):
    return lax.optimization_barrier((value,) + others)[0]


def product_kernel(groups, place_ref, *refs):
    operands, (keep_ref, send_ref, total_ref) = refs[: 4 * groups], refs[4 * groups :]
    rows = keep_ref.shape[1]
    step = 256
    left = 0
    for group in range(groups):
        left_own, left_other, right_own, right_other = operands[4 * group : 4 * group + 4]
        columns = right_own.shape[1]
        for start in range(0, left_own.shape[1], step):
            total_ref[start : start + step, left : left + columns] = dot_tn(
                left_own[:, start : start + step], right_own[...]
            ) + dot_tn(left_other[:, start : start + step], right_other[...])
        left += columns
    for at, ref in enumerate((keep_ref, send_ref)):

        @pl.loop(0, ref.shape[0])
        def _(place, at=at, ref=ref):
            block = place_ref[at * ref.shape[0] + place]
            start = pl.multiple_of(block * rows, 8)
            ref[place] = total_ref[pl.ds(start, rows), :].astype(bf16)


def product_pieces(places, *operands):
    groups = len(operands) // 4
    half = places.shape[0] // 2
    height = operands[0].shape[1]
    columns = sum(operands[4 * group + 2].shape[1] for group in range(groups))
    piece = jax.ShapeDtypeStruct((half, height // (2 * half), columns), bf16)
    return pl.pallas_call(
        functools.partial(product_kernel, groups),
        grid=(1,),
        in_specs=[in_smem] + [resident(value) for value in operands],
        out_specs=[resident(piece)] * 2,
        out_shape=[piece, piece],
        scratch_shapes=[pltpu.VMEM((height, columns), f32)],
        compiler_params=pltpu.CompilerParams(vmem_limit_bytes=60 << 20),
        cost_estimate=takes(4),
    )(places, *operands)


def cut_kernel(place_ref, vector_ref, small_ref, *refs):
    parts, (keep_ref, send_ref, turned_ref) = refs[:-3], refs[-3:]
    rows = keep_ref.shape[1]
    height = vector_ref.shape[1]
    filled = jnp.concatenate(
        [
            small_ref[...] + vector_ref[0:8, :],
            vector_ref[8:, :],
            jnp.zeros((lanes - vector_ref.shape[0], height), f32),
        ],
        axis=0,
    )
    for start in range(0, height, lanes):
        turned_ref[start : start + lanes, :] = filled[:, start : start + lanes].T
    parts = parts + (turned_ref,)
    for at, ref in enumerate((keep_ref, send_ref)):

        @pl.loop(0, ref.shape[0])
        def _(place, at=at, ref=ref):
            block = place_ref[at * ref.shape[0] + place]
            start = pl.multiple_of(block * rows, 8)
            left = 0
            for part in parts:
                columns = part.shape[1]
                ref[place, :, left : left + columns] = part[pl.ds(start, rows), :].astype(bf16)
                left += columns


def cut_gradient(places, vectors, small, *parts):
    half = places.shape[0] // 2
    height = parts[0].shape[0]
    columns = sum(part.shape[1] for part in parts) + lanes
    piece = jax.ShapeDtypeStruct((half, height // (2 * half), columns), bf16)
    return pl.pallas_call(
        cut_kernel,
        grid=(1,),
        in_specs=[in_smem] + [resident(value) for value in (vectors, small) + parts],
        out_specs=[resident(piece)] * 2,
        out_shape=[piece, piece],
        scratch_shapes=[pltpu.VMEM((height, lanes), f32)],
        compiler_params=pltpu.CompilerParams(vmem_limit_bytes=40 << 20),
        cost_estimate=free,
    )(places, vectors, small, *parts)


def lay_out_kernel(plan, place_ref, *refs):
    outputs = len(plan)
    sources, targets = refs[:-outputs], refs[-outputs:]
    halves = 2 if place_ref.shape[0] > sources[0].shape[0] + 1 else 1
    for half in range(halves):
      for runs, target in zip(plan, targets, strict=True):
        for source, first, columns, column in runs:
            piece_ref = sources[source + half]
            count, rows = piece_ref.shape[:2]

            @pl.loop(0, count)
            def _(place, piece_ref=piece_ref, rows=rows, target=target, first=first, columns=columns, column=column, half=half):
                start = pl.multiple_of(place_ref[half * count + place] * rows, 8)
                value = piece_ref[place, :, first : first + columns].astype(f32)
                if column >= 0:
                    target[pl.ds(start, rows), column : column + columns] = value
                else:
                    core = place_ref[count]
                    which = core if column == -1 else 1 - core
                    left = pl.multiple_of(which * columns, lanes)
                    target[pl.ds(start, rows), pl.ds(left, columns)] = value


def lay_out(places, plan, *pieces):
    shapes = []
    halves = 2 if places.shape[0] > pieces[0].shape[0] + 1 else 1
    for runs in plan:
        count, rows = pieces[runs[0][0]].shape[:2]
        shapes.append(jax.ShapeDtypeStruct((halves * count * rows, sum(run[2] for run in runs)), f32))
    return pl.pallas_call(
        functools.partial(lay_out_kernel, plan),
        grid=(1,),
        in_specs=[in_smem] + [resident(value) for value in pieces],
        out_specs=[resident(shape) for shape in shapes],
        out_shape=shapes,
        compiler_params=pltpu.CompilerParams(vmem_limit_bytes=40 << 20),
        cost_estimate=takes(3),
    )(places, *pieces)


def stream_bias(table_ref, head, block):
    spread = jnp.broadcast_to(table_ref[head, pl.ds(block, 1), :], (lanes, 2 * lanes))
    return pltpu.roll(spread, 0, 1, stride=1, stride_axis=0)[:, :lanes]


def tile_bias(table_ref, block):
    parts = []
    for piece in range(key_tile // lanes):
        first = stream_bias(table_ref, 0, block + piece)
        second = stream_bias(table_ref, 1, block + piece)
        parts.append(jnp.concatenate([first, first, second, second], axis=1))
    return jnp.concatenate(parts, axis=0)


def own_mask():
    row = lax.broadcasted_iota(jnp.int32, (key_tile, 4 * lanes), 0)
    column = lax.broadcasted_iota(jnp.int32, (key_tile, 4 * lanes), 1)
    stream = (column // lanes) % 2
    return jnp.where((stream == 1) & (row == column % lanes), negative, 0.0)


def forward_kernel(
    query_ref,
    content_bias_ref,
    segment_bias_ref,
    embed_ref,
    row_code_ref,
    key_code_ref,
    both_ref,
    table_ref,
    out_ref,
    log_ref,
    stack_ref,
    score_ref,
):
    rows = query_ref.shape[0]
    tiles = both_ref.shape[0] // key_tile
    lane = lax.broadcasted_iota(jnp.int32, (rows, lanes), 1)
    first = lane < lanes // 2
    query = query_ref[...]
    low = (query + content_bias_ref[...]).astype(bf16).astype(f32) * 0.125
    shifted = query + segment_bias_ref[...]
    zero_term = shifted * embed_ref[0:1, :]
    one_term = shifted * embed_ref[1:2, :]
    code = row_code_ref[...]
    for head in range(2):
        own = first if head == 0 else jnp.logical_not(first)
        zero_sum = jnp.sum(jnp.where(own, zero_term, 0.0), axis=1, keepdims=True) * 0.125
        one_sum = jnp.sum(jnp.where(own, one_term, 0.0), axis=1, keepdims=True) * 0.125
        step = zero_sum - one_sum
        step_high = step.astype(bf16).astype(f32)
        step_low = step - step_high
        one_high = one_sum.astype(bf16).astype(f32)
        one_low = one_sum - one_high
        extra = jnp.where(
            lane < 4,
            step_high,
            jnp.where(lane < 8, step_low, jnp.where(lane == 8, one_high, one_low)),
        )
        stack_ref[0, pl.ds(head * rows, rows), 0:lanes] = jnp.where(own, low, 0.0).astype(bf16)
        stack_ref[0, pl.ds(head * rows, rows), lanes : 2 * lanes] = (extra * code).astype(bf16)
    stack = stack_ref[0]

    def scores(tile, top):
        start = pl.multiple_of(tile * key_tile, key_tile)
        keys = jnp.concatenate(
            [both_ref[pl.ds(start, key_tile), :lanes], key_code_ref[pl.ds(start, key_tile), :]], axis=1
        )
        score = dot_nt(keys, stack) + tile_bias(table_ref, tile * (key_tile // lanes))
        if isinstance(tile, int) and tile == 0:
            score = score + own_mask()
        score_ref[pl.ds(start, key_tile), :] = score
        return jnp.maximum(top, jnp.max(score.reshape(key_tile // 8, 8, 4 * lanes), axis=0))

    top = jnp.full((8, 4 * lanes), negative, f32)
    top = scores(0, top)
    top = lax.fori_loop(1, tiles, scores, top, unroll=min(7, tiles - 1))
    peak = jnp.max(top, axis=0, keepdims=True)

    def gathered(tile, running):
        total, mixed = running
        start = pl.multiple_of(tile * key_tile, key_tile)
        weight = jnp.exp(score_ref[pl.ds(start, key_tile), :] - peak)
        total = total + jnp.sum(weight.reshape(key_tile // 8, 8, 4 * lanes), axis=0)
        mixed = mixed + dot_tn(both_ref[pl.ds(start, key_tile), lanes:], weight.astype(bf16))
        return total, mixed

    total, mixed = lax.fori_loop(
        0,
        tiles,
        gathered,
        (jnp.zeros((8, 4 * lanes), f32), jnp.zeros((lanes, 4 * lanes), f32)),
        unroll=min(8, tiles),
    )
    total = jnp.sum(total, axis=0, keepdims=True)
    mixed = mixed / total
    half = lanes // 2
    joined = jnp.concatenate([mixed[:half, :rows], mixed[half:, rows:]], axis=0)
    out_ref[...] = joined.T
    log_ref[0] = peak + jnp.log(total)


def diagonal_sums(square):
    lane = lax.broadcasted_iota(jnp.int32, (8, lanes), 1)
    near = square[0:8]
    far = jnp.zeros((8, lanes), f32)
    for group in range(1, lanes // 8):
        turned = pltpu.roll(square[8 * group : 8 * group + 8], lanes - 8 * group, 1)
        inside = lane < lanes - 8 * group
        near = near + jnp.where(inside, turned, 0.0)
        far = far + jnp.where(inside, 0.0, turned)
    both = jnp.concatenate([near, far], axis=1)
    row = lax.broadcasted_iota(jnp.int32, (8, 2 * lanes), 0)
    for bit in (1, 2, 4):
        both = jnp.where((row // bit) % 2 == 1, pltpu.roll(both, 2 * lanes - bit, 1), both)
    return jnp.sum(both, axis=0, keepdims=True)


def backward_kernel(
    stack_ref,
    query_ref,
    segment_bias_ref,
    embed_ref,
    row_code_ref,
    key_code_ref,
    both_ref,
    table_ref,
    number_ref,
    out_back_ref,
    attended_ref,
    log_ref,
    query_back_ref,
    both_back_ref,
    small_ref,
    diagonal_ref,
):
    rows = query_ref.shape[0]
    tiles = both_ref.shape[0] // key_tile
    half = lanes // 2
    lane = lax.broadcasted_iota(jnp.int32, (rows, lanes), 1)
    first = lane < half
    out_back = out_back_ref[...]
    product = (out_back.astype(f32) * attended_ref[...]).T
    delta = jnp.concatenate(
        [
            jnp.sum(product[:half], axis=0, keepdims=True),
            jnp.sum(product[half:], axis=0, keepdims=True),
        ],
        axis=1,
    )
    zeros = jnp.zeros_like(out_back)
    back_stack = jnp.concatenate(
        [jnp.where(first, out_back, zeros), jnp.where(first, zeros, out_back)], axis=0
    )
    stack = stack_ref[0]
    query_stack = stack[:, :lanes]
    log_row = log_ref[0]

    def step(tile, running):
        start = pl.multiple_of(tile * key_tile, key_tile)
        block = tile * (key_tile // lanes)
        keys = jnp.concatenate(
            [both_ref[pl.ds(start, key_tile), :lanes], key_code_ref[pl.ds(start, key_tile), :]], axis=1
        )
        score = dot_nt(keys, stack) + tile_bias(table_ref, block)
        if isinstance(tile, int) and tile == 0:
            score = score + own_mask()
        weight = jnp.exp(score - log_row)
        weight_back = dot_nt(both_ref[pl.ds(start, key_tile), lanes:], back_stack)
        score_back = weight * (weight_back - delta)
        score_low = score_back.astype(bf16)
        both_back_ref[pl.ds(start, key_tile), lanes:] = dot(
            weight.astype(bf16), back_stack
        ).astype(bf16)
        both_back_ref[pl.ds(start, key_tile), :lanes] = dot(score_low, query_stack).astype(bf16)
        for head in range(2):
            for piece in range(key_tile // lanes):
                part = score_back[
                    piece * lanes : (piece + 1) * lanes, head * rows : (head + 1) * rows
                ]
                square = part[:, :lanes] + part[:, lanes:]
                diagonal_ref[head, block + piece] = diagonal_sums(square)[0]
        return running + dot_tn(keys, score_low)

    diagonal_ref[2:] = jnp.zeros(diagonal_ref[2:].shape, f32)
    running = step(0, jnp.zeros((2 * lanes, 2 * rows), f32))
    running = lax.fori_loop(1, tiles, step, running, unroll=min(7, tiles - 1))
    joined = jnp.concatenate([running[:half, :rows], running[half:lanes, rows:]], axis=0).T * 0.125
    shifted = query_ref[...] + segment_bias_ref[...]
    code = row_code_ref[...]
    zero_columns = []
    one_columns = []
    for head in range(2):
        part = running[lanes:, head * rows : (head + 1) * rows].T * 0.125
        same = jnp.sum(jnp.where(lane < 4, part * code, 0.0), axis=1, keepdims=True)
        total = jnp.sum(jnp.where(lane == 8, part, 0.0), axis=1, keepdims=True)
        zero_columns.append(same)
        one_columns.append(total - same)
    zero_back = jnp.where(first, zero_columns[0], zero_columns[1])
    one_back = jnp.where(first, one_columns[0], one_columns[1])
    shift_back = zero_back * embed_ref[0:1, :] + one_back * embed_ref[1:2, :]
    query_back_ref[...] = (joined + shift_back).astype(bf16)
    small_ref[0:1, :] = jnp.sum(joined, axis=0, keepdims=True)
    small_ref[1:2, :] = jnp.sum(shift_back, axis=0, keepdims=True)
    small_ref[2:3, :] = jnp.sum(zero_back * shifted, axis=0, keepdims=True)
    small_ref[3:4, :] = jnp.sum(one_back * shifted, axis=0, keepdims=True)
    blocks = number_ref.shape[0]
    bucket = lax.broadcasted_iota(jnp.int32, (lanes, 2 * lanes), 0)
    table_back = jnp.zeros((8, lanes), f32)
    for block in range(blocks):
        chosen = jnp.where(bucket == number_ref[block : block + 1, :], 1.0, 0.0).astype(bf16)
        sums = diagonal_ref[:, block, :]
        for _ in range(3):
            part = sums.astype(bf16)
            table_back = table_back + dot_nt(part, chosen)
            sums = sums - part.astype(f32)
    small_ref[4:8, :] = table_back[:4]


def attention_specs(rows, keys, blocks, first_pair=0):
    column = lambda pair: (0, pair + first_pair)
    fixed = lambda pair: (0, 0)
    front = lambda pair: (pair + first_pair, 0, 0)
    return {
        "rows": pl.BlockSpec((rows, lanes), column),
        "row": pl.BlockSpec((1, lanes), column),
        "embed": pl.BlockSpec((2, lanes), column),
        "small": pl.BlockSpec((8, lanes), column),
        "row_code": pl.BlockSpec((rows, lanes), fixed),
        "key_code": pl.BlockSpec((keys, lanes), fixed, pipeline_mode=pl.Buffered(1)),
        "both": pl.BlockSpec((keys, 2 * lanes), column),
        "table": pl.BlockSpec((2, blocks, 2 * lanes), front),
        "log": pl.BlockSpec((1, 1, 2 * rows), front),
        "stack": pl.BlockSpec((1, 2 * rows, 2 * lanes), front),
    }


def attention_forward(query_full, bias_content, bias_segment, embed, row_code, key_code, both, table):
    rows, width = query_full.shape
    count = both.shape[0]
    pairs = width // lanes
    spec = attention_specs(rows, count, count // lanes)
    return pl.pallas_call(
        forward_kernel,
        grid=(pairs,),
        in_specs=[
            spec["rows"],
            spec["row"],
            spec["row"],
            spec["embed"],
            spec["row_code"],
            spec["key_code"],
            spec["both"],
            spec["table"],
        ],
        out_specs=[spec["rows"], spec["log"], spec["stack"]],
        out_shape=[
            jax.ShapeDtypeStruct((rows, width), f32),
            jax.ShapeDtypeStruct((pairs, 1, 2 * rows), f32),
            jax.ShapeDtypeStruct((pairs, 2 * rows, 2 * lanes), bf16),
        ],
        scratch_shapes=[pltpu.VMEM((count, 2 * rows), f32)],
        compiler_params=pltpu.CompilerParams(
            dimension_semantics=("arbitrary",), vmem_limit_bytes=60 << 20
        ),
        cost_estimate=free,
    )(query_full, bias_content, bias_segment, embed, row_code, key_code, both, table)


def attention_backward(stack, query_full, bias_segment, embed, row_code, key_code, both, table, number, out_back, attended, log_row):
    rows, width = query_full.shape
    count = both.shape[0]
    pairs = width // lanes
    blocks = count // lanes
    spec = attention_specs(rows, count, blocks)
    return pl.pallas_call(
        backward_kernel,
        grid=(pairs,),
        in_specs=[
            spec["stack"],
            spec["rows"],
            spec["row"],
            spec["embed"],
            spec["row_code"],
            spec["key_code"],
            spec["both"],
            spec["table"],
            pl.BlockSpec((blocks, 2 * lanes), lambda pair: (0, 0)),
            spec["rows"],
            spec["rows"],
            spec["log"],
        ],
        out_specs=[spec["rows"], spec["both"], spec["small"]],
        out_shape=[
            jax.ShapeDtypeStruct((rows, width), bf16),
            jax.ShapeDtypeStruct((count, 2 * width), bf16),
            jax.ShapeDtypeStruct((8, width), f32),
        ],
        scratch_shapes=[pltpu.VMEM((8, blocks, 2 * lanes), f32)],
        compiler_params=pltpu.CompilerParams(
            dimension_semantics=("arbitrary",), vmem_limit_bytes=60 << 20
        ),
        cost_estimate=takes(34),
    )(stack, query_full, bias_segment, embed, row_code, key_code, both, table, number, out_back, attended, log_row)


def marks_kernel(bound_list, meta_ref, table_ref, key_code_ref, bias_ref, number_ref, row_code_ref):
    blocks = meta_ref.shape[0]
    info = meta_ref[:, 0, :].astype(f32)
    segment = info[:, :lanes]
    rank = info[:, lanes : lanes + 1]
    first = info[:, lanes + 1 : lanes + 2] * lanes + info[:, lanes + 2 : lanes + 3]
    turn = lax.broadcasted_iota(jnp.int32, (blocks, 2 * lanes), 1)
    turn = jnp.where(turn < lanes, turn, turn - 2 * lanes)
    distance = (first[0:1, :] - first).astype(jnp.int32) + turn
    number = jnp.full(distance.shape, bucket_steps, jnp.int32)
    for bound in bound_list:
        number = number + (distance >= bound).astype(jnp.int32) - (distance <= -bound).astype(jnp.int32)
    number_ref[...] = number
    hidden = rank > rank[0:1, :]
    for head in range(bias_ref.shape[0]):
        value = jnp.zeros((blocks, 2 * lanes), f32)
        for bucket in range(2 * bucket_steps + 1):
            value = jnp.where(number == bucket, table_ref[head, bucket], value)
        bias_ref[head] = jnp.where(hidden, negative, value)
    lane = lax.broadcasted_iota(jnp.int32, (lanes, lanes), 1)
    code = (lane % 4).astype(f32)
    for block in range(blocks):
        column = jnp.broadcast_to(segment[block : block + 1, :], (lanes, lanes)).T
        marked = jnp.where(
            lane < 8, jnp.where(column == code, 1.0, 0.0), jnp.where(lane < 10, 1.0, 0.0)
        )
        key_code_ref[block * lanes : (block + 1) * lanes, :] = marked.astype(bf16)
        if block == 0:
            row_code_ref[:lanes, :] = marked
            row_code_ref[lanes:, :] = marked


def key_marks(meta_all, table_full, length):
    blocks = meta_all.shape[0]
    heads = table_full.shape[0]
    bounds = tuple(
        1 + level * level * length // (bucket_steps * bucket_steps) for level in range(bucket_steps)
    )
    return pl.pallas_call(
        functools.partial(marks_kernel, bounds),
        in_specs=[in_vmem, in_smem],
        out_specs=[in_vmem] * 4,
        out_shape=[
            jax.ShapeDtypeStruct((blocks * lanes, lanes), bf16),
            jax.ShapeDtypeStruct((heads, blocks, 2 * lanes), f32),
            jax.ShapeDtypeStruct((blocks, 2 * lanes), jnp.int32),
            jax.ShapeDtypeStruct((2 * lanes, lanes), f32),
        ],
        compiler_params=pltpu.CompilerParams(vmem_limit_bytes=40 << 20),
        cost_estimate=free,
    )(meta_all, table_full)


def assemble_pair(first_ref, second_ref, first_own_ref, second_own_ref, parts, places):
    own, *others = [pl.multiple_of(place, 16) for place in places]
    first_ref[pl.ds(own, first_own_ref.shape[0]), :] = first_own_ref[...]
    second_ref[pl.ds(own, second_own_ref.shape[0]), :] = second_own_ref[...]
    width, hidden = first_ref.shape[1], second_ref.shape[1]
    span = (width + hidden) // 2
    for (part_ref, base), other in zip(parts, others, strict=True):
        quarter = part_ref.shape[0] // 2
        rows = pl.ds(other, quarter)
        first_ref[rows, :] = part_ref[:quarter, base : base + width]
        second_ref[rows, : span - width] = part_ref[:quarter, base + width : base + span]
        second_ref[rows, span - width :] = part_ref[quarter:, base : base + span]


def assemble(target_ref, own_ref, parts, columns, places):
    own, *others = [pl.multiple_of(place, 16) for place in places]
    target_ref[pl.ds(own, own_ref.shape[0]), :] = own_ref[...]
    for part_ref, other in zip(parts, others, strict=True):
        target_ref[pl.ds(other, part_ref.shape[0]), :] = part_ref[:, columns]


def forward_half_kernel(
    place_ref,
    attended_ref,
    content_ref,
    stream_ref,
    output_own_ref,
    inner_own_ref,
    got_ref,
    near_ref,
    rest_ref,
    far_ref,
    vector_ref,
    bias_ref,
    out_low_ref,
    normed_ref,
    rows_ref,
    scale_ref,
    normed_low_ref,
    active_ref,
    slope_ref,
    square_ref,
    weight_output_ref,
    weight_inner_ref,
):
    width = attended_ref.shape[1]
    hidden = inner_own_ref.shape[1]
    half = content_ref.shape[0]
    places = [place_ref[at] for at in range(1, 6)]
    base = 3 * width
    assemble_pair(
        weight_output_ref,
        weight_inner_ref,
        output_own_ref,
        inner_own_ref,
        ((got_ref, base), (near_ref, 0), (rest_ref, base), (far_ref, 0)),
        places,
    )
    out_low = attended_ref[...].astype(bf16)
    out_low_ref[...] = out_low
    attention_out = dot(out_low, weight_output_ref[...])
    streams = jnp.concatenate([content_ref[...], stream_ref[...]], axis=0).astype(f32)
    residual = streams + attention_out
    rows, scale = normalized(residual)
    normed = rows * vector_ref[2:3, :] + vector_ref[3:4, :]
    normed_low = normed.astype(bf16)
    rows_ref[...] = rows
    scale_ref[...] = jnp.broadcast_to(scale, scale_ref.shape)
    normed_ref[...] = normed
    normed_low_ref[...] = normed_low
    lane = lax.broadcasted_iota(jnp.int32, (1, width), 1)
    total = jnp.zeros((1, width), f32)
    for at, value in enumerate((streams, attention_out, residual)):
        part = value[:half]
        summed = jnp.sum(jnp.sum(part * part, axis=0, keepdims=True), axis=1, keepdims=True)
        total = total + jnp.where((lane == at) | (lane == at + width // 2), summed, 0.0)
    square_ref[...] = jnp.broadcast_to(total, square_ref.shape)
    step = 512

    @pl.loop(0, hidden // step)
    def _(at):
        span = pl.ds(pl.multiple_of(at * step, step), step)
        inner = dot(normed_low, weight_inner_ref[:, span]) + bias_ref[0:1, span]
        below = 0.5 + 0.5 * lax.erf(inner * 0.7071067811865476)
        density = 0.3989422804014327 * jnp.exp(-0.5 * inner * inner)
        active_ref[:, span] = (inner * below).astype(bf16)
        slope_ref[:, span] = below + inner * density


def backward_half_kernel(
    place_ref,
    active_ref,
    slope_ref,
    normed_ref,
    rows_ref,
    scale_ref,
    weight_output_ref,
    weight_inner_ref,
    outer_own_ref,
    got_ref,
    rest_ref,
    vector_ref,
    square_ref,
    content_cotangent_ref,
    query_cotangent_ref,
    content_result_ref,
    query_result_ref,
    residual_back_ref,
    out_back_ref,
    outer_kept_ref,
    outer_sent_ref,
    inner_kept_ref,
    inner_sent_ref,
    attention_kept_ref,
    attention_sent_ref,
    sums_ref,
    weight_outer_ref,
    inner_back_ref,
    held_ref,
    bias_back_ref,
):
    width = normed_ref.shape[1]
    hidden = active_ref.shape[1]
    count = content_cotangent_ref.shape[0]
    core = place_ref[6]
    assemble(
        weight_outer_ref,
        outer_own_ref,
        (got_ref, rest_ref),
        slice(0, width),
        [place_ref[at] for at in range(7, 10)],
    )

    def give(value_ref, kept_ref, sent_ref):
        columns = kept_ref.shape[1]
        kept_ref[...] = value_ref[:, pl.ds(pl.multiple_of(core * columns, lanes), columns)]
        sent_ref[...] = value_ref[:, pl.ds(pl.multiple_of((1 - core) * columns, lanes), columns)]

    outer = dot(active_ref[...], weight_outer_ref[...]) + vector_ref[4:5, :]
    final_rows, final_scale = normalized(normed_ref[...] + outer)
    result = (final_rows * vector_ref[5:6, :] + vector_ref[6:7, :]).astype(bf16)
    content_result_ref[...] = result[:count]
    query_result_ref[...] = result[count:]
    cotangent = jnp.concatenate(
        [content_cotangent_ref[...], query_cotangent_ref[...]], axis=0
    ).astype(f32)
    sums_ref[9:10, :] = jnp.sum(cotangent * final_rows, axis=0, keepdims=True)
    sums_ref[10:11, :] = jnp.sum(cotangent, axis=0, keepdims=True)
    back_second = norm_back(cotangent * vector_ref[5:6, :], final_rows, final_scale)
    outer_back = back_second.astype(bf16)
    sums_ref[8:9, :] = jnp.sum(outer_back.astype(f32), axis=0, keepdims=True)
    held_ref[...] = outer_back
    give(held_ref, outer_kept_ref, outer_sent_ref)
    residual_back_ref[...] = back_second
    step = 512

    @pl.loop(0, hidden // step)
    def _(at):
        span = pl.ds(pl.multiple_of(at * step, step), step)
        back = dot_nt(outer_back, weight_outer_ref[span, :]) * slope_ref[:, span]
        low = back.astype(bf16)
        inner_back_ref[:, span] = low
        bias_back_ref[0:1, span] = jnp.sum(low.astype(f32), axis=0, keepdims=True)
        residual_back_ref[...] += dot_nt(low, weight_inner_ref[:, span])

    give(inner_back_ref, inner_kept_ref, inner_sent_ref)
    normed_back = residual_back_ref[...]
    rows = rows_ref[...]
    sums_ref[6:7, :] = jnp.sum(normed_back * rows, axis=0, keepdims=True)
    sums_ref[7:8, :] = jnp.sum(normed_back, axis=0, keepdims=True)
    residual_back = norm_back(normed_back * vector_ref[2:3, :], rows, scale_ref[:, 0:1])
    residual_back_ref[...] = residual_back
    attention_back = residual_back.astype(bf16)
    held_ref[...] = attention_back
    give(held_ref, attention_kept_ref, attention_sent_ref)
    out_back_ref[...] = dot_nt(attention_back, weight_output_ref[...]).astype(bf16)
    part = width // 2
    for at in range(hidden // width):
        sums_ref[11 + at : 12 + at, :part] = bias_back_ref[0:1, at * part : (at + 1) * part]
        sums_ref[11 + at : 12 + at, part:] = bias_back_ref[
            0:1, hidden // 2 + at * part : hidden // 2 + (at + 1) * part
        ]
    last = 11 + hidden // width
    sums_ref[last : last + 1, :] = square_ref[0:1, :]
    sums_ref[0:6, :] = jnp.zeros((6, width), f32)


def forward_half(places, *operands):
    rows, width = operands[0].shape
    hidden = operands[4].shape[1]
    shapes = [
        jax.ShapeDtypeStruct((rows, width), bf16),
        jax.ShapeDtypeStruct((rows, width), f32),
        jax.ShapeDtypeStruct((rows, width), f32),
        jax.ShapeDtypeStruct((rows, lanes), f32),
        jax.ShapeDtypeStruct((rows, width), bf16),
        jax.ShapeDtypeStruct((rows, hidden), bf16),
        jax.ShapeDtypeStruct((rows, hidden), f32),
        jax.ShapeDtypeStruct((8, width), f32),
        jax.ShapeDtypeStruct((width, width), bf16),
        jax.ShapeDtypeStruct((width, hidden), bf16),
    ]
    return pl.pallas_call(
        forward_half_kernel,
        grid=(1,),
        in_specs=[in_smem] + [resident(value) for value in operands],
        out_specs=[resident(shape) for shape in shapes],
        out_shape=shapes,
        compiler_params=pltpu.CompilerParams(vmem_limit_bytes=60 << 20),
        cost_estimate=takes(8),
    )(places, *operands)


def backward_half(places, *operands):
    active, normed = operands[0], operands[2]
    rows, width = normed.shape
    hidden = active.shape[1]
    count = rows // 2
    shapes = (
        [jax.ShapeDtypeStruct((count, width), bf16)] * 2
        + [jax.ShapeDtypeStruct((rows, width), f32), jax.ShapeDtypeStruct((rows, width), bf16)]
        + [jax.ShapeDtypeStruct((rows, width // 2), bf16)] * 2
        + [jax.ShapeDtypeStruct((rows, hidden // 2), bf16)] * 2
        + [jax.ShapeDtypeStruct((rows, width // 2), bf16)] * 2
        + [jax.ShapeDtypeStruct((16, width), f32)]
    )
    return pl.pallas_call(
        backward_half_kernel,
        grid=(1,),
        in_specs=[in_smem] + [resident(value) for value in operands],
        out_specs=[resident(shape) for shape in shapes],
        out_shape=shapes,
        scratch_shapes=[
            pltpu.VMEM((hidden, width), bf16),
            pltpu.VMEM((rows, hidden), bf16),
            pltpu.VMEM((rows, width), bf16),
            pltpu.VMEM((8, hidden), f32),
        ],
        compiler_params=pltpu.CompilerParams(vmem_limit_bytes=60 << 20),
        cost_estimate=takes(12),
    )(places, *operands)


def body(
    content,
    query_stream,
    block_rank,
    segments,
    positions,
    query_weight,
    key_weight,
    value_weight,
    output_weight,
    content_bias,
    segment_bias,
    segment_embed,
    relative_table,
    attention_gain,
    attention_shift,
    inner_weight,
    inner_bias,
    outer_weight,
    outer_bias,
    final_gain,
    final_shift,
    content_cotangent,
    query_cotangent,
):
    block_rows = content.shape[1]
    width = content.shape[2]
    rows = 2 * block_rows
    count = lax.axis_size("ctx")
    sides = lax.axis_size("wsh")
    side = lax.axis_index("wsh")
    core = lax.axis_index("ctx") % 2
    length = block_rows * count
    own_content = content[0]
    own_query = query_stream[0]
    part = width // sides
    table_heads, bucket_count = relative_table.shape
    head_count = table_heads * sides
    inner_rows = inner_bias.shape[0] // part
    low = 2

    first_places = shard_places(query_weight.shape[0])
    hidden = inner_weight.shape[1]
    near = (lax.axis_index("ctx") // low) % 2
    shard_rows = query_weight.shape[0]
    half, quarter = shard_rows // 2, shard_rows // 4
    base, span = 3 * width, (width + hidden) // 2
    (first_sent,) = moved(
        tuple(
            (at, window("0", half, 0, width), 0, window(0, half, at * width, width))
            for at in range(3)
        )
        + (
            (3, window("1", quarter, 0, width), 0, window(0, quarter, base, width)),
            (
                4,
                window("1", quarter, 0, span - width),
                0,
                window(0, quarter, base + width, span - width),
            ),
            (4, window("1", quarter, span - width, span), 0, window(quarter, quarter, base, span)),
        ),
        [jax.ShapeDtypeStruct((half, base + span), bf16)],
        jnp.stack([core * half, (2 * core + near) * quarter]).astype(jnp.int32),
        query_weight,
        key_weight,
        value_weight,
        output_weight,
        inner_weight,
    )
    first_got = across(first_sent)
    mark_rows = 16
    marks = jnp.concatenate(
        [
            segments[0].astype(bf16),
            block_rank[0].astype(bf16),
            (positions[0, :1] // lanes).astype(bf16),
            (positions[0, :1] % lanes).astype(bf16),
        ]
    )
    marks = jnp.pad(marks[None], ((0, mark_rows - 1), (0, width - marks.shape[0])))
    block = jnp.concatenate([own_content, marks], axis=0)
    gathered = gather_blocks(block)
    small_height = 16
    small = jnp.zeros((small_height * part,), bf16)
    filled = 0
    for vector in (
        content_bias,
        segment_bias,
        attention_gain,
        attention_shift,
        outer_bias,
        final_gain,
        final_shift,
        segment_embed.reshape(-1),
        inner_bias,
        relative_table.reshape(-1),
    ):
        small = small + jnp.pad(vector, (filled, small.shape[0] - filled - vector.shape[0]))
        filled += vector.shape[0]
    small = small.reshape(small_height, part)
    small_other = across(small)
    first_rest = partner(first_got, 1)
    second_near = partner(first_got[:, base:], low)
    third_places = shard_places(outer_weight.shape[0])
    third_sent = half_rows(third_places, 1, outer_weight)
    third_got = across(third_sent)

    small_pair = jnp.where(
        side == 0,
        jnp.concatenate([small, small_other], axis=1),
        jnp.concatenate([small_other, small], axis=1),
    ).astype(f32)
    bias_content = small_pair[0:1]
    bias_segment = small_pair[1:2]
    embed = small_pair[7:9]
    bias_inner = jnp.concatenate(
        [
            small_pair[9 : 9 + inner_rows, :part].reshape(-1),
            small_pair[9 : 9 + inner_rows, part:].reshape(-1),
        ]
    )
    table_row = small_pair[9 + inner_rows]
    table_full = jnp.concatenate(
        [
            table_row[: table_heads * bucket_count],
            table_row[part : part + table_heads * bucket_count],
        ]
    ).reshape(head_count, bucket_count)

    held = block_rows + mark_rows
    if len(gathered) == 1:
        stacked = gathered[0].reshape(count, held, width)
        content_all = stacked[:, :block_rows].reshape(length, width)
        meta_all = stacked[:, block_rows:]
    else:
        plan = []
        place = 0
        for at, piece in enumerate(gathered):
            for row in range(0, piece.shape[0], held):
                plan.append(
                    (at, window(row, block_rows), 0, window(place * block_rows, block_rows))
                )
                plan.append(
                    (at, window(row + block_rows, mark_rows), 1, window(place * mark_rows, mark_rows))
                )
                place += 1
        content_all, meta_all = moved(
            tuple(plan),
            [
                jax.ShapeDtypeStruct((length, width), bf16),
                jax.ShapeDtypeStruct((count * mark_rows, width), bf16),
            ],
            first_places,
            *gathered,
        )
        meta_all = meta_all.reshape(count, mark_rows, width)
    pairs = width // lanes
    runs = [(0, 0, width, 0, 0)]
    for pair in range(pairs):
        runs.append((1, pair * lanes, lanes, 1, 2 * pair * lanes))
        runs.append((2, pair * lanes, lanes, 1, (2 * pair + 1) * lanes))
    weight_query, weight_both = whole_rows(
        first_places, runs, (width, 2 * width), first_got, first_rest, query_weight, key_weight, value_weight
    )
    key_code, table, number, row_code = key_marks(meta_all, table_full, length)

    streams = jnp.concatenate([own_content, own_query], axis=0)
    query_full = dot(streams, weight_query)
    both = dot(content_all, weight_both).astype(bf16)
    attended, log_row, stack = attention_forward(
        query_full, bias_content, bias_segment, embed, row_code, key_code, both, table
    )

    hidden = inner_weight.shape[1]
    second_near, third_got, attended = lax.optimization_barrier(
        (second_near, third_got, attended)
    )
    second_far = partner(second_near, 1)
    third_rest = partner(third_got, 1)
    half_places = jnp.concatenate(
        [
            quarter_places(query_weight.shape[0]),
            core[None].astype(jnp.int32),
            third_places[1:],
        ]
    )
    (
        out_low,
        normed,
        norm_rows,
        norm_scale,
        normed_low,
        active_low,
        slope,
        squares,
        weight_output,
        weight_inner,
    ) = forward_half(
        half_places,
        attended,
        own_content,
        own_query,
        output_weight,
        inner_weight,
        first_got,
        second_near,
        first_rest,
        second_far,
        small_pair,
        bias_inner[None],
    )
    out_low_other = partner(out_low, 1)
    normed_other = partner(normed_low, 1)
    active_other = partner(active_low, 1)
    (
        content_result,
        query_result,
        residual_back,
        out_back,
        outer_kept,
        outer_sent,
        inner_kept,
        inner_sent,
        attention_kept,
        attention_sent,
        vectors,
    ) = backward_half(
        half_places,
        active_low,
        slope,
        normed,
        norm_rows,
        norm_scale,
        weight_output,
        weight_inner,
        outer_weight,
        third_got,
        third_rest,
        small_pair,
        squares,
        content_cotangent[0],
        query_cotangent[0],
    )

    cuts, extra = split_bits(count)
    wide_cuts = [1] + cuts
    order_one = [0] + cuts
    order_two = cuts[:1] + [0] + cuts[1:]
    places_one = piece_places(order_one, cuts)
    places_two = piece_places(order_two, cuts)
    wide_places = by_core(
        piece_places([1, 0] + cuts, wide_cuts),
        piece_places([1, cuts[0], 0] + cuts[1:], wide_cuts),
        2 << len(cuts),
    )
    places_out = jnp.concatenate([piece_places(cuts, cuts), core[None].astype(jnp.int32)])
    wide_places_out = by_core(
        piece_places(wide_cuts, wide_cuts),
        piece_places([1] + cuts[1:] + cuts[:1], wide_cuts),
        1 << len(cuts),
    )

    outer_keep, outer_send = product_pieces(
        places_one, active_low, active_other, outer_kept, partner(outer_sent, 1)
    )
    outer_got = pass_on(outer_send, order_one[0])
    inner_keep, inner_send = product_pieces(
        places_two,
        normed_low,
        normed_other,
        inner_kept,
        partner(inner_sent, 1),
        out_low,
        out_low_other,
        attention_kept,
        partner(attention_sent, 1),
    )
    inner_got = pass_on(inner_send, order_two[0])

    line = cuts[1:]
    last = cuts[2]

    def add_extra(value):
        for bit in extra:
            value = fold_last(value, partner(value, bit))
        return value

    query_back, both_back, small_back = attention_backward(
        stack,
        query_full,
        bias_segment,
        embed,
        row_code,
        key_code,
        both,
        table,
        number,
        after(out_back, outer_send, inner_send),
        attended,
        log_row,
    )
    hidden_rows = hidden // part // sides
    order = Sequence(after(wide_places_out, small_back))
    outer_got, inner_got = order.wait(outer_got, inner_got)
    outer_keep, outer_send = fold(outer_keep, outer_got)
    outer_send = order.ready(outer_send)
    outer_got = partner(outer_send, cuts[0])
    inner_keep, inner_send = fold(inner_keep, inner_got)
    inner_send = order.ready(inner_send)
    inner_got = across(inner_send)
    content_share = order.ready(share_of_content(order.ready(both_back), weight_both))
    tail_keep, tail_send = cut_gradient(
        wide_places,
        vectors,
        small_back,
        dot_tn(streams, query_back),
        dot_tn(content_all, order.ready(both_back)),
    )
    tail_keep = order.ready(tail_keep)
    outer_got = order.wait(outer_got)
    inner_got = order.wait(inner_got)
    tail_send = order.ready(tail_send)
    tail_got = partner(tail_send, 1)
    outer_keep, outer_send = fold(outer_keep, outer_got)
    outer_send = order.ready(outer_send)
    outer_got = partner(outer_send, line[0])
    inner_keep, inner_send = fold(inner_keep, inner_got)
    inner_send = order.ready(inner_send)
    inner_got = partner(inner_send, line[0])
    share_keep, share_send = content_share[: count // 2], order.ready(content_share[count // 2 :])
    share_got = partner(share_send, 1)
    tail_got = order.wait(tail_got)
    tail_keep, tail_send = fold(tail_keep, tail_got)
    tail_send = order.ready(tail_send)
    tail_got = pass_mixed(tail_send, 0, cuts[0])
    share_got = order.wait(share_got)
    share_keep, share_send = fold(share_keep, share_got)
    share_send = order.ready(share_send)
    share_got = partner(share_send, cuts[0])
    outer_got = order.wait(outer_got)
    outer_keep, outer_send = fold(outer_keep, outer_got)
    outer_send = order.ready(outer_send)
    outer_got = partner(outer_send, last)
    inner_got = order.wait(inner_got)
    inner_keep, inner_send = fold(inner_keep, inner_got)
    inner_send = order.ready(inner_send)
    inner_got = partner(inner_send, last)
    tail_got = order.wait(tail_got)
    tail_keep, tail_send = fold(tail_keep, tail_got)
    tail_send = order.ready(tail_send)
    tail_got = pass_mixed(tail_send, cuts[0], 0)
    outer_got = order.wait(outer_got)
    outer_value = order.ready(add_extra(fold_last(outer_keep, outer_got)))
    outer_got = partner(outer_value, last)
    inner_got = order.wait(inner_got)
    inner_value = order.ready(add_extra(fold_last(inner_keep, inner_got)))
    inner_got = partner(inner_value, last)
    tail_got = order.wait(tail_got)
    tail_keep, tail_send = fold(tail_keep, tail_got)
    tail_send = order.ready(tail_send)
    tail_got = partner(tail_send, line[0])
    share_got = order.wait(share_got)
    share_keep, share_send = fold(share_keep, share_got)
    share_send = order.ready(share_send)
    share_got = partner(share_send, line[0])
    outer_got = order.wait(outer_got)
    outer_value = order.ready(piled(outer_value, outer_got))
    outer_got = partner(outer_value, line[0])
    inner_got = order.wait(inner_got)
    inner_value = order.ready(piled(inner_value, inner_got))
    inner_got = partner(inner_value, line[0])
    tail_got = order.wait(tail_got)
    tail_keep, tail_send = fold(tail_keep, tail_got)
    tail_send = order.ready(tail_send)
    tail_got = partner(tail_send, last)
    outer_got = order.wait(outer_got)
    outer_value = order.ready(piled(outer_value, outer_got))
    outer_got = partner(outer_value, cuts[0])
    share_got = order.wait(share_got)
    share_keep, share_send = fold(share_keep, share_got)
    share_send = order.ready(share_send)
    share_got = partner(share_send, last)
    streams_back = residual_back + dot_nt(order.ready(query_back), weight_query)
    tail_got = order.wait(tail_got)
    tail_value = order.ready(add_extra(fold_last(tail_keep, tail_got)))
    tail_got = pass_mixed(tail_value, last, cuts[0])
    inner_got = order.wait(inner_got)
    inner_value = order.ready(piled(inner_value, inner_got))
    inner_got = partner(inner_value, cuts[0])
    tail_got = order.wait(tail_got)
    tail_value = order.ready(piled(tail_value, tail_got))
    tail_got = pass_mixed(tail_value, line[0], last)
    outer_got = order.wait(outer_got)
    outer_value = order.ready(piled(outer_value, outer_got))
    outer_got = partner(outer_value, 1)
    share_got = order.wait(share_got)
    for bit in extra:
        share_keep, share_send = fold(share_keep, share_got)
        share_got = partner(share_send, bit)
    content_back = streams_back[:block_rows] + share_keep[0].astype(f32) + share_got[0].astype(f32)
    content_back = order.ready(content_back)
    tail_got = order.wait(tail_got)
    tail_value = order.ready(piled(tail_value, tail_got))
    tail_got = pass_mixed(tail_value, cuts[0], line[0])
    inner_got = order.wait(inner_got)
    inner_value = order.ready(piled(inner_value, inner_got))
    inner_got = partner(inner_value, 1)
    outer_got = order.wait(outer_got)
    (outer_weight_sum,) = lay_out(
        places_out,
        (((0, 0, width // 2, -1), (1, 0, width // 2, -2)),),
        outer_value,
        outer_got,
    )
    outer_weight_sum = order.ready(outer_weight_sum)
    tail_got = order.wait(tail_got)
    tail_value = order.ready(piled(tail_value, tail_got))
    tail_got = partner(tail_value, 1)
    inner_got = order.wait(inner_got)
    inner_weight_sum, output_weight_sum = lay_out(
        places_out,
        (
            ((0, 0, hidden // 2, -1), (1, 0, hidden // 2, -2)),
            ((0, hidden // 2, width // 2, -1), (1, hidden // 2, width // 2, -2)),
        ),
        inner_value,
        inner_got,
    )
    inner_weight_sum, output_weight_sum = order.ready(inner_weight_sum, output_weight_sum)
    tail_got = order.wait(tail_got)
    plan = []
    for kind in range(3):
        row = []
        for pair in range(pairs):
            taken = pair * lanes if kind == 0 else width + (2 * pair + kind - 1) * lanes
            row.append((0, taken, lanes, pair * lanes))
        plan.append(tuple(row))
    plan.append(((0, 3 * width, lanes, 0),))
    query_weight_sum, key_weight_sum, value_weight_sum, vector_sums = lay_out(
        order.mark, tuple(plan), tail_value, tail_got
    )
    sums = vector_sums[:, :16].T
    table_sum = jnp.swapaxes(sums[4:6].reshape(2, -1, lanes)[:, :, :bucket_count], 0, 1).reshape(
        table_heads, bucket_count
    )
    inner_bias_sum = sums[11 : 11 + hidden_rows].reshape(-1)
    token_total = length * sides * width
    root_mean = jnp.sqrt(sums[11 + hidden_rows, :3] / token_total)
    return (
        content_result[None],
        query_result[None],
        content_back[None],
        streams_back[block_rows:][None],
        query_weight_sum,
        key_weight_sum,
        value_weight_sum,
        output_weight_sum,
        sums[0],
        sums[1],
        sums[2:4],
        table_sum,
        sums[6],
        sums[7],
        inner_weight_sum,
        inner_bias_sum,
        outer_weight_sum,
        sums[8],
        sums[9],
        sums[10],
        root_mean,
    )


def solution(mesh):
    tokens = P("wsh", "ctx", None)
    marks = P("wsh", "ctx")
    matrix = P("wsh", None)
    vector = P("wsh")
    placed = (
        (tokens, tokens, marks, marks, marks)
        + (matrix,) * 4
        + (vector, vector, P(None, "wsh"), matrix, vector, vector, matrix, vector, matrix)
        + (vector,) * 3
        + (tokens, tokens)
    )
    given = (
        (tokens,) * 4
        + (matrix,) * 4
        + (vector, vector, P(None, "wsh"), matrix, vector, vector, matrix, vector, matrix)
        + (vector,) * 3
        + (P(),)
    )
    return jax.shard_map(body, mesh=mesh, in_specs=placed, out_specs=given, check_vma=False)
```

```python
import functools

import jax
import jax.numpy as jnp
from jax import lax
from jax.experimental import pallas as pl
from jax.experimental.pallas import tpu as pltpu
from jax.sharding import PartitionSpec as P

negative = -1e30
epsilon = 1e-05
bucket_steps = 16
key_tile = 256
lanes = 128
highest = lax.Precision.HIGHEST
f32 = jnp.float32
bf16 = jnp.bfloat16


free = pl.CostEstimate(flops=0, bytes_accessed=0, transcendentals=0)
in_vmem = pl.BlockSpec(memory_space=pltpu.VMEM)
in_smem = pl.BlockSpec(memory_space=pltpu.SMEM)


def resident(value):
    rank = len(value.shape)
    return pl.BlockSpec(value.shape, lambda at: (0,) * rank, pipeline_mode=pl.Buffered(1))


def takes(microseconds):
    return pl.CostEstimate(
        flops=microseconds * 1_000_000_000, bytes_accessed=0, transcendentals=0
    )


def normalized(values):
    centred = values - jnp.mean(values, axis=-1, keepdims=True)
    spread = jnp.mean(centred * centred, axis=-1, keepdims=True)
    scale = lax.rsqrt(spread + epsilon)
    return centred * scale, scale


def norm_back(cotangent, rows, scale):
    mean = jnp.mean(cotangent, axis=-1, keepdims=True)
    along = jnp.mean(cotangent * rows, axis=-1, keepdims=True)
    return scale * (cotangent - mean - rows * along)


def dot(left, right):
    return jnp.dot(left, right, preferred_element_type=f32)


def dot_nt(left, right):
    return lax.dot_general(left, right, (((1,), (1,)), ((), ())), preferred_element_type=f32)


def dot_tn(left, right):
    return lax.dot_general(left, right, (((0,), (0,)), ((), ())), preferred_element_type=f32)


def partner(value, bit):
    count = lax.axis_size("ctx")
    return lax.ppermute(value, "ctx", [(place, place ^ bit) for place in range(count)])


def across(value):
    return lax.ppermute(value, "wsh", [(0, 1), (1, 0)])


def bits_of(count):
    result = []
    bit = 1
    while bit < count:
        result.append(bit)
        bit *= 2
    return result


def block_order(count):
    order = [0]
    for bit in reversed(bits_of(count)):
        order = order + [place | bit for place in order]
    return order


def gather_blocks(own):
    count = lax.axis_size("ctx")
    bits = bits_of(count)
    if count != 16:
        held = own
        for bit in reversed(bits):
            held = jnp.concatenate([held, partner(held, bit)], axis=0)
        return [held]
    low = bits[1]
    near = partner(own, low)
    first = [own] + [partner(own, place) for place in (bits[3], bits[2], bits[2] | bits[3])]
    second = [near] + [partner(block, low) for block in first[1:]]
    others = partner(jnp.concatenate(first + second, axis=0), 1)
    return first + second + [others]


def move_kernel(plan, inputs, place_ref, *refs):
    sources, targets = refs[:inputs], refs[inputs:]
    for source, taken, target, put in plan:
        targets[target][put(place_ref)] = sources[source][taken(place_ref)]


def moved(plan, shapes, places, *sources):
    return pl.pallas_call(
        functools.partial(move_kernel, plan, len(sources)),
        grid=(1,),
        in_specs=[in_smem] + [resident(value) for value in sources],
        out_specs=[resident(shape) for shape in shapes],
        out_shape=shapes,
        compiler_params=pltpu.CompilerParams(vmem_limit_bytes=40 << 20),
        cost_estimate=free,
    )(places, *sources)


def window(start, rows, left=None, columns=None):
    def make(place_ref):
        first = start
        if isinstance(start, str):
            first = pl.multiple_of(place_ref[int(start)], 16)
        if left is None:
            return (pl.ds(first, rows), slice(None))
        return (pl.ds(first, rows), pl.ds(left, columns))

    return make


def half_rows(places, cut, *shards):
    rows = shards[0].shape[0] // 2 // cut
    plan = []
    left = 0
    for at, shard in enumerate(shards):
        columns = shard.shape[1]
        plan.append((at, window("0", rows, 0, columns), 0, window(0, rows, left, columns)))
        left += columns
    return moved(tuple(plan), [jax.ShapeDtypeStruct((rows, left), bf16)], places, *shards)[0]


def whole_rows(places, runs, widths, got, rest, *shards):
    rows = shards[0].shape[0]
    half = rows // 2
    lefts = [0]
    for shard in shards:
        lefts.append(lefts[-1] + shard.shape[1])
    plan = []
    for shard, first, columns, target, column in runs:
        plan.append(
            (2 + shard, window(0, rows, first, columns), target, window("1", rows, column, columns))
        )
        for source, place in ((0, "2"), (1, "3")):
            plan.append(
                (
                    source,
                    window(0, half, lefts[shard] + first, columns),
                    target,
                    window(place, half, column, columns),
                )
            )
    shapes = [jax.ShapeDtypeStruct((2 * rows, width), bf16) for width in widths]
    return moved(tuple(plan), shapes, places, got, rest, *shards)


def quarter_places(rows):
    core = lax.axis_index("ctx") % 2
    near = (lax.axis_index("ctx") // 2) % 2
    side = lax.axis_index("wsh")
    quarter = rows // 4
    base = (1 - side) * rows
    spots = [(core, near), (core, 1 - near), (1 - core, near), (1 - core, 1 - near)]
    return jnp.stack(
        [(2 * core + near) * quarter, side * rows]
        + [base + (2 * first + second) * quarter for first, second in spots]
    ).astype(jnp.int32)


def shard_places(rows):
    core = lax.axis_index("ctx") % 2
    side = lax.axis_index("wsh")
    half = rows // 2
    base = (1 - side) * rows
    return jnp.stack(
        [core * half, side * rows, base + core * half, base + (1 - core) * half]
    ).astype(jnp.int32)


def split_bits(count):
    bits = bits_of(count)
    return bits[1:4], bits[4:]


def own_bit(bit):
    if bit == 0:
        return lax.axis_index("wsh")
    return (lax.axis_index("ctx") // bit) % 2


def pass_on(value, bit):
    return across(value) if bit == 0 else partner(value, bit)


def pass_mixed(value, even_bit, odd_bit):
    count = lax.axis_size("ctx")
    pairs = []
    for place in range(count):
        bit = odd_bit if place % 2 else even_bit
        for side in range(2):
            other = (place, 1 - side) if bit == 0 else (place ^ bit, side)
            pairs.append((2 * place + side, 2 * other[0] + other[1]))
    return lax.ppermute(value, ("ctx", "wsh"), pairs)


def by_core(even, odd, half):
    core = lax.axis_index("ctx") % 2
    return jnp.where(
        core == 0,
        jnp.concatenate([even[:half], odd[half:]]),
        jnp.concatenate([odd[:half], even[half:]]),
    )


class Sequence:
    def __init__(self, mark):
        self.mark = mark

    def wait(self, *values):
        *values, self.mark = lax.optimization_barrier(tuple(values) + (self.mark,))
        return values[0] if len(values) == 1 else tuple(values)

    ready = wait


def piece_places(order, cuts):
    total = len(order)
    place = jnp.arange(1 << total, dtype=jnp.int32)
    result = jnp.zeros_like(place)
    for at, bit in enumerate(order):
        value = ((place >> (total - 1 - at)) & 1) ^ own_bit(bit)
        weight = 1 << len(cuts) if bit == 0 else 1 << (len(cuts) - 1 - cuts.index(bit))
        result = result + value * weight
    return result


def fold_kernel(keep_ref, received_ref, *target_refs):
    first = 0
    for target_ref in target_refs:

        @pl.loop(0, target_ref.shape[0])
        def _(place, first=first, target_ref=target_ref):
            target_ref[place] = (
                keep_ref[first + place].astype(f32) + received_ref[first + place].astype(f32)
            ).astype(bf16)

        first += target_ref.shape[0]


def fold_parts(keep, received, parts):
    piece = jax.ShapeDtypeStruct((keep.shape[0] // parts,) + keep.shape[1:], bf16)
    return pl.pallas_call(
        fold_kernel,
        grid=(1,),
        in_specs=[resident(keep)] * 2,
        out_specs=[resident(piece)] * parts,
        out_shape=[piece] * parts,
        compiler_params=pltpu.CompilerParams(vmem_limit_bytes=40 << 20),
        cost_estimate=free,
    )(keep, received)


def fold(keep, received):
    return fold_parts(keep, received, 2)


def fold_last(keep, received):
    return fold_parts(keep, received, 1)[0]


def pile_kernel(*refs):
    target_ref = refs[-1]
    first = 0
    for source_ref in refs[:-1]:

        @pl.loop(0, source_ref.shape[0])
        def _(place, first=first, source_ref=source_ref):
            target_ref[first + place] = source_ref[place]

        first += source_ref.shape[0]


def piled(*values):
    height = sum(value.shape[0] for value in values)
    return pl.pallas_call(
        pile_kernel,
        in_specs=[in_vmem] * len(values),
        out_specs=in_vmem,
        out_shape=jax.ShapeDtypeStruct((height,) + values[0].shape[1:], values[0].dtype),
        compiler_params=pltpu.CompilerParams(vmem_limit_bytes=40 << 20),
        cost_estimate=free,
    )(*values)


def share_kernel(back_ref, weight_ref, out_ref):
    out_ref[...] = dot_nt(back_ref[...], weight_ref[...]).astype(bf16).reshape(out_ref.shape)


def share_of_content(both_back, weight_both):
    count, columns = both_back.shape
    width = weight_both.shape[0]
    step = 2 * lanes
    return pl.pallas_call(
        share_kernel,
        grid=(count // step,),
        in_specs=[
            pl.BlockSpec((step, columns), lambda at: (at, 0)),
            pl.BlockSpec((width, columns), lambda at: (0, 0), pipeline_mode=pl.Buffered(1)),
        ],
        out_specs=pl.BlockSpec((2, lanes, width), lambda at: (at, 0, 0)),
        out_shape=jax.ShapeDtypeStruct((count // lanes, lanes, width), bf16),
        compiler_params=pltpu.CompilerParams(vmem_limit_bytes=40 << 20),
        cost_estimate=free,
    )(both_back, weight_both)


def after(value, *others):
    return lax.optimization_barrier((value,) + others)[0]


def product_kernel(groups, place_ref, *refs):
    operands, (keep_ref, send_ref, total_ref) = refs[: 4 * groups], refs[4 * groups :]
    rows = keep_ref.shape[1]
    step = 256
    left = 0
    for group in range(groups):
        left_own, left_other, right_own, right_other = operands[4 * group : 4 * group + 4]
        columns = right_own.shape[1]
        for start in range(0, left_own.shape[1], step):
            total_ref[start : start + step, left : left + columns] = dot_tn(
                left_own[:, start : start + step], right_own[...]
            ) + dot_tn(left_other[:, start : start + step], right_other[...])
        left += columns
    for at, ref in enumerate((keep_ref, send_ref)):

        @pl.loop(0, ref.shape[0])
        def _(place, at=at, ref=ref):
            block = place_ref[at * ref.shape[0] + place]
            start = pl.multiple_of(block * rows, 8)
            ref[place] = total_ref[pl.ds(start, rows), :].astype(bf16)


def product_pieces(places, *operands):
    groups = len(operands) // 4
    half = places.shape[0] // 2
    height = operands[0].shape[1]
    columns = sum(operands[4 * group + 2].shape[1] for group in range(groups))
    piece = jax.ShapeDtypeStruct((half, height // (2 * half), columns), bf16)
    return pl.pallas_call(
        functools.partial(product_kernel, groups),
        grid=(1,),
        in_specs=[in_smem] + [resident(value) for value in operands],
        out_specs=[resident(piece)] * 2,
        out_shape=[piece, piece],
        scratch_shapes=[pltpu.VMEM((height, columns), f32)],
        compiler_params=pltpu.CompilerParams(vmem_limit_bytes=60 << 20),
        cost_estimate=takes(4),
    )(places, *operands)


def cut_kernel(place_ref, vector_ref, small_ref, *refs):
    parts, (keep_ref, send_ref, turned_ref) = refs[:-3], refs[-3:]
    rows = keep_ref.shape[1]
    height = vector_ref.shape[1]
    filled = jnp.concatenate(
        [
            small_ref[...] + vector_ref[0:8, :],
            vector_ref[8:, :],
            jnp.zeros((lanes - vector_ref.shape[0], height), f32),
        ],
        axis=0,
    )
    for start in range(0, height, lanes):
        turned_ref[start : start + lanes, :] = filled[:, start : start + lanes].T
    parts = parts + (turned_ref,)
    for at, ref in enumerate((keep_ref, send_ref)):

        @pl.loop(0, ref.shape[0])
        def _(place, at=at, ref=ref):
            block = place_ref[at * ref.shape[0] + place]
            start = pl.multiple_of(block * rows, 8)
            left = 0
            for part in parts:
                columns = part.shape[1]
                ref[place, :, left : left + columns] = part[pl.ds(start, rows), :].astype(bf16)
                left += columns


def cut_gradient(places, vectors, small, *parts):
    half = places.shape[0] // 2
    height = parts[0].shape[0]
    columns = sum(part.shape[1] for part in parts) + lanes
    piece = jax.ShapeDtypeStruct((half, height // (2 * half), columns), bf16)
    return pl.pallas_call(
        cut_kernel,
        grid=(1,),
        in_specs=[in_smem] + [resident(value) for value in (vectors, small) + parts],
        out_specs=[resident(piece)] * 2,
        out_shape=[piece, piece],
        scratch_shapes=[pltpu.VMEM((height, lanes), f32)],
        compiler_params=pltpu.CompilerParams(vmem_limit_bytes=40 << 20),
        cost_estimate=free,
    )(places, vectors, small, *parts)


def lay_out_kernel(plan, place_ref, *refs):
    outputs = len(plan)
    sources, targets = refs[:-outputs], refs[-outputs:]
    halves = 2 if place_ref.shape[0] > sources[0].shape[0] + 1 else 1
    for half in range(halves):
      for runs, target in zip(plan, targets, strict=True):
        for source, first, columns, column in runs:
            piece_ref = sources[source + half]
            count, rows = piece_ref.shape[:2]

            @pl.loop(0, count)
            def _(place, piece_ref=piece_ref, rows=rows, target=target, first=first, columns=columns, column=column, half=half):
                start = pl.multiple_of(place_ref[half * count + place] * rows, 8)
                value = piece_ref[place, :, first : first + columns].astype(f32)
                if column >= 0:
                    target[pl.ds(start, rows), column : column + columns] = value
                else:
                    core = place_ref[count]
                    which = core if column == -1 else 1 - core
                    left = pl.multiple_of(which * columns, lanes)
                    target[pl.ds(start, rows), pl.ds(left, columns)] = value


def lay_out(places, plan, *pieces):
    shapes = []
    halves = 2 if places.shape[0] > pieces[0].shape[0] + 1 else 1
    for runs in plan:
        count, rows = pieces[runs[0][0]].shape[:2]
        shapes.append(jax.ShapeDtypeStruct((halves * count * rows, sum(run[2] for run in runs)), f32))
    return pl.pallas_call(
        functools.partial(lay_out_kernel, plan),
        grid=(1,),
        in_specs=[in_smem] + [resident(value) for value in pieces],
        out_specs=[resident(shape) for shape in shapes],
        out_shape=shapes,
        compiler_params=pltpu.CompilerParams(vmem_limit_bytes=40 << 20),
        cost_estimate=takes(3),
    )(places, *pieces)


def stream_bias(table_ref, head, block):
    spread = jnp.broadcast_to(table_ref[head, pl.ds(block, 1), :], (lanes, 2 * lanes))
    return pltpu.roll(spread, 0, 1, stride=1, stride_axis=0)[:, :lanes]


def tile_bias(table_ref, block):
    parts = []
    for piece in range(key_tile // lanes):
        first = stream_bias(table_ref, 0, block + piece)
        second = stream_bias(table_ref, 1, block + piece)
        parts.append(jnp.concatenate([first, first, second, second], axis=1))
    return jnp.concatenate(parts, axis=0)


def own_mask():
    row = lax.broadcasted_iota(jnp.int32, (key_tile, 4 * lanes), 0)
    column = lax.broadcasted_iota(jnp.int32, (key_tile, 4 * lanes), 1)
    stream = (column // lanes) % 2
    return jnp.where((stream == 1) & (row == column % lanes), negative, 0.0)


def forward_kernel(
    query_ref,
    content_bias_ref,
    segment_bias_ref,
    embed_ref,
    row_code_ref,
    key_code_ref,
    both_ref,
    table_ref,
    out_ref,
    log_ref,
    stack_ref,
    score_ref,
):
    rows = query_ref.shape[0]
    tiles = both_ref.shape[0] // key_tile
    lane = lax.broadcasted_iota(jnp.int32, (rows, lanes), 1)
    first = lane < lanes // 2
    query = query_ref[...]
    low = (query + content_bias_ref[...]).astype(bf16).astype(f32) * 0.125
    shifted = query + segment_bias_ref[...]
    zero_term = shifted * embed_ref[0:1, :]
    one_term = shifted * embed_ref[1:2, :]
    code = row_code_ref[...]
    for head in range(2):
        own = first if head == 0 else jnp.logical_not(first)
        zero_sum = jnp.sum(jnp.where(own, zero_term, 0.0), axis=1, keepdims=True) * 0.125
        one_sum = jnp.sum(jnp.where(own, one_term, 0.0), axis=1, keepdims=True) * 0.125
        step = zero_sum - one_sum
        step_high = step.astype(bf16).astype(f32)
        step_low = step - step_high
        one_high = one_sum.astype(bf16).astype(f32)
        one_low = one_sum - one_high
        extra = jnp.where(
            lane < 4,
            step_high,
            jnp.where(lane < 8, step_low, jnp.where(lane == 8, one_high, one_low)),
        )
        stack_ref[0, pl.ds(head * rows, rows), 0:lanes] = jnp.where(own, low, 0.0).astype(bf16)
        stack_ref[0, pl.ds(head * rows, rows), lanes : 2 * lanes] = (extra * code).astype(bf16)
    stack = stack_ref[0]

    def scores(tile, top):
        start = pl.multiple_of(tile * key_tile, key_tile)
        keys = jnp.concatenate(
            [both_ref[pl.ds(start, key_tile), :lanes], key_code_ref[pl.ds(start, key_tile), :]], axis=1
        )
        score = dot_nt(keys, stack) + tile_bias(table_ref, tile * (key_tile // lanes))
        if isinstance(tile, int) and tile == 0:
            score = score + own_mask()
        score_ref[pl.ds(start, key_tile), :] = score
        return jnp.maximum(top, jnp.max(score.reshape(key_tile // 8, 8, 4 * lanes), axis=0))

    top = jnp.full((8, 4 * lanes), negative, f32)
    top = scores(0, top)
    top = lax.fori_loop(1, tiles, scores, top, unroll=min(7, tiles - 1))
    peak = jnp.max(top, axis=0, keepdims=True)

    def gathered(tile, running):
        total, mixed = running
        start = pl.multiple_of(tile * key_tile, key_tile)
        weight = jnp.exp(score_ref[pl.ds(start, key_tile), :] - peak)
        total = total + jnp.sum(weight.reshape(key_tile // 8, 8, 4 * lanes), axis=0)
        mixed = mixed + dot_tn(both_ref[pl.ds(start, key_tile), lanes:], weight.astype(bf16))
        return total, mixed

    total, mixed = lax.fori_loop(
        0,
        tiles,
        gathered,
        (jnp.zeros((8, 4 * lanes), f32), jnp.zeros((lanes, 4 * lanes), f32)),
        unroll=min(8, tiles),
    )
    total = jnp.sum(total, axis=0, keepdims=True)
    mixed = mixed / total
    half = lanes // 2
    joined = jnp.concatenate([mixed[:half, :rows], mixed[half:, rows:]], axis=0)
    out_ref[...] = joined.T
    log_ref[0] = peak + jnp.log(total)


def diagonal_sums(square):
    lane = lax.broadcasted_iota(jnp.int32, (8, lanes), 1)
    near = square[0:8]
    far = jnp.zeros((8, lanes), f32)
    for group in range(1, lanes // 8):
        turned = pltpu.roll(square[8 * group : 8 * group + 8], lanes - 8 * group, 1)
        inside = lane < lanes - 8 * group
        near = near + jnp.where(inside, turned, 0.0)
        far = far + jnp.where(inside, 0.0, turned)
    both = jnp.concatenate([near, far], axis=1)
    row = lax.broadcasted_iota(jnp.int32, (8, 2 * lanes), 0)
    for bit in (1, 2, 4):
        both = jnp.where((row // bit) % 2 == 1, pltpu.roll(both, 2 * lanes - bit, 1), both)
    return jnp.sum(both, axis=0, keepdims=True)


def backward_kernel(
    stack_ref,
    query_ref,
    segment_bias_ref,
    embed_ref,
    row_code_ref,
    key_code_ref,
    both_ref,
    table_ref,
    number_ref,
    out_back_ref,
    attended_ref,
    log_ref,
    query_back_ref,
    both_back_ref,
    small_ref,
    diagonal_ref,
):
    rows = query_ref.shape[0]
    tiles = both_ref.shape[0] // key_tile
    half = lanes // 2
    lane = lax.broadcasted_iota(jnp.int32, (rows, lanes), 1)
    first = lane < half
    out_back = out_back_ref[...]
    product = (out_back.astype(f32) * attended_ref[...]).T
    delta = jnp.concatenate(
        [
            jnp.sum(product[:half], axis=0, keepdims=True),
            jnp.sum(product[half:], axis=0, keepdims=True),
        ],
        axis=1,
    )
    zeros = jnp.zeros_like(out_back)
    back_stack = jnp.concatenate(
        [jnp.where(first, out_back, zeros), jnp.where(first, zeros, out_back)], axis=0
    )
    stack = stack_ref[0]
    query_stack = stack[:, :lanes]
    log_row = log_ref[0]

    def step(tile, running):
        start = pl.multiple_of(tile * key_tile, key_tile)
        block = tile * (key_tile // lanes)
        keys = jnp.concatenate(
            [both_ref[pl.ds(start, key_tile), :lanes], key_code_ref[pl.ds(start, key_tile), :]], axis=1
        )
        score = dot_nt(keys, stack) + tile_bias(table_ref, block)
        if isinstance(tile, int) and tile == 0:
            score = score + own_mask()
        weight = jnp.exp(score - log_row)
        weight_back = dot_nt(both_ref[pl.ds(start, key_tile), lanes:], back_stack)
        score_back = weight * (weight_back - delta)
        score_low = score_back.astype(bf16)
        both_back_ref[pl.ds(start, key_tile), lanes:] = dot(
            weight.astype(bf16), back_stack
        ).astype(bf16)
        both_back_ref[pl.ds(start, key_tile), :lanes] = dot(score_low, query_stack).astype(bf16)
        for head in range(2):
            for piece in range(key_tile // lanes):
                part = score_back[
                    piece * lanes : (piece + 1) * lanes, head * rows : (head + 1) * rows
                ]
                square = part[:, :lanes] + part[:, lanes:]
                diagonal_ref[head, block + piece] = diagonal_sums(square)[0]
        return running + dot_tn(keys, score_low)

    diagonal_ref[2:] = jnp.zeros(diagonal_ref[2:].shape, f32)
    running = step(0, jnp.zeros((2 * lanes, 2 * rows), f32))
    running = lax.fori_loop(1, tiles, step, running, unroll=min(7, tiles - 1))
    joined = jnp.concatenate([running[:half, :rows], running[half:lanes, rows:]], axis=0).T * 0.125
    shifted = query_ref[...] + segment_bias_ref[...]
    code = row_code_ref[...]
    zero_columns = []
    one_columns = []
    for head in range(2):
        part = running[lanes:, head * rows : (head + 1) * rows].T * 0.125
        same = jnp.sum(jnp.where(lane < 4, part * code, 0.0), axis=1, keepdims=True)
        total = jnp.sum(jnp.where(lane == 8, part, 0.0), axis=1, keepdims=True)
        zero_columns.append(same)
        one_columns.append(total - same)
    zero_back = jnp.where(first, zero_columns[0], zero_columns[1])
    one_back = jnp.where(first, one_columns[0], one_columns[1])
    shift_back = zero_back * embed_ref[0:1, :] + one_back * embed_ref[1:2, :]
    query_back_ref[...] = (joined + shift_back).astype(bf16)
    small_ref[0:1, :] = jnp.sum(joined, axis=0, keepdims=True)
    small_ref[1:2, :] = jnp.sum(shift_back, axis=0, keepdims=True)
    small_ref[2:3, :] = jnp.sum(zero_back * shifted, axis=0, keepdims=True)
    small_ref[3:4, :] = jnp.sum(one_back * shifted, axis=0, keepdims=True)
    blocks = number_ref.shape[0]
    bucket = lax.broadcasted_iota(jnp.int32, (lanes, 2 * lanes), 0)
    table_back = jnp.zeros((8, lanes), f32)
    for block in range(blocks):
        chosen = jnp.where(bucket == number_ref[block : block + 1, :], 1.0, 0.0).astype(bf16)
        sums = diagonal_ref[:, block, :]
        for _ in range(3):
            part = sums.astype(bf16)
            table_back = table_back + dot_nt(part, chosen)
            sums = sums - part.astype(f32)
    small_ref[4:8, :] = table_back[:4]


def attention_specs(rows, keys, blocks, first_pair=0):
    column = lambda pair: (0, pair + first_pair)
    fixed = lambda pair: (0, 0)
    front = lambda pair: (pair + first_pair, 0, 0)
    return {
        "rows": pl.BlockSpec((rows, lanes), column),
        "row": pl.BlockSpec((1, lanes), column),
        "embed": pl.BlockSpec((2, lanes), column),
        "small": pl.BlockSpec((8, lanes), column),
        "row_code": pl.BlockSpec((rows, lanes), fixed),
        "key_code": pl.BlockSpec((keys, lanes), fixed, pipeline_mode=pl.Buffered(1)),
        "both": pl.BlockSpec((keys, 2 * lanes), column),
        "table": pl.BlockSpec((2, blocks, 2 * lanes), front),
        "log": pl.BlockSpec((1, 1, 2 * rows), front),
        "stack": pl.BlockSpec((1, 2 * rows, 2 * lanes), front),
    }


def attention_forward(query_full, bias_content, bias_segment, embed, row_code, key_code, both, table):
    rows, width = query_full.shape
    count = both.shape[0]
    pairs = width // lanes
    spec = attention_specs(rows, count, count // lanes)
    return pl.pallas_call(
        forward_kernel,
        grid=(pairs,),
        in_specs=[
            spec["rows"],
            spec["row"],
            spec["row"],
            spec["embed"],
            spec["row_code"],
            spec["key_code"],
            spec["both"],
            spec["table"],
        ],
        out_specs=[spec["rows"], spec["log"], spec["stack"]],
        out_shape=[
            jax.ShapeDtypeStruct((rows, width), f32),
            jax.ShapeDtypeStruct((pairs, 1, 2 * rows), f32),
            jax.ShapeDtypeStruct((pairs, 2 * rows, 2 * lanes), bf16),
        ],
        scratch_shapes=[pltpu.VMEM((count, 2 * rows), f32)],
        compiler_params=pltpu.CompilerParams(
            dimension_semantics=("arbitrary",), vmem_limit_bytes=60 << 20
        ),
        cost_estimate=free,
    )(query_full, bias_content, bias_segment, embed, row_code, key_code, both, table)


def attention_backward(stack, query_full, bias_segment, embed, row_code, key_code, both, table, number, out_back, attended, log_row):
    rows, width = query_full.shape
    count = both.shape[0]
    pairs = width // lanes
    blocks = count // lanes
    spec = attention_specs(rows, count, blocks)
    return pl.pallas_call(
        backward_kernel,
        grid=(pairs,),
        in_specs=[
            spec["stack"],
            spec["rows"],
            spec["row"],
            spec["embed"],
            spec["row_code"],
            spec["key_code"],
            spec["both"],
            spec["table"],
            pl.BlockSpec((blocks, 2 * lanes), lambda pair: (0, 0)),
            spec["rows"],
            spec["rows"],
            spec["log"],
        ],
        out_specs=[spec["rows"], spec["both"], spec["small"]],
        out_shape=[
            jax.ShapeDtypeStruct((rows, width), bf16),
            jax.ShapeDtypeStruct((count, 2 * width), bf16),
            jax.ShapeDtypeStruct((8, width), f32),
        ],
        scratch_shapes=[pltpu.VMEM((8, blocks, 2 * lanes), f32)],
        compiler_params=pltpu.CompilerParams(
            dimension_semantics=("arbitrary",), vmem_limit_bytes=60 << 20
        ),
        cost_estimate=takes(34),
    )(stack, query_full, bias_segment, embed, row_code, key_code, both, table, number, out_back, attended, log_row)


def marks_kernel(bound_list, meta_ref, table_ref, key_code_ref, bias_ref, number_ref, row_code_ref):
    blocks = meta_ref.shape[0]
    info = meta_ref[:, 0, :].astype(f32)
    segment = info[:, :lanes]
    rank = info[:, lanes : lanes + 1]
    first = info[:, lanes + 1 : lanes + 2] * lanes + info[:, lanes + 2 : lanes + 3]
    turn = lax.broadcasted_iota(jnp.int32, (blocks, 2 * lanes), 1)
    turn = jnp.where(turn < lanes, turn, turn - 2 * lanes)
    distance = (first[0:1, :] - first).astype(jnp.int32) + turn
    number = jnp.full(distance.shape, bucket_steps, jnp.int32)
    for bound in bound_list:
        number = number + (distance >= bound).astype(jnp.int32) - (distance <= -bound).astype(jnp.int32)
    number_ref[...] = number
    hidden = rank > rank[0:1, :]
    for head in range(bias_ref.shape[0]):
        value = jnp.zeros((blocks, 2 * lanes), f32)
        for bucket in range(2 * bucket_steps + 1):
            value = jnp.where(number == bucket, table_ref[head, bucket], value)
        bias_ref[head] = jnp.where(hidden, negative, value)
    lane = lax.broadcasted_iota(jnp.int32, (lanes, lanes), 1)
    code = (lane % 4).astype(f32)
    for block in range(blocks):
        column = jnp.broadcast_to(segment[block : block + 1, :], (lanes, lanes)).T
        marked = jnp.where(
            lane < 8, jnp.where(column == code, 1.0, 0.0), jnp.where(lane < 10, 1.0, 0.0)
        )
        key_code_ref[block * lanes : (block + 1) * lanes, :] = marked.astype(bf16)
        if block == 0:
            row_code_ref[:lanes, :] = marked
            row_code_ref[lanes:, :] = marked


def key_marks(meta_all, table_full, length):
    blocks = meta_all.shape[0]
    heads = table_full.shape[0]
    bounds = tuple(
        1 + level * level * length // (bucket_steps * bucket_steps) for level in range(bucket_steps)
    )
    return pl.pallas_call(
        functools.partial(marks_kernel, bounds),
        in_specs=[in_vmem, in_smem],
        out_specs=[in_vmem] * 4,
        out_shape=[
            jax.ShapeDtypeStruct((blocks * lanes, lanes), bf16),
            jax.ShapeDtypeStruct((heads, blocks, 2 * lanes), f32),
            jax.ShapeDtypeStruct((blocks, 2 * lanes), jnp.int32),
            jax.ShapeDtypeStruct((2 * lanes, lanes), f32),
        ],
        compiler_params=pltpu.CompilerParams(vmem_limit_bytes=40 << 20),
        cost_estimate=free,
    )(meta_all, table_full)


def assemble_pair(first_ref, second_ref, first_own_ref, second_own_ref, parts, places):
    own, *others = [pl.multiple_of(place, 16) for place in places]
    first_ref[pl.ds(own, first_own_ref.shape[0]), :] = first_own_ref[...]
    second_ref[pl.ds(own, second_own_ref.shape[0]), :] = second_own_ref[...]
    width, hidden = first_ref.shape[1], second_ref.shape[1]
    span = (width + hidden) // 2
    for (part_ref, base), other in zip(parts, others, strict=True):
        quarter = part_ref.shape[0] // 2
        rows = pl.ds(other, quarter)
        first_ref[rows, :] = part_ref[:quarter, base : base + width]
        second_ref[rows, : span - width] = part_ref[:quarter, base + width : base + span]
        second_ref[rows, span - width :] = part_ref[quarter:, base : base + span]


def assemble(target_ref, own_ref, parts, columns, places):
    own, *others = [pl.multiple_of(place, 16) for place in places]
    target_ref[pl.ds(own, own_ref.shape[0]), :] = own_ref[...]
    for part_ref, other in zip(parts, others, strict=True):
        target_ref[pl.ds(other, part_ref.shape[0]), :] = part_ref[:, columns]


def forward_half_kernel(
    place_ref,
    attended_ref,
    content_ref,
    stream_ref,
    output_own_ref,
    inner_own_ref,
    got_ref,
    near_ref,
    rest_ref,
    far_ref,
    vector_ref,
    bias_ref,
    out_low_ref,
    normed_ref,
    rows_ref,
    scale_ref,
    normed_low_ref,
    active_ref,
    slope_ref,
    square_ref,
    weight_output_ref,
    weight_inner_ref,
):
    width = attended_ref.shape[1]
    hidden = inner_own_ref.shape[1]
    half = content_ref.shape[0]
    places = [place_ref[at] for at in range(1, 6)]
    base = 3 * width
    assemble_pair(
        weight_output_ref,
        weight_inner_ref,
        output_own_ref,
        inner_own_ref,
        ((got_ref, base), (near_ref, 0), (rest_ref, base), (far_ref, 0)),
        places,
    )
    out_low = attended_ref[...].astype(bf16)
    out_low_ref[...] = out_low
    attention_out = dot(out_low, weight_output_ref[...])
    streams = jnp.concatenate([content_ref[...], stream_ref[...]], axis=0).astype(f32)
    residual = streams + attention_out
    rows, scale = normalized(residual)
    normed = rows * vector_ref[2:3, :] + vector_ref[3:4, :]
    normed_low = normed.astype(bf16)
    rows_ref[...] = rows
    scale_ref[...] = jnp.broadcast_to(scale, scale_ref.shape)
    normed_ref[...] = normed
    normed_low_ref[...] = normed_low
    lane = lax.broadcasted_iota(jnp.int32, (1, width), 1)
    total = jnp.zeros((1, width), f32)
    for at, value in enumerate((streams, attention_out, residual)):
        part = value[:half]
        summed = jnp.sum(jnp.sum(part * part, axis=0, keepdims=True), axis=1, keepdims=True)
        total = total + jnp.where((lane == at) | (lane == at + width // 2), summed, 0.0)
    square_ref[...] = jnp.broadcast_to(total, square_ref.shape)
    step = 512

    @pl.loop(0, hidden // step)
    def _(at):
        span = pl.ds(pl.multiple_of(at * step, step), step)
        inner = dot(normed_low, weight_inner_ref[:, span]) + bias_ref[0:1, span]
        below = 0.5 + 0.5 * lax.erf(inner * 0.7071067811865476)
        density = 0.3989422804014327 * jnp.exp(-0.5 * inner * inner)
        active_ref[:, span] = (inner * below).astype(bf16)
        slope_ref[:, span] = below + inner * density


def backward_half_kernel(
    place_ref,
    active_ref,
    slope_ref,
    normed_ref,
    rows_ref,
    scale_ref,
    weight_output_ref,
    weight_inner_ref,
    outer_own_ref,
    got_ref,
    rest_ref,
    vector_ref,
    square_ref,
    content_cotangent_ref,
    query_cotangent_ref,
    content_result_ref,
    query_result_ref,
    residual_back_ref,
    out_back_ref,
    outer_kept_ref,
    outer_sent_ref,
    inner_kept_ref,
    inner_sent_ref,
    attention_kept_ref,
    attention_sent_ref,
    sums_ref,
    weight_outer_ref,
    inner_back_ref,
    held_ref,
    bias_back_ref,
):
    width = normed_ref.shape[1]
    hidden = active_ref.shape[1]
    count = content_cotangent_ref.shape[0]
    core = place_ref[6]
    assemble(
        weight_outer_ref,
        outer_own_ref,
        (got_ref, rest_ref),
        slice(0, width),
        [place_ref[at] for at in range(7, 10)],
    )

    def give(value_ref, kept_ref, sent_ref):
        columns = kept_ref.shape[1]
        kept_ref[...] = value_ref[:, pl.ds(pl.multiple_of(core * columns, lanes), columns)]
        sent_ref[...] = value_ref[:, pl.ds(pl.multiple_of((1 - core) * columns, lanes), columns)]

    outer = dot(active_ref[...], weight_outer_ref[...]) + vector_ref[4:5, :]
    final_rows, final_scale = normalized(normed_ref[...] + outer)
    result = (final_rows * vector_ref[5:6, :] + vector_ref[6:7, :]).astype(bf16)
    content_result_ref[...] = result[:count]
    query_result_ref[...] = result[count:]
    cotangent = jnp.concatenate(
        [content_cotangent_ref[...], query_cotangent_ref[...]], axis=0
    ).astype(f32)
    sums_ref[9:10, :] = jnp.sum(cotangent * final_rows, axis=0, keepdims=True)
    sums_ref[10:11, :] = jnp.sum(cotangent, axis=0, keepdims=True)
    back_second = norm_back(cotangent * vector_ref[5:6, :], final_rows, final_scale)
    outer_back = back_second.astype(bf16)
    sums_ref[8:9, :] = jnp.sum(outer_back.astype(f32), axis=0, keepdims=True)
    held_ref[...] = outer_back
    give(held_ref, outer_kept_ref, outer_sent_ref)
    residual_back_ref[...] = back_second
    step = 512

    @pl.loop(0, hidden // step)
    def _(at):
        span = pl.ds(pl.multiple_of(at * step, step), step)
        back = dot_nt(outer_back, weight_outer_ref[span, :]) * slope_ref[:, span]
        low = back.astype(bf16)
        inner_back_ref[:, span] = low
        bias_back_ref[0:1, span] = jnp.sum(low.astype(f32), axis=0, keepdims=True)
        residual_back_ref[...] += dot_nt(low, weight_inner_ref[:, span])

    give(inner_back_ref, inner_kept_ref, inner_sent_ref)
    normed_back = residual_back_ref[...]
    rows = rows_ref[...]
    sums_ref[6:7, :] = jnp.sum(normed_back * rows, axis=0, keepdims=True)
    sums_ref[7:8, :] = jnp.sum(normed_back, axis=0, keepdims=True)
    residual_back = norm_back(normed_back * vector_ref[2:3, :], rows, scale_ref[:, 0:1])
    residual_back_ref[...] = residual_back
    attention_back = residual_back.astype(bf16)
    held_ref[...] = attention_back
    give(held_ref, attention_kept_ref, attention_sent_ref)
    out_back_ref[...] = dot_nt(attention_back, weight_output_ref[...]).astype(bf16)
    part = width // 2
    for at in range(hidden // width):
        sums_ref[11 + at : 12 + at, :part] = bias_back_ref[0:1, at * part : (at + 1) * part]
        sums_ref[11 + at : 12 + at, part:] = bias_back_ref[
            0:1, hidden // 2 + at * part : hidden // 2 + (at + 1) * part
        ]
    last = 11 + hidden // width
    sums_ref[last : last + 1, :] = square_ref[0:1, :]
    sums_ref[0:6, :] = jnp.zeros((6, width), f32)


def forward_half(places, *operands):
    rows, width = operands[0].shape
    hidden = operands[4].shape[1]
    shapes = [
        jax.ShapeDtypeStruct((rows, width), bf16),
        jax.ShapeDtypeStruct((rows, width), f32),
        jax.ShapeDtypeStruct((rows, width), f32),
        jax.ShapeDtypeStruct((rows, lanes), f32),
        jax.ShapeDtypeStruct((rows, width), bf16),
        jax.ShapeDtypeStruct((rows, hidden), bf16),
        jax.ShapeDtypeStruct((rows, hidden), f32),
        jax.ShapeDtypeStruct((8, width), f32),
        jax.ShapeDtypeStruct((width, width), bf16),
        jax.ShapeDtypeStruct((width, hidden), bf16),
    ]
    return pl.pallas_call(
        forward_half_kernel,
        grid=(1,),
        in_specs=[in_smem] + [resident(value) for value in operands],
        out_specs=[resident(shape) for shape in shapes],
        out_shape=shapes,
        compiler_params=pltpu.CompilerParams(vmem_limit_bytes=60 << 20),
        cost_estimate=takes(8),
    )(places, *operands)


def backward_half(places, *operands):
    active, normed = operands[0], operands[2]
    rows, width = normed.shape
    hidden = active.shape[1]
    count = rows // 2
    shapes = (
        [jax.ShapeDtypeStruct((count, width), bf16)] * 2
        + [jax.ShapeDtypeStruct((rows, width), f32), jax.ShapeDtypeStruct((rows, width), bf16)]
        + [jax.ShapeDtypeStruct((rows, width // 2), bf16)] * 2
        + [jax.ShapeDtypeStruct((rows, hidden // 2), bf16)] * 2
        + [jax.ShapeDtypeStruct((rows, width // 2), bf16)] * 2
        + [jax.ShapeDtypeStruct((16, width), f32)]
    )
    return pl.pallas_call(
        backward_half_kernel,
        grid=(1,),
        in_specs=[in_smem] + [resident(value) for value in operands],
        out_specs=[resident(shape) for shape in shapes],
        out_shape=shapes,
        scratch_shapes=[
            pltpu.VMEM((hidden, width), bf16),
            pltpu.VMEM((rows, hidden), bf16),
            pltpu.VMEM((rows, width), bf16),
            pltpu.VMEM((8, hidden), f32),
        ],
        compiler_params=pltpu.CompilerParams(vmem_limit_bytes=60 << 20),
        cost_estimate=takes(12),
    )(places, *operands)


def body(
    content,
    query_stream,
    block_rank,
    segments,
    positions,
    query_weight,
    key_weight,
    value_weight,
    output_weight,
    content_bias,
    segment_bias,
    segment_embed,
    relative_table,
    attention_gain,
    attention_shift,
    inner_weight,
    inner_bias,
    outer_weight,
    outer_bias,
    final_gain,
    final_shift,
    content_cotangent,
    query_cotangent,
):
    block_rows = content.shape[1]
    width = content.shape[2]
    rows = 2 * block_rows
    count = lax.axis_size("ctx")
    sides = lax.axis_size("wsh")
    side = lax.axis_index("wsh")
    core = lax.axis_index("ctx") % 2
    length = block_rows * count
    own_content = content[0]
    own_query = query_stream[0]
    part = width // sides
    table_heads, bucket_count = relative_table.shape
    head_count = table_heads * sides
    inner_rows = inner_bias.shape[0] // part
    low = 2

    first_places = shard_places(query_weight.shape[0])
    hidden = inner_weight.shape[1]
    near = (lax.axis_index("ctx") // low) % 2
    shard_rows = query_weight.shape[0]
    half, quarter = shard_rows // 2, shard_rows // 4
    base, span = 3 * width, (width + hidden) // 2
    (first_sent,) = moved(
        tuple(
            (at, window("0", half, 0, width), 0, window(0, half, at * width, width))
            for at in range(3)
        )
        + (
            (3, window("1", quarter, 0, width), 0, window(0, quarter, base, width)),
            (
                4,
                window("1", quarter, 0, span - width),
                0,
                window(0, quarter, base + width, span - width),
            ),
            (4, window("1", quarter, span - width, span), 0, window(quarter, quarter, base, span)),
        ),
        [jax.ShapeDtypeStruct((half, base + span), bf16)],
        jnp.stack([core * half, (2 * core + near) * quarter]).astype(jnp.int32),
        query_weight,
        key_weight,
        value_weight,
        output_weight,
        inner_weight,
    )
    first_got = across(first_sent)
    mark_rows = 16
    marks = jnp.concatenate(
        [
            segments[0].astype(bf16),
            block_rank[0].astype(bf16),
            (positions[0, :1] // lanes).astype(bf16),
            (positions[0, :1] % lanes).astype(bf16),
        ]
    )
    marks = jnp.pad(marks[None], ((0, mark_rows - 1), (0, width - marks.shape[0])))
    block = jnp.concatenate([own_content, marks], axis=0)
    gathered = gather_blocks(block)
    small_height = 16
    small = jnp.zeros((small_height * part,), bf16)
    filled = 0
    for vector in (
        content_bias,
        segment_bias,
        attention_gain,
        attention_shift,
        outer_bias,
        final_gain,
        final_shift,
        segment_embed.reshape(-1),
        inner_bias,
        relative_table.reshape(-1),
    ):
        small = small + jnp.pad(vector, (filled, small.shape[0] - filled - vector.shape[0]))
        filled += vector.shape[0]
    small = small.reshape(small_height, part)
    small_other = across(small)
    first_rest = partner(first_got, 1)
    second_near = partner(first_got[:, base:], low)
    third_places = shard_places(outer_weight.shape[0])
    third_sent = half_rows(third_places, 1, outer_weight)
    third_got = across(third_sent)

    small_pair = jnp.where(
        side == 0,
        jnp.concatenate([small, small_other], axis=1),
        jnp.concatenate([small_other, small], axis=1),
    ).astype(f32)
    bias_content = small_pair[0:1]
    bias_segment = small_pair[1:2]
    embed = small_pair[7:9]
    bias_inner = jnp.concatenate(
        [
            small_pair[9 : 9 + inner_rows, :part].reshape(-1),
            small_pair[9 : 9 + inner_rows, part:].reshape(-1),
        ]
    )
    table_row = small_pair[9 + inner_rows]
    table_full = jnp.concatenate(
        [
            table_row[: table_heads * bucket_count],
            table_row[part : part + table_heads * bucket_count],
        ]
    ).reshape(head_count, bucket_count)

    held = block_rows + mark_rows
    if len(gathered) == 1:
        stacked = gathered[0].reshape(count, held, width)
        content_all = stacked[:, :block_rows].reshape(length, width)
        meta_all = stacked[:, block_rows:]
    else:
        plan = []
        place = 0
        for at, piece in enumerate(gathered):
            for row in range(0, piece.shape[0], held):
                plan.append(
                    (at, window(row, block_rows), 0, window(place * block_rows, block_rows))
                )
                plan.append(
                    (at, window(row + block_rows, mark_rows), 1, window(place * mark_rows, mark_rows))
                )
                place += 1
        content_all, meta_all = moved(
            tuple(plan),
            [
                jax.ShapeDtypeStruct((length, width), bf16),
                jax.ShapeDtypeStruct((count * mark_rows, width), bf16),
            ],
            first_places,
            *gathered,
        )
        meta_all = meta_all.reshape(count, mark_rows, width)
    pairs = width // lanes
    runs = [(0, 0, width, 0, 0)]
    for pair in range(pairs):
        runs.append((1, pair * lanes, lanes, 1, 2 * pair * lanes))
        runs.append((2, pair * lanes, lanes, 1, (2 * pair + 1) * lanes))
    weight_query, weight_both = whole_rows(
        first_places, runs, (width, 2 * width), first_got, first_rest, query_weight, key_weight, value_weight
    )
    key_code, table, number, row_code = key_marks(meta_all, table_full, length)

    streams = jnp.concatenate([own_content, own_query], axis=0)
    query_full = dot(streams, weight_query)
    both = dot(content_all, weight_both).astype(bf16)
    attended, log_row, stack = attention_forward(
        query_full, bias_content, bias_segment, embed, row_code, key_code, both, table
    )

    hidden = inner_weight.shape[1]
    second_near, third_got, attended = lax.optimization_barrier(
        (second_near, third_got, attended)
    )
    second_far = partner(second_near, 1)
    third_rest = partner(third_got, 1)
    half_places = jnp.concatenate(
        [
            quarter_places(query_weight.shape[0]),
            core[None].astype(jnp.int32),
            third_places[1:],
        ]
    )
    (
        out_low,
        normed,
        norm_rows,
        norm_scale,
        normed_low,
        active_low,
        slope,
        squares,
        weight_output,
        weight_inner,
    ) = forward_half(
        half_places,
        attended,
        own_content,
        own_query,
        output_weight,
        inner_weight,
        first_got,
        second_near,
        first_rest,
        second_far,
        small_pair,
        bias_inner[None],
    )
    out_low_other = partner(out_low, 1)
    normed_other = partner(normed_low, 1)
    active_other = partner(active_low, 1)
    (
        content_result,
        query_result,
        residual_back,
        out_back,
        outer_kept,
        outer_sent,
        inner_kept,
        inner_sent,
        attention_kept,
        attention_sent,
        vectors,
    ) = backward_half(
        half_places,
        active_low,
        slope,
        normed,
        norm_rows,
        norm_scale,
        weight_output,
        weight_inner,
        outer_weight,
        third_got,
        third_rest,
        small_pair,
        squares,
        content_cotangent[0],
        query_cotangent[0],
    )

    cuts, extra = split_bits(count)
    wide_cuts = [1] + cuts
    order_one = [0] + cuts
    order_two = cuts[:1] + [0] + cuts[1:]
    places_one = piece_places(order_one, cuts)
    places_two = piece_places(order_two, cuts)
    wide_places = by_core(
        piece_places([1, 0] + cuts, wide_cuts),
        piece_places([1, cuts[0], 0] + cuts[1:], wide_cuts),
        2 << len(cuts),
    )
    places_out = jnp.concatenate([piece_places(cuts, cuts), core[None].astype(jnp.int32)])
    wide_places_out = by_core(
        piece_places(wide_cuts, wide_cuts),
        piece_places([1] + cuts[1:] + cuts[:1], wide_cuts),
        1 << len(cuts),
    )

    outer_keep, outer_send = product_pieces(
        places_one, active_low, active_other, outer_kept, partner(outer_sent, 1)
    )
    outer_got = pass_on(outer_send, order_one[0])
    inner_keep, inner_send = product_pieces(
        places_two,
        normed_low,
        normed_other,
        inner_kept,
        partner(inner_sent, 1),
        out_low,
        out_low_other,
        attention_kept,
        partner(attention_sent, 1),
    )
    inner_got = pass_on(inner_send, order_two[0])

    line = cuts[1:]
    last = cuts[2]

    def add_extra(value):
        for bit in extra:
            value = fold_last(value, partner(value, bit))
        return value

    query_back, both_back, small_back = attention_backward(
        stack,
        query_full,
        bias_segment,
        embed,
        row_code,
        key_code,
        both,
        table,
        number,
        after(out_back, outer_send, inner_send),
        attended,
        log_row,
    )
    hidden_rows = hidden // part // sides
    order = Sequence(after(wide_places_out, small_back))
    outer_got, inner_got = order.wait(outer_got, inner_got)
    outer_keep, outer_send = fold(outer_keep, outer_got)
    outer_send = order.ready(outer_send)
    outer_got = partner(outer_send, cuts[0])
    inner_keep, inner_send = fold(inner_keep, inner_got)
    inner_send = order.ready(inner_send)
    inner_got = across(inner_send)
    tail_keep, tail_send = cut_gradient(
        wide_places,
        vectors,
        small_back,
        dot_tn(streams, query_back),
        dot_tn(content_all, order.ready(both_back)),
    )
    tail_keep = order.ready(tail_keep)
    content_share = order.ready(share_of_content(order.ready(both_back), weight_both))
    outer_got = order.wait(outer_got)
    inner_got = order.wait(inner_got)
    tail_send = order.ready(tail_send)
    tail_got = partner(tail_send, 1)
    outer_keep, outer_send = fold(outer_keep, outer_got)
    outer_send = order.ready(outer_send)
    outer_got = partner(outer_send, line[0])
    inner_keep, inner_send = fold(inner_keep, inner_got)
    inner_send = order.ready(inner_send)
    inner_got = partner(inner_send, line[0])
    share_keep, share_send = content_share[: count // 2], order.ready(content_share[count // 2 :])
    share_got = partner(share_send, 1)
    tail_got = order.wait(tail_got)
    tail_keep, tail_send = fold(tail_keep, tail_got)
    tail_send = order.ready(tail_send)
    tail_got = pass_mixed(tail_send, 0, cuts[0])
    share_got = order.wait(share_got)
    share_keep, share_send = fold(share_keep, share_got)
    share_send = order.ready(share_send)
    share_got = partner(share_send, cuts[0])
    outer_got = order.wait(outer_got)
    outer_keep, outer_send = fold(outer_keep, outer_got)
    outer_send = order.ready(outer_send)
    outer_got = partner(outer_send, last)
    inner_got = order.wait(inner_got)
    inner_keep, inner_send = fold(inner_keep, inner_got)
    inner_send = order.ready(inner_send)
    inner_got = partner(inner_send, last)
    tail_got = order.wait(tail_got)
    tail_keep, tail_send = fold(tail_keep, tail_got)
    tail_send = order.ready(tail_send)
    tail_got = pass_mixed(tail_send, cuts[0], 0)
    tail_got = order.wait(tail_got)
    tail_keep, tail_send = fold(tail_keep, tail_got)
    tail_send = order.ready(tail_send)
    tail_got = partner(tail_send, line[0])
    outer_got = order.wait(outer_got)
    outer_value = order.ready(add_extra(fold_last(outer_keep, outer_got)))
    outer_got = partner(outer_value, last)
    inner_got = order.wait(inner_got)
    inner_value = order.ready(add_extra(fold_last(inner_keep, inner_got)))
    inner_got = partner(inner_value, last)
    tail_got = order.wait(tail_got)
    tail_keep, tail_send = fold(tail_keep, tail_got)
    tail_send = order.ready(tail_send)
    tail_got = partner(tail_send, last)
    share_got = order.wait(share_got)
    share_keep, share_send = fold(share_keep, share_got)
    share_send = order.ready(share_send)
    share_got = partner(share_send, line[0])
    outer_got = order.wait(outer_got)
    outer_value = order.ready(piled(outer_value, outer_got))
    outer_got = partner(outer_value, line[0])
    inner_got = order.wait(inner_got)
    inner_value = order.ready(piled(inner_value, inner_got))
    inner_got = partner(inner_value, line[0])
    tail_got = order.wait(tail_got)
    tail_value = order.ready(add_extra(fold_last(tail_keep, tail_got)))
    tail_got = pass_mixed(tail_value, last, cuts[0])
    outer_got = order.wait(outer_got)
    outer_value = order.ready(piled(outer_value, outer_got))
    outer_got = partner(outer_value, cuts[0])
    share_got = order.wait(share_got)
    share_keep, share_send = fold(share_keep, share_got)
    share_send = order.ready(share_send)
    share_got = partner(share_send, last)
    streams_back = residual_back + dot_nt(order.ready(query_back), weight_query)
    tail_got = order.wait(tail_got)
    tail_value = order.ready(piled(tail_value, tail_got))
    tail_got = pass_mixed(tail_value, line[0], last)
    inner_got = order.wait(inner_got)
    inner_value = order.ready(piled(inner_value, inner_got))
    inner_got = partner(inner_value, cuts[0])
    tail_got = order.wait(tail_got)
    tail_value = order.ready(piled(tail_value, tail_got))
    tail_got = pass_mixed(tail_value, cuts[0], line[0])
    outer_got = order.wait(outer_got)
    outer_value = order.ready(piled(outer_value, outer_got))
    outer_got = partner(outer_value, 1)
    outer_got = order.wait(outer_got)
    (outer_weight_sum,) = lay_out(
        places_out,
        (((0, 0, width // 2, -1), (1, 0, width // 2, -2)),),
        outer_value,
        outer_got,
    )
    outer_weight_sum = order.ready(outer_weight_sum)
    share_got = order.wait(share_got)
    for bit in extra:
        share_keep, share_send = fold(share_keep, share_got)
        share_got = partner(share_send, bit)
    content_back = streams_back[:block_rows] + share_keep[0].astype(f32) + share_got[0].astype(f32)
    content_back = order.ready(content_back)
    tail_got = order.wait(tail_got)
    tail_value = order.ready(piled(tail_value, tail_got))
    tail_got = partner(tail_value, 1)
    inner_got = order.wait(inner_got)
    inner_value = order.ready(piled(inner_value, inner_got))
    inner_got = partner(inner_value, 1)
    inner_got = order.wait(inner_got)
    inner_weight_sum, output_weight_sum = lay_out(
        places_out,
        (
            ((0, 0, hidden // 2, -1), (1, 0, hidden // 2, -2)),
            ((0, hidden // 2, width // 2, -1), (1, hidden // 2, width // 2, -2)),
        ),
        inner_value,
        inner_got,
    )
    inner_weight_sum, output_weight_sum = order.ready(inner_weight_sum, output_weight_sum)
    tail_got = order.wait(tail_got)
    plan = []
    for kind in range(3):
        row = []
        for pair in range(pairs):
            taken = pair * lanes if kind == 0 else width + (2 * pair + kind - 1) * lanes
            row.append((0, taken, lanes, pair * lanes))
        plan.append(tuple(row))
    plan.append(((0, 3 * width, lanes, 0),))
    query_weight_sum, key_weight_sum, value_weight_sum, vector_sums = lay_out(
        order.mark, tuple(plan), tail_value, tail_got
    )
    sums = vector_sums[:, :16].T
    table_sum = jnp.swapaxes(sums[4:6].reshape(2, -1, lanes)[:, :, :bucket_count], 0, 1).reshape(
        table_heads, bucket_count
    )
    inner_bias_sum = sums[11 : 11 + hidden_rows].reshape(-1)
    token_total = length * sides * width
    root_mean = jnp.sqrt(sums[11 + hidden_rows, :3] / token_total)
    return (
        content_result[None],
        query_result[None],
        content_back[None],
        streams_back[block_rows:][None],
        query_weight_sum,
        key_weight_sum,
        value_weight_sum,
        output_weight_sum,
        sums[0],
        sums[1],
        sums[2:4],
        table_sum,
        sums[6],
        sums[7],
        inner_weight_sum,
        inner_bias_sum,
        outer_weight_sum,
        sums[8],
        sums[9],
        sums[10],
        root_mean,
    )


def solution(mesh):
    tokens = P("wsh", "ctx", None)
    marks = P("wsh", "ctx")
    matrix = P("wsh", None)
    vector = P("wsh")
    placed = (
        (tokens, tokens, marks, marks, marks)
        + (matrix,) * 4
        + (vector, vector, P(None, "wsh"), matrix, vector, vector, matrix, vector, matrix)
        + (vector,) * 3
        + (tokens, tokens)
    )
    given = (
        (tokens,) * 4
        + (matrix,) * 4
        + (vector, vector, P(None, "wsh"), matrix, vector, vector, matrix, vector, matrix)
        + (vector,) * 3
        + (P(),)
    )
    return jax.shard_map(body, mesh=mesh, in_specs=placed, out_specs=given, check_vma=False)
```

```python
import functools

import jax
import jax.numpy as jnp
from jax import lax
from jax.experimental import pallas as pl
from jax.experimental.pallas import tpu as pltpu
from jax.sharding import PartitionSpec as P

negative = -1e30
epsilon = 1e-05
bucket_steps = 16
key_tile = 256
lanes = 128
highest = lax.Precision.HIGHEST
f32 = jnp.float32
bf16 = jnp.bfloat16


free = pl.CostEstimate(flops=0, bytes_accessed=0, transcendentals=0)
in_vmem = pl.BlockSpec(memory_space=pltpu.VMEM)
in_smem = pl.BlockSpec(memory_space=pltpu.SMEM)


def resident(value):
    rank = len(value.shape)
    return pl.BlockSpec(value.shape, lambda at: (0,) * rank, pipeline_mode=pl.Buffered(1))


def takes(microseconds):
    return pl.CostEstimate(
        flops=microseconds * 1_000_000_000, bytes_accessed=0, transcendentals=0
    )


def normalized(values):
    centred = values - jnp.mean(values, axis=-1, keepdims=True)
    spread = jnp.mean(centred * centred, axis=-1, keepdims=True)
    scale = lax.rsqrt(spread + epsilon)
    return centred * scale, scale


def norm_back(cotangent, rows, scale):
    mean = jnp.mean(cotangent, axis=-1, keepdims=True)
    along = jnp.mean(cotangent * rows, axis=-1, keepdims=True)
    return scale * (cotangent - mean - rows * along)


def dot(left, right):
    return jnp.dot(left, right, preferred_element_type=f32)


def dot_nt(left, right):
    return lax.dot_general(left, right, (((1,), (1,)), ((), ())), preferred_element_type=f32)


def dot_tn(left, right):
    return lax.dot_general(left, right, (((0,), (0,)), ((), ())), preferred_element_type=f32)


def partner(value, bit):
    count = lax.axis_size("ctx")
    return lax.ppermute(value, "ctx", [(place, place ^ bit) for place in range(count)])


def across(value):
    return lax.ppermute(value, "wsh", [(0, 1), (1, 0)])


def bits_of(count):
    result = []
    bit = 1
    while bit < count:
        result.append(bit)
        bit *= 2
    return result


def block_order(count):
    order = [0]
    for bit in reversed(bits_of(count)):
        order = order + [place | bit for place in order]
    return order


def gather_blocks(own):
    count = lax.axis_size("ctx")
    bits = bits_of(count)
    if count != 16:
        held = own
        for bit in reversed(bits):
            held = jnp.concatenate([held, partner(held, bit)], axis=0)
        return [held]
    low = bits[1]
    near = partner(own, low)
    first = [own] + [partner(own, place) for place in (bits[3], bits[2], bits[2] | bits[3])]
    second = [near] + [partner(block, low) for block in first[1:]]
    others = partner(jnp.concatenate(first + second, axis=0), 1)
    return first + second + [others]


def move_kernel(plan, inputs, place_ref, *refs):
    sources, targets = refs[:inputs], refs[inputs:]
    for source, taken, target, put in plan:
        targets[target][put(place_ref)] = sources[source][taken(place_ref)]


def moved(plan, shapes, places, *sources, limit=40):
    return pl.pallas_call(
        functools.partial(move_kernel, plan, len(sources)),
        grid=(1,),
        in_specs=[in_smem] + [resident(value) for value in sources],
        out_specs=[resident(shape) for shape in shapes],
        out_shape=shapes,
        compiler_params=pltpu.CompilerParams(vmem_limit_bytes=limit << 20),
        cost_estimate=free,
    )(places, *sources)


def window(start, rows, left=None, columns=None):
    def make(place_ref):
        first = start
        if isinstance(start, str):
            first = pl.multiple_of(place_ref[int(start)], 16)
        if left is None:
            return (pl.ds(first, rows), slice(None))
        return (pl.ds(first, rows), pl.ds(left, columns))

    return make


def half_rows(places, cut, *shards):
    rows = shards[0].shape[0] // 2 // cut
    plan = []
    left = 0
    for at, shard in enumerate(shards):
        columns = shard.shape[1]
        plan.append((at, window("0", rows, 0, columns), 0, window(0, rows, left, columns)))
        left += columns
    return moved(tuple(plan), [jax.ShapeDtypeStruct((rows, left), bf16)], places, *shards)[0]


def whole_rows(places, runs, widths, got, rest, *shards):
    rows = shards[0].shape[0]
    half = rows // 2
    lefts = [0]
    for shard in shards:
        lefts.append(lefts[-1] + shard.shape[1])
    plan = []
    for shard, first, columns, target, column in runs:
        plan.append(
            (2 + shard, window(0, rows, first, columns), target, window("1", rows, column, columns))
        )
        for source, place in ((0, "2"), (1, "3")):
            plan.append(
                (
                    source,
                    window(0, half, lefts[shard] + first, columns),
                    target,
                    window(place, half, column, columns),
                )
            )
    shapes = [jax.ShapeDtypeStruct((2 * rows, width), bf16) for width in widths]
    return moved(tuple(plan), shapes, places, got, rest, *shards)


def quarter_places(rows):
    core = lax.axis_index("ctx") % 2
    near = (lax.axis_index("ctx") // 2) % 2
    side = lax.axis_index("wsh")
    quarter = rows // 4
    base = (1 - side) * rows
    spots = [(core, near), (core, 1 - near), (1 - core, near), (1 - core, 1 - near)]
    return jnp.stack(
        [(2 * core + near) * quarter, side * rows]
        + [base + (2 * first + second) * quarter for first, second in spots]
    ).astype(jnp.int32)


def shard_places(rows):
    core = lax.axis_index("ctx") % 2
    side = lax.axis_index("wsh")
    half = rows // 2
    base = (1 - side) * rows
    return jnp.stack(
        [core * half, side * rows, base + core * half, base + (1 - core) * half]
    ).astype(jnp.int32)


def split_bits(count):
    bits = bits_of(count)
    return bits[1:4], bits[4:]


def own_bit(bit):
    if bit == 0:
        return lax.axis_index("wsh")
    return (lax.axis_index("ctx") // bit) % 2


def pass_on(value, bit):
    return across(value) if bit == 0 else partner(value, bit)


def pass_mixed(value, even_bit, odd_bit):
    count = lax.axis_size("ctx")
    pairs = []
    for place in range(count):
        bit = odd_bit if place % 2 else even_bit
        for side in range(2):
            other = (place, 1 - side) if bit == 0 else (place ^ bit, side)
            pairs.append((2 * place + side, 2 * other[0] + other[1]))
    return lax.ppermute(value, ("ctx", "wsh"), pairs)


def by_core(even, odd, half):
    core = lax.axis_index("ctx") % 2
    return jnp.where(
        core == 0,
        jnp.concatenate([even[:half], odd[half:]]),
        jnp.concatenate([odd[:half], even[half:]]),
    )


class Sequence:
    def __init__(self, mark):
        self.mark = mark

    def wait(self, *values):
        *values, self.mark = lax.optimization_barrier(tuple(values) + (self.mark,))
        return values[0] if len(values) == 1 else tuple(values)

    ready = wait


def piece_places(order, cuts):
    total = len(order)
    place = jnp.arange(1 << total, dtype=jnp.int32)
    result = jnp.zeros_like(place)
    for at, bit in enumerate(order):
        value = ((place >> (total - 1 - at)) & 1) ^ own_bit(bit)
        weight = 1 << len(cuts) if bit == 0 else 1 << (len(cuts) - 1 - cuts.index(bit))
        result = result + value * weight
    return result


def fold_kernel(keep_ref, received_ref, *target_refs):
    first = 0
    for target_ref in target_refs:

        @pl.loop(0, target_ref.shape[0])
        def _(place, first=first, target_ref=target_ref):
            target_ref[place] = (
                keep_ref[first + place].astype(f32) + received_ref[first + place].astype(f32)
            ).astype(bf16)

        first += target_ref.shape[0]


def fold_parts(keep, received, parts):
    piece = jax.ShapeDtypeStruct((keep.shape[0] // parts,) + keep.shape[1:], bf16)
    return pl.pallas_call(
        fold_kernel,
        grid=(1,),
        in_specs=[resident(keep)] * 2,
        out_specs=[resident(piece)] * parts,
        out_shape=[piece] * parts,
        compiler_params=pltpu.CompilerParams(vmem_limit_bytes=40 << 20),
        cost_estimate=free,
    )(keep, received)


def fold(keep, received):
    return fold_parts(keep, received, 2)


def fold_last(keep, received):
    return fold_parts(keep, received, 1)[0]


def pile_kernel(*refs):
    target_ref = refs[-1]
    first = 0
    for source_ref in refs[:-1]:

        @pl.loop(0, source_ref.shape[0])
        def _(place, first=first, source_ref=source_ref):
            target_ref[first + place] = source_ref[place]

        first += source_ref.shape[0]


def piled(*values):
    height = sum(value.shape[0] for value in values)
    return pl.pallas_call(
        pile_kernel,
        in_specs=[in_vmem] * len(values),
        out_specs=in_vmem,
        out_shape=jax.ShapeDtypeStruct((height,) + values[0].shape[1:], values[0].dtype),
        compiler_params=pltpu.CompilerParams(vmem_limit_bytes=40 << 20),
        cost_estimate=free,
    )(*values)


def share_kernel(back_ref, weight_ref, out_ref):
    out_ref[...] = dot_nt(back_ref[...], weight_ref[...]).astype(bf16).reshape(out_ref.shape)


def share_of_content(both_back, weight_both):
    count, columns = both_back.shape
    width = weight_both.shape[0]
    step = 2 * lanes
    return pl.pallas_call(
        share_kernel,
        grid=(count // step,),
        in_specs=[
            pl.BlockSpec((step, columns), lambda at: (at, 0)),
            pl.BlockSpec((width, columns), lambda at: (0, 0), pipeline_mode=pl.Buffered(1)),
        ],
        out_specs=pl.BlockSpec((2, lanes, width), lambda at: (at, 0, 0)),
        out_shape=jax.ShapeDtypeStruct((count // lanes, lanes, width), bf16),
        compiler_params=pltpu.CompilerParams(vmem_limit_bytes=40 << 20),
        cost_estimate=free,
    )(both_back, weight_both)


def after(value, *others):
    return lax.optimization_barrier((value,) + others)[0]


def product_kernel(groups, place_ref, *refs):
    operands, (keep_ref, send_ref, total_ref) = refs[: 4 * groups], refs[4 * groups :]
    rows = keep_ref.shape[1]
    step = 256
    left = 0
    for group in range(groups):
        left_own, left_other, right_own, right_other = operands[4 * group : 4 * group + 4]
        columns = right_own.shape[1]
        for start in range(0, left_own.shape[1], step):
            total_ref[start : start + step, left : left + columns] = dot_tn(
                left_own[:, start : start + step], right_own[...]
            ) + dot_tn(left_other[:, start : start + step], right_other[...])
        left += columns
    for at, ref in enumerate((keep_ref, send_ref)):

        @pl.loop(0, ref.shape[0])
        def _(place, at=at, ref=ref):
            block = place_ref[at * ref.shape[0] + place]
            start = pl.multiple_of(block * rows, 8)
            ref[place] = total_ref[pl.ds(start, rows), :].astype(bf16)


def product_pieces(places, *operands):
    groups = len(operands) // 4
    half = places.shape[0] // 2
    height = operands[0].shape[1]
    columns = sum(operands[4 * group + 2].shape[1] for group in range(groups))
    piece = jax.ShapeDtypeStruct((half, height // (2 * half), columns), bf16)
    return pl.pallas_call(
        functools.partial(product_kernel, groups),
        grid=(1,),
        in_specs=[in_smem] + [resident(value) for value in operands],
        out_specs=[resident(piece)] * 2,
        out_shape=[piece, piece],
        scratch_shapes=[pltpu.VMEM((height, columns), f32)],
        compiler_params=pltpu.CompilerParams(vmem_limit_bytes=60 << 20),
        cost_estimate=takes(4),
    )(places, *operands)


def cut_kernel(place_ref, vector_ref, small_ref, *refs):
    parts, (keep_ref, send_ref, turned_ref) = refs[:-3], refs[-3:]
    rows = keep_ref.shape[1]
    height = vector_ref.shape[1]
    filled = jnp.concatenate(
        [
            small_ref[...] + vector_ref[0:8, :],
            vector_ref[8:, :],
            jnp.zeros((lanes - vector_ref.shape[0], height), f32),
        ],
        axis=0,
    )
    for start in range(0, height, lanes):
        turned_ref[start : start + lanes, :] = filled[:, start : start + lanes].T
    parts = parts + (turned_ref,)
    for at, ref in enumerate((keep_ref, send_ref)):

        @pl.loop(0, ref.shape[0])
        def _(place, at=at, ref=ref):
            block = place_ref[at * ref.shape[0] + place]
            start = pl.multiple_of(block * rows, 8)
            left = 0
            for part in parts:
                columns = part.shape[1]
                ref[place, :, left : left + columns] = part[pl.ds(start, rows), :].astype(bf16)
                left += columns


def cut_gradient(places, vectors, small, *parts):
    half = places.shape[0] // 2
    height = parts[0].shape[0]
    columns = sum(part.shape[1] for part in parts) + lanes
    piece = jax.ShapeDtypeStruct((half, height // (2 * half), columns), bf16)
    return pl.pallas_call(
        cut_kernel,
        grid=(1,),
        in_specs=[in_smem] + [resident(value) for value in (vectors, small) + parts],
        out_specs=[resident(piece)] * 2,
        out_shape=[piece, piece],
        scratch_shapes=[pltpu.VMEM((height, lanes), f32)],
        compiler_params=pltpu.CompilerParams(vmem_limit_bytes=40 << 20),
        cost_estimate=free,
    )(places, vectors, small, *parts)


def lay_out_kernel(plan, place_ref, *refs):
    outputs = len(plan)
    sources, targets = refs[:-outputs], refs[-outputs:]
    halves = 2 if place_ref.shape[0] > sources[0].shape[0] + 1 else 1
    for half in range(halves):
      for runs, target in zip(plan, targets, strict=True):
        for source, first, columns, column in runs:
            piece_ref = sources[source + half]
            count, rows = piece_ref.shape[:2]

            @pl.loop(0, count)
            def _(place, piece_ref=piece_ref, rows=rows, target=target, first=first, columns=columns, column=column, half=half):
                start = pl.multiple_of(place_ref[half * count + place] * rows, 8)
                value = piece_ref[place, :, first : first + columns].astype(f32)
                if column >= 0:
                    target[pl.ds(start, rows), column : column + columns] = value
                else:
                    core = place_ref[count]
                    which = core if column == -1 else 1 - core
                    left = pl.multiple_of(which * columns, lanes)
                    target[pl.ds(start, rows), pl.ds(left, columns)] = value


def lay_out(places, plan, *pieces):
    shapes = []
    halves = 2 if places.shape[0] > pieces[0].shape[0] + 1 else 1
    for runs in plan:
        count, rows = pieces[runs[0][0]].shape[:2]
        shapes.append(jax.ShapeDtypeStruct((halves * count * rows, sum(run[2] for run in runs)), f32))
    return pl.pallas_call(
        functools.partial(lay_out_kernel, plan),
        grid=(1,),
        in_specs=[in_smem] + [resident(value) for value in pieces],
        out_specs=[resident(shape) for shape in shapes],
        out_shape=shapes,
        compiler_params=pltpu.CompilerParams(vmem_limit_bytes=40 << 20),
        cost_estimate=takes(3),
    )(places, *pieces)


def stream_bias(table_ref, head, block):
    spread = jnp.broadcast_to(table_ref[head, pl.ds(block, 1), :], (lanes, 2 * lanes))
    return pltpu.roll(spread, 0, 1, stride=1, stride_axis=0)[:, :lanes]


def tile_bias(table_ref, block):
    parts = []
    for piece in range(key_tile // lanes):
        first = stream_bias(table_ref, 0, block + piece)
        second = stream_bias(table_ref, 1, block + piece)
        parts.append(jnp.concatenate([first, first, second, second], axis=1))
    return jnp.concatenate(parts, axis=0)


def own_mask():
    row = lax.broadcasted_iota(jnp.int32, (key_tile, 4 * lanes), 0)
    column = lax.broadcasted_iota(jnp.int32, (key_tile, 4 * lanes), 1)
    stream = (column // lanes) % 2
    return jnp.where((stream == 1) & (row == column % lanes), negative, 0.0)


def forward_kernel(
    query_ref,
    content_bias_ref,
    segment_bias_ref,
    embed_ref,
    row_code_ref,
    key_code_ref,
    both_ref,
    table_ref,
    out_ref,
    log_ref,
    stack_ref,
    score_ref,
):
    rows = query_ref.shape[0]
    tiles = both_ref.shape[0] // key_tile
    lane = lax.broadcasted_iota(jnp.int32, (rows, lanes), 1)
    first = lane < lanes // 2
    query = query_ref[...]
    low = (query + content_bias_ref[...]).astype(bf16).astype(f32) * 0.125
    shifted = query + segment_bias_ref[...]
    zero_term = shifted * embed_ref[0:1, :]
    one_term = shifted * embed_ref[1:2, :]
    code = row_code_ref[...]
    for head in range(2):
        own = first if head == 0 else jnp.logical_not(first)
        zero_sum = jnp.sum(jnp.where(own, zero_term, 0.0), axis=1, keepdims=True) * 0.125
        one_sum = jnp.sum(jnp.where(own, one_term, 0.0), axis=1, keepdims=True) * 0.125
        step = zero_sum - one_sum
        step_high = step.astype(bf16).astype(f32)
        step_low = step - step_high
        one_high = one_sum.astype(bf16).astype(f32)
        one_low = one_sum - one_high
        extra = jnp.where(
            lane < 4,
            step_high,
            jnp.where(lane < 8, step_low, jnp.where(lane == 8, one_high, one_low)),
        )
        stack_ref[0, pl.ds(head * rows, rows), 0:lanes] = jnp.where(own, low, 0.0).astype(bf16)
        stack_ref[0, pl.ds(head * rows, rows), lanes : 2 * lanes] = (extra * code).astype(bf16)
    stack = stack_ref[0]

    def scores(tile, top):
        start = pl.multiple_of(tile * key_tile, key_tile)
        keys = jnp.concatenate(
            [both_ref[pl.ds(start, key_tile), :lanes], key_code_ref[pl.ds(start, key_tile), :]], axis=1
        )
        score = dot_nt(keys, stack) + tile_bias(table_ref, tile * (key_tile // lanes))
        if isinstance(tile, int) and tile == 0:
            score = score + own_mask()
        score_ref[pl.ds(start, key_tile), :] = score
        return jnp.maximum(top, jnp.max(score.reshape(key_tile // 8, 8, 4 * lanes), axis=0))

    top = jnp.full((8, 4 * lanes), negative, f32)
    top = scores(0, top)
    top = lax.fori_loop(1, tiles, scores, top, unroll=min(7, tiles - 1))
    peak = jnp.max(top, axis=0, keepdims=True)

    def gathered(tile, running):
        total, mixed = running
        start = pl.multiple_of(tile * key_tile, key_tile)
        weight = jnp.exp(score_ref[pl.ds(start, key_tile), :] - peak)
        total = total + jnp.sum(weight.reshape(key_tile // 8, 8, 4 * lanes), axis=0)
        mixed = mixed + dot_tn(both_ref[pl.ds(start, key_tile), lanes:], weight.astype(bf16))
        return total, mixed

    total, mixed = lax.fori_loop(
        0,
        tiles,
        gathered,
        (jnp.zeros((8, 4 * lanes), f32), jnp.zeros((lanes, 4 * lanes), f32)),
        unroll=min(8, tiles),
    )
    total = jnp.sum(total, axis=0, keepdims=True)
    mixed = mixed / total
    half = lanes // 2
    joined = jnp.concatenate([mixed[:half, :rows], mixed[half:, rows:]], axis=0)
    out_ref[...] = joined.T
    log_ref[0] = peak + jnp.log(total)


def diagonal_sums(square):
    lane = lax.broadcasted_iota(jnp.int32, (8, lanes), 1)
    near = square[0:8]
    far = jnp.zeros((8, lanes), f32)
    for group in range(1, lanes // 8):
        turned = pltpu.roll(square[8 * group : 8 * group + 8], lanes - 8 * group, 1)
        inside = lane < lanes - 8 * group
        near = near + jnp.where(inside, turned, 0.0)
        far = far + jnp.where(inside, 0.0, turned)
    both = jnp.concatenate([near, far], axis=1)
    row = lax.broadcasted_iota(jnp.int32, (8, 2 * lanes), 0)
    for bit in (1, 2, 4):
        both = jnp.where((row // bit) % 2 == 1, pltpu.roll(both, 2 * lanes - bit, 1), both)
    return jnp.sum(both, axis=0, keepdims=True)


def backward_kernel(
    stack_ref,
    query_ref,
    segment_bias_ref,
    embed_ref,
    row_code_ref,
    key_code_ref,
    both_ref,
    table_ref,
    number_ref,
    out_back_ref,
    attended_ref,
    log_ref,
    query_back_ref,
    both_back_ref,
    small_ref,
    diagonal_ref,
):
    rows = query_ref.shape[0]
    tiles = both_ref.shape[0] // key_tile
    half = lanes // 2
    lane = lax.broadcasted_iota(jnp.int32, (rows, lanes), 1)
    first = lane < half
    out_back = out_back_ref[...]
    product = (out_back.astype(f32) * attended_ref[...]).T
    delta = jnp.concatenate(
        [
            jnp.sum(product[:half], axis=0, keepdims=True),
            jnp.sum(product[half:], axis=0, keepdims=True),
        ],
        axis=1,
    )
    zeros = jnp.zeros_like(out_back)
    back_stack = jnp.concatenate(
        [jnp.where(first, out_back, zeros), jnp.where(first, zeros, out_back)], axis=0
    )
    stack = stack_ref[0]
    query_stack = stack[:, :lanes]
    log_row = log_ref[0]

    def step(tile, running):
        start = pl.multiple_of(tile * key_tile, key_tile)
        block = tile * (key_tile // lanes)
        keys = jnp.concatenate(
            [both_ref[pl.ds(start, key_tile), :lanes], key_code_ref[pl.ds(start, key_tile), :]], axis=1
        )
        score = dot_nt(keys, stack) + tile_bias(table_ref, block)
        if isinstance(tile, int) and tile == 0:
            score = score + own_mask()
        weight = jnp.exp(score - log_row)
        weight_back = dot_nt(both_ref[pl.ds(start, key_tile), lanes:], back_stack)
        score_back = weight * (weight_back - delta)
        score_low = score_back.astype(bf16)
        both_back_ref[pl.ds(start, key_tile), lanes:] = dot(
            weight.astype(bf16), back_stack
        ).astype(bf16)
        both_back_ref[pl.ds(start, key_tile), :lanes] = dot(score_low, query_stack).astype(bf16)
        for head in range(2):
            for piece in range(key_tile // lanes):
                part = score_back[
                    piece * lanes : (piece + 1) * lanes, head * rows : (head + 1) * rows
                ]
                square = part[:, :lanes] + part[:, lanes:]
                diagonal_ref[head, block + piece] = diagonal_sums(square)[0]
        return running + dot_tn(keys, score_low)

    diagonal_ref[2:] = jnp.zeros(diagonal_ref[2:].shape, f32)
    running = step(0, jnp.zeros((2 * lanes, 2 * rows), f32))
    running = lax.fori_loop(1, tiles, step, running, unroll=min(7, tiles - 1))
    joined = jnp.concatenate([running[:half, :rows], running[half:lanes, rows:]], axis=0).T * 0.125
    shifted = query_ref[...] + segment_bias_ref[...]
    code = row_code_ref[...]
    zero_columns = []
    one_columns = []
    for head in range(2):
        part = running[lanes:, head * rows : (head + 1) * rows].T * 0.125
        same = jnp.sum(jnp.where(lane < 4, part * code, 0.0), axis=1, keepdims=True)
        total = jnp.sum(jnp.where(lane == 8, part, 0.0), axis=1, keepdims=True)
        zero_columns.append(same)
        one_columns.append(total - same)
    zero_back = jnp.where(first, zero_columns[0], zero_columns[1])
    one_back = jnp.where(first, one_columns[0], one_columns[1])
    shift_back = zero_back * embed_ref[0:1, :] + one_back * embed_ref[1:2, :]
    query_back_ref[...] = (joined + shift_back).astype(bf16)
    small_ref[0:1, :] = jnp.sum(joined, axis=0, keepdims=True)
    small_ref[1:2, :] = jnp.sum(shift_back, axis=0, keepdims=True)
    small_ref[2:3, :] = jnp.sum(zero_back * shifted, axis=0, keepdims=True)
    small_ref[3:4, :] = jnp.sum(one_back * shifted, axis=0, keepdims=True)
    blocks = number_ref.shape[0]
    bucket = lax.broadcasted_iota(jnp.int32, (lanes, 2 * lanes), 0)
    table_back = jnp.zeros((8, lanes), f32)
    for block in range(blocks):
        chosen = jnp.where(bucket == number_ref[block : block + 1, :], 1.0, 0.0).astype(bf16)
        sums = diagonal_ref[:, block, :]
        for _ in range(3):
            part = sums.astype(bf16)
            table_back = table_back + dot_nt(part, chosen)
            sums = sums - part.astype(f32)
    small_ref[4:8, :] = table_back[:4]


def attention_specs(rows, keys, blocks, first_pair=0):
    column = lambda pair: (0, pair + first_pair)
    fixed = lambda pair: (0, 0)
    front = lambda pair: (pair + first_pair, 0, 0)
    return {
        "rows": pl.BlockSpec((rows, lanes), column),
        "row": pl.BlockSpec((1, lanes), column),
        "embed": pl.BlockSpec((2, lanes), column),
        "small": pl.BlockSpec((8, lanes), column),
        "row_code": pl.BlockSpec((rows, lanes), fixed),
        "key_code": pl.BlockSpec((keys, lanes), fixed, pipeline_mode=pl.Buffered(1)),
        "both": pl.BlockSpec((keys, 2 * lanes), column),
        "table": pl.BlockSpec((2, blocks, 2 * lanes), front),
        "log": pl.BlockSpec((1, 1, 2 * rows), front),
        "stack": pl.BlockSpec((1, 2 * rows, 2 * lanes), front),
    }


def attention_forward(query_full, bias_content, bias_segment, embed, row_code, key_code, both, table):
    rows, width = query_full.shape
    count = both.shape[0]
    pairs = width // lanes
    spec = attention_specs(rows, count, count // lanes)
    return pl.pallas_call(
        forward_kernel,
        grid=(pairs,),
        in_specs=[
            spec["rows"],
            spec["row"],
            spec["row"],
            spec["embed"],
            spec["row_code"],
            spec["key_code"],
            spec["both"],
            spec["table"],
        ],
        out_specs=[spec["rows"], spec["log"], spec["stack"]],
        out_shape=[
            jax.ShapeDtypeStruct((rows, width), f32),
            jax.ShapeDtypeStruct((pairs, 1, 2 * rows), f32),
            jax.ShapeDtypeStruct((pairs, 2 * rows, 2 * lanes), bf16),
        ],
        scratch_shapes=[pltpu.VMEM((count, 2 * rows), f32)],
        compiler_params=pltpu.CompilerParams(
            dimension_semantics=("arbitrary",), vmem_limit_bytes=60 << 20
        ),
        cost_estimate=free,
    )(query_full, bias_content, bias_segment, embed, row_code, key_code, both, table)


def attention_backward(stack, query_full, bias_segment, embed, row_code, key_code, both, table, number, out_back, attended, log_row):
    rows, width = query_full.shape
    count = both.shape[0]
    pairs = width // lanes
    blocks = count // lanes
    spec = attention_specs(rows, count, blocks)
    return pl.pallas_call(
        backward_kernel,
        grid=(pairs,),
        in_specs=[
            spec["stack"],
            spec["rows"],
            spec["row"],
            spec["embed"],
            spec["row_code"],
            spec["key_code"],
            spec["both"],
            spec["table"],
            pl.BlockSpec((blocks, 2 * lanes), lambda pair: (0, 0)),
            spec["rows"],
            spec["rows"],
            spec["log"],
        ],
        out_specs=[spec["rows"], spec["both"], spec["small"]],
        out_shape=[
            jax.ShapeDtypeStruct((rows, width), bf16),
            jax.ShapeDtypeStruct((count, 2 * width), bf16),
            jax.ShapeDtypeStruct((8, width), f32),
        ],
        scratch_shapes=[pltpu.VMEM((8, blocks, 2 * lanes), f32)],
        compiler_params=pltpu.CompilerParams(
            dimension_semantics=("arbitrary",), vmem_limit_bytes=60 << 20
        ),
        cost_estimate=takes(34),
    )(stack, query_full, bias_segment, embed, row_code, key_code, both, table, number, out_back, attended, log_row)


def marks_kernel(bound_list, meta_ref, table_ref, key_code_ref, bias_ref, number_ref, row_code_ref):
    blocks = meta_ref.shape[0]
    info = meta_ref[:, 0, :].astype(f32)
    segment = info[:, :lanes]
    rank = info[:, lanes : lanes + 1]
    first = info[:, lanes + 1 : lanes + 2] * lanes + info[:, lanes + 2 : lanes + 3]
    turn = lax.broadcasted_iota(jnp.int32, (blocks, 2 * lanes), 1)
    turn = jnp.where(turn < lanes, turn, turn - 2 * lanes)
    distance = (first[0:1, :] - first).astype(jnp.int32) + turn
    number = jnp.full(distance.shape, bucket_steps, jnp.int32)
    for bound in bound_list:
        number = number + (distance >= bound).astype(jnp.int32) - (distance <= -bound).astype(jnp.int32)
    number_ref[...] = number
    hidden = rank > rank[0:1, :]
    for head in range(bias_ref.shape[0]):
        value = jnp.zeros((blocks, 2 * lanes), f32)
        for bucket in range(2 * bucket_steps + 1):
            value = jnp.where(number == bucket, table_ref[head, bucket], value)
        bias_ref[head] = jnp.where(hidden, negative, value)
    lane = lax.broadcasted_iota(jnp.int32, (lanes, lanes), 1)
    code = (lane % 4).astype(f32)
    for block in range(blocks):
        column = jnp.broadcast_to(segment[block : block + 1, :], (lanes, lanes)).T
        marked = jnp.where(
            lane < 8, jnp.where(column == code, 1.0, 0.0), jnp.where(lane < 10, 1.0, 0.0)
        )
        key_code_ref[block * lanes : (block + 1) * lanes, :] = marked.astype(bf16)
        if block == 0:
            row_code_ref[:lanes, :] = marked
            row_code_ref[lanes:, :] = marked


def key_marks(meta_all, table_full, length):
    blocks = meta_all.shape[0]
    heads = table_full.shape[0]
    bounds = tuple(
        1 + level * level * length // (bucket_steps * bucket_steps) for level in range(bucket_steps)
    )
    return pl.pallas_call(
        functools.partial(marks_kernel, bounds),
        in_specs=[in_vmem, in_smem],
        out_specs=[in_vmem] * 4,
        out_shape=[
            jax.ShapeDtypeStruct((blocks * lanes, lanes), bf16),
            jax.ShapeDtypeStruct((heads, blocks, 2 * lanes), f32),
            jax.ShapeDtypeStruct((blocks, 2 * lanes), jnp.int32),
            jax.ShapeDtypeStruct((2 * lanes, lanes), f32),
        ],
        compiler_params=pltpu.CompilerParams(vmem_limit_bytes=40 << 20),
        cost_estimate=free,
    )(meta_all, table_full)


def assemble_pair(first_ref, second_ref, first_own_ref, second_own_ref, parts, places):
    own, *others = [pl.multiple_of(place, 16) for place in places]
    first_ref[pl.ds(own, first_own_ref.shape[0]), :] = first_own_ref[...]
    second_ref[pl.ds(own, second_own_ref.shape[0]), :] = second_own_ref[...]
    width, hidden = first_ref.shape[1], second_ref.shape[1]
    span = (width + hidden) // 2
    for (part_ref, base), other in zip(parts, others, strict=True):
        quarter = part_ref.shape[0] // 2
        rows = pl.ds(other, quarter)
        first_ref[rows, :] = part_ref[:quarter, base : base + width]
        second_ref[rows, : span - width] = part_ref[:quarter, base + width : base + span]
        second_ref[rows, span - width :] = part_ref[quarter:, base : base + span]


def assemble(target_ref, own_ref, parts, columns, places):
    own, *others = [pl.multiple_of(place, 16) for place in places]
    target_ref[pl.ds(own, own_ref.shape[0]), :] = own_ref[...]
    for part_ref, other in zip(parts, others, strict=True):
        target_ref[pl.ds(other, part_ref.shape[0]), :] = part_ref[:, columns]


def forward_half_kernel(
    place_ref,
    attended_ref,
    content_ref,
    stream_ref,
    output_own_ref,
    inner_own_ref,
    got_ref,
    near_ref,
    rest_ref,
    far_ref,
    vector_ref,
    bias_ref,
    out_low_ref,
    normed_ref,
    rows_ref,
    scale_ref,
    normed_low_ref,
    active_ref,
    slope_ref,
    square_ref,
    weight_output_ref,
    weight_inner_ref,
):
    width = attended_ref.shape[1]
    hidden = inner_own_ref.shape[1]
    half = content_ref.shape[0]
    places = [place_ref[at] for at in range(1, 6)]
    base = 3 * width
    assemble_pair(
        weight_output_ref,
        weight_inner_ref,
        output_own_ref,
        inner_own_ref,
        ((got_ref, base), (near_ref, 0), (rest_ref, base), (far_ref, 0)),
        places,
    )
    out_low = attended_ref[...].astype(bf16)
    out_low_ref[...] = out_low
    attention_out = dot(out_low, weight_output_ref[...])
    streams = jnp.concatenate([content_ref[...], stream_ref[...]], axis=0).astype(f32)
    residual = streams + attention_out
    rows, scale = normalized(residual)
    normed = rows * vector_ref[2:3, :] + vector_ref[3:4, :]
    normed_low = normed.astype(bf16)
    rows_ref[...] = rows
    scale_ref[...] = jnp.broadcast_to(scale, scale_ref.shape)
    normed_ref[...] = normed
    normed_low_ref[...] = normed_low
    lane = lax.broadcasted_iota(jnp.int32, (1, width), 1)
    total = jnp.zeros((1, width), f32)
    for at, value in enumerate((streams, attention_out, residual)):
        part = value[:half]
        summed = jnp.sum(jnp.sum(part * part, axis=0, keepdims=True), axis=1, keepdims=True)
        total = total + jnp.where((lane == at) | (lane == at + width // 2), summed, 0.0)
    square_ref[...] = jnp.broadcast_to(total, square_ref.shape)
    step = 512

    @pl.loop(0, hidden // step)
    def _(at):
        span = pl.ds(pl.multiple_of(at * step, step), step)
        inner = dot(normed_low, weight_inner_ref[:, span]) + bias_ref[0:1, span]
        below = 0.5 + 0.5 * lax.erf(inner * 0.7071067811865476)
        density = 0.3989422804014327 * jnp.exp(-0.5 * inner * inner)
        active_ref[:, span] = (inner * below).astype(bf16)
        slope_ref[:, span] = below + inner * density


def backward_half_kernel(
    place_ref,
    active_ref,
    slope_ref,
    normed_ref,
    rows_ref,
    scale_ref,
    weight_output_ref,
    weight_inner_ref,
    outer_own_ref,
    got_ref,
    rest_ref,
    vector_ref,
    square_ref,
    content_cotangent_ref,
    query_cotangent_ref,
    content_result_ref,
    query_result_ref,
    residual_back_ref,
    out_back_ref,
    outer_kept_ref,
    outer_sent_ref,
    inner_kept_ref,
    inner_sent_ref,
    attention_kept_ref,
    attention_sent_ref,
    sums_ref,
    weight_outer_ref,
    inner_back_ref,
    held_ref,
    bias_back_ref,
):
    width = normed_ref.shape[1]
    hidden = active_ref.shape[1]
    count = content_cotangent_ref.shape[0]
    core = place_ref[6]
    assemble(
        weight_outer_ref,
        outer_own_ref,
        (got_ref, rest_ref),
        slice(0, width),
        [place_ref[at] for at in range(7, 10)],
    )

    def give(value_ref, kept_ref, sent_ref):
        columns = kept_ref.shape[1]
        kept_ref[...] = value_ref[:, pl.ds(pl.multiple_of(core * columns, lanes), columns)]
        sent_ref[...] = value_ref[:, pl.ds(pl.multiple_of((1 - core) * columns, lanes), columns)]

    outer = dot(active_ref[...], weight_outer_ref[...]) + vector_ref[4:5, :]
    final_rows, final_scale = normalized(normed_ref[...] + outer)
    result = (final_rows * vector_ref[5:6, :] + vector_ref[6:7, :]).astype(bf16)
    content_result_ref[...] = result[:count]
    query_result_ref[...] = result[count:]
    cotangent = jnp.concatenate(
        [content_cotangent_ref[...], query_cotangent_ref[...]], axis=0
    ).astype(f32)
    sums_ref[9:10, :] = jnp.sum(cotangent * final_rows, axis=0, keepdims=True)
    sums_ref[10:11, :] = jnp.sum(cotangent, axis=0, keepdims=True)
    back_second = norm_back(cotangent * vector_ref[5:6, :], final_rows, final_scale)
    outer_back = back_second.astype(bf16)
    sums_ref[8:9, :] = jnp.sum(outer_back.astype(f32), axis=0, keepdims=True)
    held_ref[...] = outer_back
    give(held_ref, outer_kept_ref, outer_sent_ref)
    residual_back_ref[...] = back_second
    step = 512

    @pl.loop(0, hidden // step)
    def _(at):
        span = pl.ds(pl.multiple_of(at * step, step), step)
        back = dot_nt(outer_back, weight_outer_ref[span, :]) * slope_ref[:, span]
        low = back.astype(bf16)
        inner_back_ref[:, span] = low
        bias_back_ref[0:1, span] = jnp.sum(low.astype(f32), axis=0, keepdims=True)
        residual_back_ref[...] += dot_nt(low, weight_inner_ref[:, span])

    give(inner_back_ref, inner_kept_ref, inner_sent_ref)
    normed_back = residual_back_ref[...]
    rows = rows_ref[...]
    sums_ref[6:7, :] = jnp.sum(normed_back * rows, axis=0, keepdims=True)
    sums_ref[7:8, :] = jnp.sum(normed_back, axis=0, keepdims=True)
    residual_back = norm_back(normed_back * vector_ref[2:3, :], rows, scale_ref[:, 0:1])
    residual_back_ref[...] = residual_back
    attention_back = residual_back.astype(bf16)
    held_ref[...] = attention_back
    give(held_ref, attention_kept_ref, attention_sent_ref)
    out_back_ref[...] = dot_nt(attention_back, weight_output_ref[...]).astype(bf16)
    part = width // 2
    for at in range(hidden // width):
        sums_ref[11 + at : 12 + at, :part] = bias_back_ref[0:1, at * part : (at + 1) * part]
        sums_ref[11 + at : 12 + at, part:] = bias_back_ref[
            0:1, hidden // 2 + at * part : hidden // 2 + (at + 1) * part
        ]
    last = 11 + hidden // width
    sums_ref[last : last + 1, :] = square_ref[0:1, :]
    sums_ref[0:6, :] = jnp.zeros((6, width), f32)


def forward_half(places, *operands):
    rows, width = operands[0].shape
    hidden = operands[4].shape[1]
    shapes = [
        jax.ShapeDtypeStruct((rows, width), bf16),
        jax.ShapeDtypeStruct((rows, width), f32),
        jax.ShapeDtypeStruct((rows, width), f32),
        jax.ShapeDtypeStruct((rows, lanes), f32),
        jax.ShapeDtypeStruct((rows, width), bf16),
        jax.ShapeDtypeStruct((rows, hidden), bf16),
        jax.ShapeDtypeStruct((rows, hidden), f32),
        jax.ShapeDtypeStruct((8, width), f32),
        jax.ShapeDtypeStruct((width, width), bf16),
        jax.ShapeDtypeStruct((width, hidden), bf16),
    ]
    return pl.pallas_call(
        forward_half_kernel,
        grid=(1,),
        in_specs=[in_smem] + [resident(value) for value in operands],
        out_specs=[resident(shape) for shape in shapes],
        out_shape=shapes,
        compiler_params=pltpu.CompilerParams(vmem_limit_bytes=60 << 20),
        cost_estimate=takes(8),
    )(places, *operands)


def backward_half(places, *operands):
    active, normed = operands[0], operands[2]
    rows, width = normed.shape
    hidden = active.shape[1]
    count = rows // 2
    shapes = (
        [jax.ShapeDtypeStruct((count, width), bf16)] * 2
        + [jax.ShapeDtypeStruct((rows, width), f32), jax.ShapeDtypeStruct((rows, width), bf16)]
        + [jax.ShapeDtypeStruct((rows, width // 2), bf16)] * 2
        + [jax.ShapeDtypeStruct((rows, hidden // 2), bf16)] * 2
        + [jax.ShapeDtypeStruct((rows, width // 2), bf16)] * 2
        + [jax.ShapeDtypeStruct((16, width), f32)]
    )
    return pl.pallas_call(
        backward_half_kernel,
        grid=(1,),
        in_specs=[in_smem] + [resident(value) for value in operands],
        out_specs=[resident(shape) for shape in shapes],
        out_shape=shapes,
        scratch_shapes=[
            pltpu.VMEM((hidden, width), bf16),
            pltpu.VMEM((rows, hidden), bf16),
            pltpu.VMEM((rows, width), bf16),
            pltpu.VMEM((8, hidden), f32),
        ],
        compiler_params=pltpu.CompilerParams(vmem_limit_bytes=60 << 20),
        cost_estimate=takes(12),
    )(places, *operands)


def body(
    content,
    query_stream,
    block_rank,
    segments,
    positions,
    query_weight,
    key_weight,
    value_weight,
    output_weight,
    content_bias,
    segment_bias,
    segment_embed,
    relative_table,
    attention_gain,
    attention_shift,
    inner_weight,
    inner_bias,
    outer_weight,
    outer_bias,
    final_gain,
    final_shift,
    content_cotangent,
    query_cotangent,
):
    block_rows = content.shape[1]
    width = content.shape[2]
    rows = 2 * block_rows
    count = lax.axis_size("ctx")
    sides = lax.axis_size("wsh")
    side = lax.axis_index("wsh")
    core = lax.axis_index("ctx") % 2
    length = block_rows * count
    own_content = content[0]
    own_query = query_stream[0]
    part = width // sides
    table_heads, bucket_count = relative_table.shape
    head_count = table_heads * sides
    inner_rows = inner_bias.shape[0] // part
    low = 2

    first_places = shard_places(query_weight.shape[0])
    hidden = inner_weight.shape[1]
    near = (lax.axis_index("ctx") // low) % 2
    shard_rows = query_weight.shape[0]
    half, quarter = shard_rows // 2, shard_rows // 4
    base, span = 3 * width, (width + hidden) // 2
    (first_sent,) = moved(
        tuple(
            (at, window("0", half, 0, width), 0, window(0, half, at * width, width))
            for at in range(3)
        )
        + (
            (3, window("1", quarter, 0, width), 0, window(0, quarter, base, width)),
            (
                4,
                window("1", quarter, 0, span - width),
                0,
                window(0, quarter, base + width, span - width),
            ),
            (4, window("1", quarter, span - width, span), 0, window(quarter, quarter, base, span)),
        ),
        [jax.ShapeDtypeStruct((half, base + span), bf16)],
        jnp.stack([core * half, (2 * core + near) * quarter]).astype(jnp.int32),
        query_weight,
        key_weight,
        value_weight,
        output_weight,
        inner_weight,
        limit=60,
    )
    first_got = across(first_sent)
    mark_rows = 16
    marks = jnp.concatenate(
        [
            segments[0].astype(bf16),
            block_rank[0].astype(bf16),
            (positions[0, :1] // lanes).astype(bf16),
            (positions[0, :1] % lanes).astype(bf16),
        ]
    )
    marks = jnp.pad(marks[None], ((0, mark_rows - 1), (0, width - marks.shape[0])))
    block = jnp.concatenate([own_content, marks], axis=0)
    gathered = gather_blocks(block)
    small_height = 16
    small = jnp.zeros((small_height * part,), bf16)
    filled = 0
    for vector in (
        content_bias,
        segment_bias,
        attention_gain,
        attention_shift,
        outer_bias,
        final_gain,
        final_shift,
        segment_embed.reshape(-1),
        inner_bias,
        relative_table.reshape(-1),
    ):
        small = small + jnp.pad(vector, (filled, small.shape[0] - filled - vector.shape[0]))
        filled += vector.shape[0]
    small = small.reshape(small_height, part)
    small_other = across(small)
    first_rest = partner(first_got, 1)
    second_near = partner(first_got[:, base:], low)
    third_places = shard_places(outer_weight.shape[0])
    third_sent = half_rows(third_places, 1, outer_weight)
    third_got = across(third_sent)

    small_pair = jnp.where(
        side == 0,
        jnp.concatenate([small, small_other], axis=1),
        jnp.concatenate([small_other, small], axis=1),
    ).astype(f32)
    bias_content = small_pair[0:1]
    bias_segment = small_pair[1:2]
    embed = small_pair[7:9]
    bias_inner = jnp.concatenate(
        [
            small_pair[9 : 9 + inner_rows, :part].reshape(-1),
            small_pair[9 : 9 + inner_rows, part:].reshape(-1),
        ]
    )
    table_row = small_pair[9 + inner_rows]
    table_full = jnp.concatenate(
        [
            table_row[: table_heads * bucket_count],
            table_row[part : part + table_heads * bucket_count],
        ]
    ).reshape(head_count, bucket_count)

    held = block_rows + mark_rows
    if len(gathered) == 1:
        stacked = gathered[0].reshape(count, held, width)
        content_all = stacked[:, :block_rows].reshape(length, width)
        meta_all = stacked[:, block_rows:]
    else:
        plan = []
        place = 0
        for at, piece in enumerate(gathered):
            for row in range(0, piece.shape[0], held):
                plan.append(
                    (at, window(row, block_rows), 0, window(place * block_rows, block_rows))
                )
                plan.append(
                    (at, window(row + block_rows, mark_rows), 1, window(place * mark_rows, mark_rows))
                )
                place += 1
        content_all, meta_all = moved(
            tuple(plan),
            [
                jax.ShapeDtypeStruct((length, width), bf16),
                jax.ShapeDtypeStruct((count * mark_rows, width), bf16),
            ],
            first_places,
            *gathered,
        )
        meta_all = meta_all.reshape(count, mark_rows, width)
    pairs = width // lanes
    runs = [(0, 0, width, 0, 0)]
    for pair in range(pairs):
        runs.append((1, pair * lanes, lanes, 1, 2 * pair * lanes))
        runs.append((2, pair * lanes, lanes, 1, (2 * pair + 1) * lanes))
    weight_query, weight_both = whole_rows(
        first_places, runs, (width, 2 * width), first_got, first_rest, query_weight, key_weight, value_weight
    )
    key_code, table, number, row_code = key_marks(meta_all, table_full, length)

    streams = jnp.concatenate([own_content, own_query], axis=0)
    query_full = dot(streams, weight_query)
    both = dot(content_all, weight_both).astype(bf16)
    attended, log_row, stack = attention_forward(
        query_full, bias_content, bias_segment, embed, row_code, key_code, both, table
    )

    hidden = inner_weight.shape[1]
    second_near, third_got, attended = lax.optimization_barrier(
        (second_near, third_got, attended)
    )
    second_far = partner(second_near, 1)
    third_rest = partner(third_got, 1)
    half_places = jnp.concatenate(
        [
            quarter_places(query_weight.shape[0]),
            core[None].astype(jnp.int32),
            third_places[1:],
        ]
    )
    (
        out_low,
        normed,
        norm_rows,
        norm_scale,
        normed_low,
        active_low,
        slope,
        squares,
        weight_output,
        weight_inner,
    ) = forward_half(
        half_places,
        attended,
        own_content,
        own_query,
        output_weight,
        inner_weight,
        first_got,
        second_near,
        first_rest,
        second_far,
        small_pair,
        bias_inner[None],
    )
    out_low_other = partner(out_low, 1)
    normed_other = partner(normed_low, 1)
    active_other = partner(active_low, 1)
    (
        content_result,
        query_result,
        residual_back,
        out_back,
        outer_kept,
        outer_sent,
        inner_kept,
        inner_sent,
        attention_kept,
        attention_sent,
        vectors,
    ) = backward_half(
        half_places,
        active_low,
        slope,
        normed,
        norm_rows,
        norm_scale,
        weight_output,
        weight_inner,
        outer_weight,
        third_got,
        third_rest,
        small_pair,
        squares,
        content_cotangent[0],
        query_cotangent[0],
    )

    cuts, extra = split_bits(count)
    wide_cuts = [1] + cuts
    order_one = [0] + cuts
    order_two = cuts[:1] + [0] + cuts[1:]
    places_one = piece_places(order_one, cuts)
    places_two = piece_places(order_two, cuts)
    wide_places = by_core(
        piece_places([1, 0] + cuts, wide_cuts),
        piece_places([1, cuts[0], 0] + cuts[1:], wide_cuts),
        2 << len(cuts),
    )
    places_out = jnp.concatenate([piece_places(cuts, cuts), core[None].astype(jnp.int32)])
    wide_places_out = by_core(
        piece_places(wide_cuts, wide_cuts),
        piece_places([1] + cuts[1:] + cuts[:1], wide_cuts),
        1 << len(cuts),
    )

    outer_keep, outer_send = product_pieces(
        places_one, active_low, active_other, outer_kept, partner(outer_sent, 1)
    )
    outer_got = pass_on(outer_send, order_one[0])
    inner_keep, inner_send = product_pieces(
        places_two,
        normed_low,
        normed_other,
        inner_kept,
        partner(inner_sent, 1),
        out_low,
        out_low_other,
        attention_kept,
        partner(attention_sent, 1),
    )
    inner_got = pass_on(inner_send, order_two[0])

    line = cuts[1:]
    last = cuts[2]

    def add_extra(value):
        for bit in extra:
            value = fold_last(value, partner(value, bit))
        return value

    query_back, both_back, small_back = attention_backward(
        stack,
        query_full,
        bias_segment,
        embed,
        row_code,
        key_code,
        both,
        table,
        number,
        after(out_back, outer_send, inner_send),
        attended,
        log_row,
    )
    hidden_rows = hidden // part // sides
    order = Sequence(after(wide_places_out, small_back))
    outer_got, inner_got = order.wait(outer_got, inner_got)
    outer_keep, outer_send = fold(outer_keep, outer_got)
    outer_send = order.ready(outer_send)
    outer_got = partner(outer_send, cuts[0])
    inner_keep, inner_send = fold(inner_keep, inner_got)
    inner_send = order.ready(inner_send)
    inner_got = across(inner_send)
    tail_keep, tail_send = cut_gradient(
        wide_places,
        vectors,
        small_back,
        dot_tn(streams, query_back),
        dot_tn(content_all, order.ready(both_back)),
    )
    tail_keep = order.ready(tail_keep)
    content_share = order.ready(share_of_content(order.ready(both_back), weight_both))
    outer_got = order.wait(outer_got)
    inner_got = order.wait(inner_got)
    tail_send = order.ready(tail_send)
    tail_got = partner(tail_send, 1)
    outer_keep, outer_send = fold(outer_keep, outer_got)
    outer_send = order.ready(outer_send)
    outer_got = partner(outer_send, line[0])
    inner_keep, inner_send = fold(inner_keep, inner_got)
    inner_send = order.ready(inner_send)
    inner_got = partner(inner_send, line[0])
    share_keep, share_send = content_share[: count // 2], order.ready(content_share[count // 2 :])
    share_got = partner(share_send, 1)
    tail_got = order.wait(tail_got)
    tail_keep, tail_send = fold(tail_keep, tail_got)
    tail_send = order.ready(tail_send)
    tail_got = pass_mixed(tail_send, 0, cuts[0])
    share_got = order.wait(share_got)
    share_keep, share_send = fold(share_keep, share_got)
    share_send = order.ready(share_send)
    share_got = partner(share_send, cuts[0])
    outer_got = order.wait(outer_got)
    outer_keep, outer_send = fold(outer_keep, outer_got)
    outer_send = order.ready(outer_send)
    outer_got = partner(outer_send, last)
    inner_got = order.wait(inner_got)
    inner_keep, inner_send = fold(inner_keep, inner_got)
    inner_send = order.ready(inner_send)
    inner_got = partner(inner_send, last)
    tail_got = order.wait(tail_got)
    tail_keep, tail_send = fold(tail_keep, tail_got)
    tail_send = order.ready(tail_send)
    tail_got = pass_mixed(tail_send, cuts[0], 0)
    tail_got = order.wait(tail_got)
    tail_keep, tail_send = fold(tail_keep, tail_got)
    tail_send = order.ready(tail_send)
    tail_got = partner(tail_send, line[0])
    outer_got = order.wait(outer_got)
    outer_value = order.ready(add_extra(fold_last(outer_keep, outer_got)))
    outer_got = partner(outer_value, last)
    inner_got = order.wait(inner_got)
    inner_value = order.ready(add_extra(fold_last(inner_keep, inner_got)))
    inner_got = partner(inner_value, last)
    tail_got = order.wait(tail_got)
    tail_keep, tail_send = fold(tail_keep, tail_got)
    tail_send = order.ready(tail_send)
    tail_got = partner(tail_send, last)
    outer_got = order.wait(outer_got)
    outer_value = order.ready(piled(outer_value, outer_got))
    outer_got = partner(outer_value, line[0])
    inner_got = order.wait(inner_got)
    inner_value = order.ready(piled(inner_value, inner_got))
    inner_got = partner(inner_value, line[0])
    share_got = order.wait(share_got)
    share_keep, share_send = fold(share_keep, share_got)
    share_send = order.ready(share_send)
    share_got = partner(share_send, line[0])
    tail_got = order.wait(tail_got)
    tail_value = order.ready(add_extra(fold_last(tail_keep, tail_got)))
    tail_got = pass_mixed(tail_value, last, cuts[0])
    outer_got = order.wait(outer_got)
    outer_value = order.ready(piled(outer_value, outer_got))
    outer_got = partner(outer_value, cuts[0])
    inner_got = order.wait(inner_got)
    inner_value = order.ready(piled(inner_value, inner_got))
    inner_got = partner(inner_value, cuts[0])
    tail_got = order.wait(tail_got)
    tail_value = order.ready(piled(tail_value, tail_got))
    tail_got = pass_mixed(tail_value, line[0], last)
    share_got = order.wait(share_got)
    share_keep, share_send = fold(share_keep, share_got)
    share_send = order.ready(share_send)
    share_got = partner(share_send, last)
    streams_back = residual_back + dot_nt(order.ready(query_back), weight_query)
    tail_got = order.wait(tail_got)
    tail_value = order.ready(piled(tail_value, tail_got))
    tail_got = pass_mixed(tail_value, cuts[0], line[0])
    outer_got = order.wait(outer_got)
    outer_value = order.ready(piled(outer_value, outer_got))
    outer_got = partner(outer_value, 1)
    outer_got = order.wait(outer_got)
    (outer_weight_sum,) = lay_out(
        places_out,
        (((0, 0, width // 2, -1), (1, 0, width // 2, -2)),),
        outer_value,
        outer_got,
    )
    outer_weight_sum = order.ready(outer_weight_sum)
    share_got = order.wait(share_got)
    for bit in extra:
        share_keep, share_send = fold(share_keep, share_got)
        share_got = partner(share_send, bit)
    content_back = streams_back[:block_rows] + share_keep[0].astype(f32) + share_got[0].astype(f32)
    content_back = order.ready(content_back)
    tail_got = order.wait(tail_got)
    tail_value = order.ready(piled(tail_value, tail_got))
    tail_got = partner(tail_value, 1)
    inner_got = order.wait(inner_got)
    inner_value = order.ready(piled(inner_value, inner_got))
    inner_got = partner(inner_value, 1)
    inner_got = order.wait(inner_got)
    inner_weight_sum, output_weight_sum = lay_out(
        places_out,
        (
            ((0, 0, hidden // 2, -1), (1, 0, hidden // 2, -2)),
            ((0, hidden // 2, width // 2, -1), (1, hidden // 2, width // 2, -2)),
        ),
        inner_value,
        inner_got,
    )
    inner_weight_sum, output_weight_sum = order.ready(inner_weight_sum, output_weight_sum)
    tail_got = order.wait(tail_got)
    plan = []
    for kind in range(3):
        row = []
        for pair in range(pairs):
            taken = pair * lanes if kind == 0 else width + (2 * pair + kind - 1) * lanes
            row.append((0, taken, lanes, pair * lanes))
        plan.append(tuple(row))
    plan.append(((0, 3 * width, lanes, 0),))
    query_weight_sum, key_weight_sum, value_weight_sum, vector_sums = lay_out(
        order.mark, tuple(plan), tail_value, tail_got
    )
    sums = vector_sums[:, :16].T
    table_sum = jnp.swapaxes(sums[4:6].reshape(2, -1, lanes)[:, :, :bucket_count], 0, 1).reshape(
        table_heads, bucket_count
    )
    inner_bias_sum = sums[11 : 11 + hidden_rows].reshape(-1)
    token_total = length * sides * width
    root_mean = jnp.sqrt(sums[11 + hidden_rows, :3] / token_total)
    return (
        content_result[None],
        query_result[None],
        content_back[None],
        streams_back[block_rows:][None],
        query_weight_sum,
        key_weight_sum,
        value_weight_sum,
        output_weight_sum,
        sums[0],
        sums[1],
        sums[2:4],
        table_sum,
        sums[6],
        sums[7],
        inner_weight_sum,
        inner_bias_sum,
        outer_weight_sum,
        sums[8],
        sums[9],
        sums[10],
        root_mean,
    )


def solution(mesh):
    tokens = P("wsh", "ctx", None)
    marks = P("wsh", "ctx")
    matrix = P("wsh", None)
    vector = P("wsh")
    placed = (
        (tokens, tokens, marks, marks, marks)
        + (matrix,) * 4
        + (vector, vector, P(None, "wsh"), matrix, vector, vector, matrix, vector, matrix)
        + (vector,) * 3
        + (tokens, tokens)
    )
    given = (
        (tokens,) * 4
        + (matrix,) * 4
        + (vector, vector, P(None, "wsh"), matrix, vector, vector, matrix, vector, matrix)
        + (vector,) * 3
        + (P(),)
    )
    return jax.shard_map(body, mesh=mesh, in_specs=placed, out_specs=given, check_vma=False)
```
